32 devices in a mesh: fsdp: 32 (over z, y, x, core).
Axes of the slice: x: 2, y: 2, z: 4, core: 2. Of those that a mesh axis runs over, the one named last changes fastest.
Arguments:
- tokens: bfloat16 [32768, 768], P('fsdp'), may hold values from -6 to 6
- attn_matrices: bfloat16 [18432, 128], P('fsdp')
- ffn_matrices: bfloat16 [36864, 128], P('fsdp')
- vectors: bfloat16 [9216], P('fsdp')
- segments: int32 [64, 512], P('fsdp'), may hold values from 0 to 24, as said below
- pad_segment: int32 [64], P('fsdp'), may hold values from 1 to 24, as said below
- cotangent: bfloat16 [32768, 768], P('fsdp'), may hold values from -6 to 6
Outputs:
- block_output: bfloat16 [32768, 768], P('fsdp')
- input_grad: bfloat16 [32768, 768], P('fsdp')
- attn_grad: float32 [18432, 128], P('fsdp')
- ffn_grad: float32 [36864, 128], P('fsdp')
- vector_grad: float32 [9216], P('fsdp')
The draws below stay inside these ranges and needn't reach their ends.
Inputs may be any that keep to these rules, and one draw needn't show every extreme that they name: `segments`: in each row the ids start at 0 and never fall; each passage covers 20 to 200 slots; the row's last segment is its padding, 16 slots or more at the row's end; the most is reached in every draw. `pad_segment`: the id of the row's padding segment, equal to the number of its passages; the most is reached in every draw.
All inputs are finite; a program needn't handle non-finite values.
Results may differ from the reference program's by a relative error of at most 0.012.
Values may be sent and summed in bfloat16 or wider, within the bound.
No kernel may reach another device: no remote copies, remote signals or barrier semaphores. Data moves between devices by JAX's collectives and lax.ppermute only.
A program may use at most 192 MiB of HBM per device.

```python
import jax
import jax.numpy as jnp
from jax import lax

D = 768
FF = 3072
HEADS = 12
HEAD_DIM = 64
SLOTS = 512
PMIN = 20
PMAX = 200
ROWS = 64
TOKENS = 32768
AROWS = 18432
FROWS = 36864
VECS = 9216


def base_normal(key, shape):
    return jnp.clip(jax.random.normal(key, shape, jnp.float32), -6.0, 6.0)


def draw_attn_matrices(key, part):
    row_index = jnp.arange(AROWS, dtype=jnp.int32)[:, None] * 128
    flat_index = row_index + jnp.arange(128, dtype=jnp.int32)[None, :]
    square = D * D
    scale_in = D ** (-0.5)
    scales = jnp.where(flat_index < 2 * square, 1.2 * scale_in, jnp.where(flat_index < 3 * square, scale_in, 4.0 * scale_in))
    return (base_normal(key, (AROWS, 128)) * scales).astype(jnp.bfloat16)


def draw_ffn_matrices(key, part):
    row_index = jnp.arange(FROWS, dtype=jnp.int32)[:, None] * 128
    flat_index = row_index + jnp.arange(128, dtype=jnp.int32)[None, :]
    wide = D * FF
    scales = jnp.where(flat_index < wide, D ** (-0.5), FF ** (-0.5))
    return (base_normal(key, (FROWS, 128)) * scales).astype(jnp.bfloat16)


def draw_vectors(key, part):
    flat_index = jnp.arange(VECS, dtype=jnp.int32)
    gain_first = (flat_index >= 3 * D) & (flat_index < 4 * D)
    gain_second = (flat_index >= 6 * D + FF) & (flat_index < 7 * D + FF)
    is_gain = gain_first | gain_second
    base_draw = jnp.clip(jax.random.normal(key, (VECS,), jnp.float32), -4.0, 4.0)
    values = jnp.where(is_gain, 1.0 + 0.1 * base_draw, 0.2 * base_draw)
    return values.astype(jnp.bfloat16)


def segment_layout(key):
    base_key = jax.random.fold_in(key, 17)
    row_keys = jax.random.split(base_key, ROWS)
    row_numbers = jnp.arange(ROWS, dtype=jnp.int32)

    def one_row(row_key, row_number):
        length_key, limit_key = jax.random.split(row_key)
        candidates = SLOTS // PMIN + 1
        dense_row = row_number == 0
        drawn_lengths = jax.random.randint(length_key, (candidates,), PMIN, PMAX + 1)
        lengths = jnp.where(dense_row, jnp.full((candidates,), PMIN, jnp.int32), drawn_lengths)
        passage_ends = jnp.cumsum(lengths)
        drawn_limit = jax.random.randint(limit_key, (), SLOTS - SLOTS // 8, SLOTS - SLOTS // 32 + 1)
        fill_limit = jnp.where(dense_row, SLOTS - SLOTS // 32, drawn_limit)
        included = passage_ends <= fill_limit
        slot_index = jnp.arange(SLOTS, dtype=jnp.int32)
        segment_ids = jnp.sum((passage_ends[None, :] <= slot_index[:, None]) & included[None, :], axis=1)
        return (segment_ids.astype(jnp.int32), jnp.sum(included).astype(jnp.int32))
    return jax.vmap(one_row)(row_keys, row_numbers)


def draw_segments(key, part):
    return segment_layout(key)[0]


def draw_pad_segment(key, part):
    return segment_layout(key)[1]


def steps_of(stream_key, shape, cuts, least, top_value):
    factor_of = 1.0
    for position, parts in cuts:
        steps = jax.random.uniform(jax.random.fold_in(jax.random.fold_in(stream_key, 6), position), (parts,), jnp.float32, least / len(cuts), top_value / len(cuts))
        factor_of = factor_of * jnp.repeat(jnp.exp(steps), shape[position] // parts).reshape((-1,) + (1,) * (len(shape) - 1 - position))
    return factor_of


def normal_values(stream_key, extent, width, limit, pieces=(), kind=jnp.bfloat16):
    loudness = steps_of(stream_key, extent, pieces, -0.22, 0.18) if pieces else 1.0
    entries = jax.random.normal(stream_key, extent, jnp.float32) * width * loudness
    return jnp.minimum(jnp.maximum(entries, -limit), limit).astype(kind)


def setup_inputs(seed: int = 0) -> dict:
    key_of = jax.random.split(jax.random.key(seed), 8)
    tokens = normal_values(key_of[0], (TOKENS, D), 1.0, 6.0, ((0, 32),))
    attn_matrices = draw_attn_matrices(jax.random.fold_in(key_of[7], 71), 0)
    ffn_matrices = draw_ffn_matrices(jax.random.fold_in(key_of[7], 71), 0)
    vectors = draw_vectors(jax.random.fold_in(key_of[7], 71), 0)
    segments = draw_segments(jax.random.fold_in(key_of[7], 71), 0)
    pad_segment = draw_pad_segment(jax.random.fold_in(key_of[7], 71), 0)
    cotangent = normal_values(key_of[6], (TOKENS, D), 1.0, 6.0, ((0, 32),))
    return dict(tokens=tokens, attn_matrices=attn_matrices, ffn_matrices=ffn_matrices, vectors=vectors, segments=segments, pad_segment=pad_segment, cotangent=cotangent)


@jax.custom_vjp
def low(v):
    return lax.optimization_barrier(v.astype(jnp.bfloat16)).astype(jnp.float32)

@jax.custom_vjp
def low_back(v):
    return v

def low_keep(v):
    return (low(v), None)

def low_pass(kept, grad):
    return (grad,)

def back_keep(v):
    return (v, None)

def back_low(kept, grad):
    return (low(grad),)
low.defvjp(low_keep, low_pass)
low_back.defvjp(back_keep, back_low)

def round_both(value):
    return low_back(low(value))

def matmul_high(left, right):
    return jnp.dot(left, right, precision=lax.Precision.HIGHEST)

def layer_norm(hidden, gain, bias):
    mean_val = lax.optimization_barrier(jnp.mean(hidden, axis=-1, keepdims=True))
    centered = hidden - mean_val
    variance = lax.optimization_barrier(jnp.mean(centered * centered, axis=-1, keepdims=True))
    return centered * lax.rsqrt(variance + 1e-12) * gain + bias

def unpack(attn_full, ffn_full, vector_full):
    flat_attn = attn_full.reshape(-1)
    flat_ffn = ffn_full.reshape(-1)
    square = D * D
    wide = D * FF
    w_query = flat_attn[0:square].reshape(D, D)
    w_key = flat_attn[square:2 * square].reshape(D, D)
    w_value = flat_attn[2 * square:3 * square].reshape(D, D)
    w_output = flat_attn[3 * square:4 * square].reshape(D, D)
    w_up = flat_ffn[0:wide].reshape(D, FF)
    w_down = flat_ffn[wide:2 * wide].reshape(FF, D)
    b_query = vector_full[0:D]
    b_value = vector_full[D:2 * D]
    b_output = vector_full[2 * D:3 * D]
    gain_one = vector_full[3 * D:4 * D]
    bias_one = vector_full[4 * D:5 * D]
    b_up = vector_full[5 * D:5 * D + FF]
    b_down = vector_full[5 * D + FF:6 * D + FF]
    gain_two = vector_full[6 * D + FF:7 * D + FF]
    bias_two = vector_full[7 * D + FF:8 * D + FF]
    return (w_query, w_key, w_value, w_output, w_up, w_down, b_query, b_value, b_output, gain_one, bias_one, b_up, b_down, gain_two, bias_two)

def group_block(params, group_x, group_seg, group_pad):
    w_query, w_key, w_value, w_output, w_up, w_down, b_query, b_value, b_output, gain_one, bias_one, b_up, b_down, gain_two, bias_two = params
    row_count = group_x.shape[0]
    tokens_flat = group_x.reshape(-1, D)
    head_shape = (row_count, SLOTS, HEADS, HEAD_DIM)
    query = round_both(matmul_high(tokens_flat, w_query) + b_query).reshape(head_shape)
    key_proj = round_both(matmul_high(tokens_flat, w_key)).reshape(head_shape)
    value_proj = round_both(matmul_high(tokens_flat, w_value) + b_value).reshape(head_shape)
    scores = low_back(jnp.einsum('gqhd,gkhd->ghqk', query, key_proj, precision=lax.Precision.HIGHEST) * 0.125)
    allowed = (group_seg[:, :, None] == group_seg[:, None, :])[:, None, :, :]
    scores = jnp.where(allowed, scores, -1000000000.0)
    prob_low = low(jax.nn.softmax(scores, axis=-1))
    context = jnp.einsum('ghqk,gkhd->gqhd', prob_low, value_proj, precision=lax.Precision.HIGHEST)
    keep_mask = (group_seg != group_pad[:, None]).astype(jnp.float32).reshape(-1, 1)
    context = round_both(context.reshape(-1, D) * keep_mask)
    attn_out = low_back(matmul_high(context, w_output) + b_output)
    normed_one = layer_norm(tokens_flat + attn_out, gain_one, bias_one)
    hidden_pre = low_back(matmul_high(low(normed_one), w_up) + b_up)
    hidden_act = low(jax.nn.gelu(hidden_pre, approximate=False))
    ffn_out = low_back(matmul_high(hidden_act, w_down) + b_down)
    return layer_norm(normed_one + ffn_out, gain_two, bias_two).reshape(group_x.shape)

def forward_all(tokens_in, attn_in, ffn_in, vector_in, segments, pad_segment):
    params = unpack(attn_in, ffn_in, vector_in)
    group_rows = 8 if ROWS % 8 == 0 else 1
    grouped_x = tokens_in.reshape(ROWS // group_rows, group_rows, SLOTS, D)
    grouped_seg = segments.reshape(ROWS // group_rows, group_rows, SLOTS)
    grouped_pad = pad_segment.reshape(ROWS // group_rows, group_rows)
    step_block = jax.checkpoint(group_block)

    def scan_step(carry, row_items):
        return (carry, step_block(params, row_items[0], row_items[1], row_items[2]))
    _, outputs = lax.scan(scan_step, jnp.zeros((), jnp.float32), (grouped_x, grouped_seg, grouped_pad))
    return outputs.reshape(ROWS * SLOTS, D)

def reference(tokens, attn_matrices, ffn_matrices, vectors, segments, pad_segment, cotangent):

    def forward_fn(tokens_in, attn_in, ffn_in, vector_in):
        return forward_all(tokens_in, attn_in, ffn_in, vector_in, segments, pad_segment)
    result, pullback = jax.vjp(forward_fn, tokens.astype(jnp.float32), attn_matrices.astype(jnp.float32), ffn_matrices.astype(jnp.float32), vectors.astype(jnp.float32))
    grad_tokens, grad_attn, grad_ffn, grad_vectors = pullback(cotangent.astype(jnp.float32))
    return (result.astype(jnp.bfloat16), grad_tokens.astype(jnp.bfloat16), grad_attn, grad_ffn, grad_vectors)
```

```python
import functools

import jax
import jax.numpy as jnp
from jax import lax
from jax.experimental import pallas as pl
from jax.experimental.pallas import tpu as pltpu
from jax.sharding import PartitionSpec as P

D = 768
FF = 3072
SLOTS = 512
BF = jnp.bfloat16
F32 = jnp.float32
NN = ((1,), (0,))
NT = ((1,), (1,))
TN = ((0,), (0,))
OWNERS = 32
ATTN_TILES = 36
FFN_TILES = 72
COST_SCALE = 1
VMEM_LIMIT = 60 * 1024 * 1024

TAIL_SLOPE = 0.39 * 0.5**0.5
TAIL_POLY = (
    0.11766260955586648,
    0.04569420719462487,
    0.32477969950633645,
    -0.3177001395785759,
    0.44333218507090993,
    -0.11376856259852677,
)


def dot(left, right, dims):
    return lax.dot_general(left, right, (dims, ((), ())), preferred_element_type=F32)


def params(**kwargs):
    return pltpu.CompilerParams(vmem_limit_bytes=VMEM_LIMIT, **kwargs)


def cost(flops, bytes_accessed, transcendentals):
    return pl.CostEstimate(
        flops=flops // COST_SCALE,
        bytes_accessed=bytes_accessed // COST_SCALE,
        transcendentals=transcendentals // COST_SCALE,
    )


def whole(shape):
    zeros = (0,) * len(shape)
    return pl.BlockSpec(shape, lambda *_: zeros)


ANY = pl.BlockSpec(memory_space=pl.ANY)


def square_cols(tiles, first, col):
    parts = [tiles[pl.ds(first, 8), i * 6 + col] for i in range(6)]
    return jnp.stack(parts, axis=1).reshape(D, 128)


def square(tiles, first):
    return jnp.concatenate([square_cols(tiles, first, col) for col in range(6)], axis=1)


def up_chunk(tiles, chunk):
    cols = []
    for col in range(6):
        parts = [tiles[:, i * 24 + chunk * 6 + col] for i in range(3)]
        cols.append(jnp.stack(parts, axis=1).reshape(D, 128))
    return jnp.concatenate(cols, axis=1)


def down_chunk(tiles, chunk):
    cols = []
    for col in range(6):
        parts = [tiles[pl.ds(4 * chunk, 4), i * 6 + col] for i in range(12)]
        cols.append(jnp.stack(parts, axis=1).reshape(D, 128))
    return jnp.concatenate(cols, axis=1)


def attn_fwd_kernel(
    gw_ref, x_ref, vec_ref, segc_ref, segr_ref, keep_ref,
    q_ref, k_ref, v_ref, ctx_ref, lse_ref, w_s, sems,
):
    row, col = pl.program_id(0), pl.program_id(1)

    @pl.when((row == 0) & (col == 0))
    def _():
        copies = [
            pltpu.make_async_copy(
                gw_ref.at[pl.ds(8 * m, 8), pl.ds(FFN_TILES, ATTN_TILES)],
                w_s.at[pl.ds(8 * m, 8)],
                sems.at[m],
            )
            for m in range(3)
        ]
        for copy in copies:
            copy.start()
        for copy in copies:
            copy.wait()

    lanes = pl.ds(pl.multiple_of(col * 128, 128), 128)
    weight = jnp.concatenate([square_cols(w_s, 8 * m, col) for m in range(3)], axis=1)
    qkv = dot(x_ref[...], weight, NN)
    query = (qkv[:, :128] + vec_ref[0:1, lanes]).astype(BF)
    key = qkv[:, 128:256].astype(BF)
    value = (qkv[:, 256:] + vec_ref[1:2, lanes]).astype(BF)
    q_ref[...] = query
    k_ref[...] = key
    v_ref[...] = value
    lane = lax.broadcasted_iota(jnp.int32, (1, 128), 1)
    low = lane < 64
    zero = jnp.zeros((), BF)
    keys = [jnp.where(low, key, zero), jnp.where(low, zero, key)]
    values = [jnp.where(low, value, zero), jnp.where(low, zero, value)]
    seg_row = segr_ref[...]
    for block in range(4):
        rows = pl.ds(block * 128, 128)
        allowed = segc_ref[rows, :] == seg_row
        q_block = query[block * 128 : block * 128 + 128]
        acc = jnp.zeros((128, 128), F32)
        lse = lse_ref[rows, :]
        for head in range(2):
            scores = dot(q_block, keys[head], NT) * 0.125
            scores = jnp.where(allowed, scores, -1e9)
            top = jnp.max(scores, axis=1, keepdims=True)
            expd = jnp.exp(scores - top)
            total = jnp.sum(expd, axis=1, keepdims=True)
            prob = (expd * (1.0 / total)).astype(BF)
            acc = acc + dot(prob, values[head], NN)
            lse = jnp.where(lane == 2 * col + head, top + jnp.log(total), lse)
        ctx_ref[rows, :] = (acc * keep_ref[rows, :]).astype(BF)
        lse_ref[rows, :] = lse


def attn_fwd(gw, tokens, vec, segc, segr, keep):
    count = tokens.shape[0]
    rows = count // SLOTS
    part = pl.BlockSpec((SLOTS, 128), lambda r, j: (r, j))
    slot = pl.BlockSpec((SLOTS, 1), lambda r, j: (r, 0))
    return pl.pallas_call(
        attn_fwd_kernel,
        grid=(rows, 6),
        in_specs=[
            ANY,
            pl.BlockSpec((SLOTS, D), lambda r, j: (r, 0)),
            whole((12, D)),
            slot,
            pl.BlockSpec((None, 1, SLOTS), lambda r, j: (r, 0, 0)),
            slot,
        ],
        out_specs=[part] * 4 + [pl.BlockSpec((SLOTS, 128), lambda r, j: (r, 0))],
        out_shape=[jax.ShapeDtypeStruct((count, D), BF)] * 4
        + [jax.ShapeDtypeStruct((count, 128), F32)],
        scratch_shapes=[
            pltpu.VMEM((24, ATTN_TILES, 16, 128), BF),
            pltpu.SemaphoreType.DMA((3,)),
        ],
        compiler_params=params(),
        cost_estimate=cost(
            flops=2 * count * D * (3 * D + 4 * SLOTS), bytes_accessed=count * D * 12, transcendentals=count * SLOTS * 12
        ),
        name="attn_fwd",
    )(gw, tokens, vec, segc, segr, keep)


def norm_parts(hidden):
    mean = jnp.mean(hidden, axis=1, keepdims=True)
    centered = hidden - mean
    var = jnp.mean(centered * centered, axis=1, keepdims=True)
    rstd = lax.rsqrt(var + 1e-12)
    return centered * rstd, rstd


def gelu_parts(u):
    size = jnp.abs(u)
    t = pl.reciprocal(1.0 + TAIL_SLOPE * size)
    poly = jnp.full_like(t, TAIL_POLY[-1])
    for coef in TAIL_POLY[-2::-1]:
        poly = poly * t + coef
    bell = jnp.exp(u * u * -0.5)
    tail = poly * t * bell
    phi_cdf = jnp.where(u > 0, 1.0 - tail, tail)
    return u * phi_cdf, phi_cdf + u * bell * 0.3989422804014327


def mid_copies(gw_ref, w1_s, w2_s, sems):
    copies = []
    for chunk in range(4):
        here = []
        for i in range(3):
            tiles = pl.ds(i * 24 + chunk * 6, 6)
            here.append((gw_ref.at[pl.ds(0, 16), tiles], w1_s.at[:, tiles]))
        owners = pl.ds(4 * chunk, 4)
        here.append((gw_ref.at[pl.ds(16 + 4 * chunk, 4), pl.ds(0, FFN_TILES)], w2_s.at[owners]))
        copies.append(
            [pltpu.make_async_copy(src, dst, sems.at[chunk, i]) for i, (src, dst) in enumerate(here)]
        )
    return copies


MID_TILE = 256


def mid_fwd_kernel(
    gw_ref, ctx_ref, x_ref, cot_ref, vec_ref,
    g_ref, gp_ref, n1_ref, rstd_ref, yb_ref, out_ref, dz_ref, dh2_ref, vg_ref,
    wo_s, w1_s, w2_s, h2_s, sems, wo_sem,
):
    chunk = pl.program_id(0)
    copies = mid_copies(gw_ref, w1_s, w2_s, sems)
    count = x_ref.shape[0]
    steps = count // MID_TILE

    def tile(i):
        return pl.ds(pl.multiple_of(i * MID_TILE, MID_TILE), MID_TILE)

    @pl.when(chunk == 0)
    def _():
        wo_copy = pltpu.make_async_copy(
            gw_ref.at[pl.ds(24, 8), pl.ds(FFN_TILES, ATTN_TILES)], wo_s, wo_sem
        )
        wo_copy.start()
        for group in copies:
            for copy in group:
                copy.start()
        wo_copy.wait()

        def body(i, carry):
            rows = tile(i)
            hidden = x_ref[rows, :].astype(F32) + dot(ctx_ref[rows, :], square(wo_s, 0), NN)
            hidden = hidden + vec_ref[2:3, :]
            normed, rstd = norm_parts(hidden)
            y_one = normed * vec_ref[3:4, :] + vec_ref[4:5, :]
            n1_ref[rows, :] = normed
            rstd_ref[rows, :] = jnp.broadcast_to(rstd, (MID_TILE, 128))
            yb_ref[rows, :] = y_one.astype(BF)
            h2_s[rows, :] = y_one + vec_ref[9:10, :]
            return carry

        lax.fori_loop(0, steps, body, 0)

    for index in range(4):

        @pl.when(chunk == index)
        def _(index=index):
            for copy in copies[index]:
                copy.wait()

    def ffn(i, carry):
        rows = tile(i)
        u = dot(yb_ref[rows, :], up_chunk(w1_s, chunk), NN) + vec_ref[pl.ds(5 + chunk, 1), :]
        act, slope = gelu_parts(u)
        act = act.astype(BF)
        g_ref[rows, :] = act
        gp_ref[rows, :] = slope.astype(BF)
        h2_s[rows, :] += dot(act, down_chunk(w2_s, chunk), NN)
        return carry

    lax.fori_loop(0, steps, ffn, 0)

    @pl.when(chunk == 3)
    def _():
        def body(i, carry):
            gain_sum, bias_sum, dz_sum = carry
            rows = tile(i)
            normed, rstd = norm_parts(h2_s[rows, :])
            gain = vec_ref[10:11, :]
            out_ref[rows, :] = (normed * gain + vec_ref[11:12, :]).astype(BF)
            err = cot_ref[rows, :].astype(F32)
            t = gain * err
            mean_t = jnp.mean(t, axis=1, keepdims=True)
            mean_tn = jnp.mean(t * normed, axis=1, keepdims=True)
            dh2 = (t - mean_t - normed * mean_tn) * rstd
            dz = dh2.astype(BF)
            dh2_ref[rows, :] = dh2
            dz_ref[rows, :] = dz
            return (
                gain_sum + jnp.sum(err * normed, axis=0, keepdims=True),
                bias_sum + jnp.sum(err, axis=0, keepdims=True),
                dz_sum + jnp.sum(dz.astype(F32), axis=0, keepdims=True),
            )

        zero = jnp.zeros((1, D), F32)
        gain_sum, bias_sum, dz_sum = lax.fori_loop(0, steps, body, (zero, zero, zero))
        vg_ref[0:1, :] = gain_sum
        vg_ref[1:2, :] = bias_sum
        vg_ref[2:3, :] = dz_sum
        vg_ref[3:8, :] = jnp.zeros((5, D), F32)


def mid_fwd(gw, ctx, tokens, cotangent, vec):
    count = tokens.shape[0]
    full = whole((count, D))
    part = pl.BlockSpec((count, D), lambda c: (0, c))
    shape = jax.ShapeDtypeStruct
    return pl.pallas_call(
        mid_fwd_kernel,
        grid=(4,),
        in_specs=[ANY, full, full, full, whole((12, D))],
        out_specs=[part, part, full, whole((count, 128)), full, full, full, full, whole((8, D))],
        out_shape=[
            shape((count, FF), BF),
            shape((count, FF), BF),
            shape((count, D), F32),
            shape((count, 128), F32),
            shape((count, D), BF),
            shape((count, D), BF),
            shape((count, D), BF),
            shape((count, D), F32),
            shape((8, D), F32),
        ],
        scratch_shapes=[
            pltpu.VMEM((8, ATTN_TILES, 16, 128), BF),
            pltpu.VMEM((16, FFN_TILES, 16, 128), BF),
            pltpu.VMEM((16, FFN_TILES, 16, 128), BF),
            pltpu.VMEM((count, D), F32),
            pltpu.SemaphoreType.DMA((4, 4)),
            pltpu.SemaphoreType.DMA,
        ],
        compiler_params=params(),
        cost_estimate=cost(
            flops=2 * count * D * (D + 2 * FF), bytes_accessed=count * D * 40, transcendentals=count * FF
        ),
        name="mid_fwd",
    )(gw, ctx, tokens, cotangent, vec)


def pick(mine, even, odd):
    return jnp.where(mine == 0, even, odd), jnp.where(mine == 0, odd, even)


def ffn_bwd_kernel(
    me_ref, gw_ref, dz_ref, yb_ref, dh2_ref, g_ref, gp_ref,
    dw1k_ref, dw1s_ref, dw2k_ref, dw2s_ref, db1_ref, dy1_ref,
    w1_s, w2_s, ybt_s, du_s, r_s, sems,
):
    chunk = pl.program_id(0)
    me = me_ref[0]
    core, my_x, my_y = me & 1, (me >> 1) & 1, (me >> 2) & 1
    copies = mid_copies(gw_ref, w1_s, w2_s, sems)
    count = dz_ref.shape[0]
    steps = count // MID_TILE

    @pl.when(chunk == 0)
    def _():
        for group in copies:
            for copy in group:
                copy.start()
        ybt_s[...] = yb_ref[...].T

    for index in range(4):

        @pl.when(chunk == index)
        def _(index=index):
            for copy in copies[index]:
                copy.wait()

    def grad_act(i, total):
        rows = pl.ds(pl.multiple_of(i * MID_TILE, MID_TILE), MID_TILE)
        dg = dot(dz_ref[rows, :], down_chunk(w2_s, chunk), NT)
        du = (gp_ref[rows, :].astype(F32) * dg).astype(BF)
        du_s[rows, :] = du
        back = dot(du, up_chunk(w1_s, chunk), NT)

        @pl.when(chunk == 0)
        def _():
            dy1_ref[rows, :] = dh2_ref[rows, :] + back

        @pl.when(chunk > 0)
        def _():
            dy1_ref[rows, :] += back

        return total + jnp.sum(du.astype(F32), axis=0, keepdims=True)

    db1_ref[...] = lax.fori_loop(0, steps, grad_act, jnp.zeros((1, D), F32))

    r_s[...] = dot(ybt_s[...], du_s[...], NN).astype(BF)
    for pair in range(8):
        even, odd = r_s[pl.ds(pair * 96, 48), :], r_s[pl.ds(pair * 96 + 48, 48), :]
        keep, send = pick(core, even, odd)
        place = ((((pair >> 1) & 1) ^ my_y) << 1) | ((pair & 1) ^ my_x)
        for col in range(6):
            lanes = slice(col * 128, col * 128 + 128)
            dw1k_ref[place, pair >> 2, :, col] = keep[:, lanes].reshape(3, 16, 128)
            dw1s_ref[place, pair >> 2, :, col] = send[:, lanes].reshape(3, 16, 128)

    r_s[...] = dot(g_ref[...], dz_ref[...], TN).astype(BF)
    for pair in range(2):
        even, odd = r_s[pl.ds(pair * 384, 192), :], r_s[pl.ds(pair * 384 + 192, 192), :]
        keep, send = pick(core, even, odd)
        for col in range(6):
            lanes = slice(col * 128, col * 128 + 128)
            dw2k_ref[pair ^ my_x, 0, :, col] = keep[:, lanes].reshape(12, 16, 128)
            dw2s_ref[pair ^ my_x, 0, :, col] = send[:, lanes].reshape(12, 16, 128)


def ffn_bwd(me, gw, dz, yb, dh2, g, gp):
    count = dz.shape[0]
    full = pl.BlockSpec((count, D), lambda c, m: (0, 0))
    part = pl.BlockSpec((count, D), lambda c, m: (0, c))
    up = pl.BlockSpec((4, 2, 3, 6, 16, 128), lambda c, m: (0, 0, 0, c, 0, 0))
    down = pl.BlockSpec(
        (2, 1, 12, 6, 16, 128), lambda c, m: ((c % 2) ^ ((m[0] >> 2) & 1), c // 2, 0, 0, 0, 0)
    )
    shape = jax.ShapeDtypeStruct
    return pl.pallas_call(
        ffn_bwd_kernel,
        grid_spec=pltpu.PrefetchScalarGridSpec(
            num_scalar_prefetch=1,
            grid=(4,),
            in_specs=[ANY, full, full, full, part, part],
            out_specs=[up, up, down, down, pl.BlockSpec((1, D), lambda c, m: (0, c)), full],
            scratch_shapes=[
                pltpu.VMEM((16, FFN_TILES, 16, 128), BF),
                pltpu.VMEM((16, FFN_TILES, 16, 128), BF),
                pltpu.VMEM((D, count), BF),
                pltpu.VMEM((count, D), BF),
                pltpu.VMEM((D, D), BF),
                pltpu.SemaphoreType.DMA((4, 4)),
            ],
        ),
        out_shape=[shape((4, 2, 3, 24, 16, 128), BF)] * 2
        + [shape((4, 2, 12, 6, 16, 128), BF)] * 2
        + [shape((1, FF), F32), shape((count, D), F32)],
        compiler_params=params(),
        cost_estimate=cost(
            flops=8 * count * D * FF, bytes_accessed=count * D * 40, transcendentals=0
        ),
        name="ffn_bwd",
    )(me, gw, dz, yb, dh2, g, gp)


def split_square(r_s, core, my_x, my_y, keep_ref, send_ref, index, cols=6):
    for pair in range(4):
        even, odd = r_s[pl.ds(pair * 192, 96), :], r_s[pl.ds(pair * 192 + 96, 96), :]
        keep, send = pick(core, even, odd)
        place = (((pair >> 1) ^ my_y) << 1) | ((pair & 1) ^ my_x)
        for col in range(cols):
            lanes = slice(col * 128, col * 128 + 128)
            keep_ref[place, index, :, col] = keep[:, lanes].reshape(6, 16, 128)
            send_ref[place, index, :, col] = send[:, lanes].reshape(6, 16, 128)


def norm_bwd_kernel(
    me_ref, gw_ref, dy1_ref, n1_ref, rstd_ref, ctx_ref, keep_ref, vec_ref,
    dh1_ref, dctx_ref, dwk_ref, dws_ref, vg_ref,
    wo_s, da_s, r_s, sem,
):
    step = pl.program_id(0)
    me = me_ref[0]
    tile = dy1_ref.shape[0]
    copy = pltpu.make_async_copy(
        gw_ref.at[pl.ds(24, 8), pl.ds(FFN_TILES, ATTN_TILES)], wo_s, sem
    )

    @pl.when(step == 0)
    def _():
        copy.start()
        vg_ref[...] = jnp.zeros_like(vg_ref)

    dy1 = dy1_ref[...]
    normed = n1_ref[...]
    t = dy1 * vec_ref[3:4, :]
    mean_t = jnp.mean(t, axis=1, keepdims=True)
    mean_tn = jnp.mean(t * normed, axis=1, keepdims=True)
    dh1 = (t - mean_t - normed * mean_tn) * rstd_ref[:, 0:1]
    dh1_ref[...] = dh1
    da = dh1.astype(BF)
    rows = pl.ds(pl.multiple_of(step * tile, tile), tile)
    da_s[rows, :] = da
    vg_ref[0:1, :] += jnp.sum(dy1 * normed, axis=0, keepdims=True)
    vg_ref[1:2, :] += jnp.sum(dy1, axis=0, keepdims=True)
    vg_ref[2:3, :] += jnp.sum(da.astype(F32), axis=0, keepdims=True)

    @pl.when(step == 0)
    def _():
        copy.wait()

    back = dot(da, square(wo_s, 0), NT).astype(BF).astype(F32)
    dctx_ref[...] = (back * keep_ref[...]).astype(BF)

    @pl.when(step == pl.num_programs(0) - 1)
    def _():
        r_s[...] = dot(ctx_ref[...], da_s[...], TN).astype(BF)
        split_square(r_s, me & 1, (me >> 1) & 1, (me >> 2) & 1, dwk_ref, dws_ref, 0)


def norm_bwd(me, gw, dy1, n1, rstd, ctx, keep, vec):
    count = dy1.shape[0]
    tile = MID_TILE
    rows = pl.BlockSpec((tile, D), lambda i, m: (i, 0))
    shape = jax.ShapeDtypeStruct
    grads = pl.BlockSpec((4, 1, 6, 6, 16, 128), lambda i, m: (0, 0, 0, 0, 0, 0))
    return pl.pallas_call(
        norm_bwd_kernel,
        grid_spec=pltpu.PrefetchScalarGridSpec(
            num_scalar_prefetch=1,
            grid=(count // tile,),
            in_specs=[
                ANY,
                rows,
                rows,
                pl.BlockSpec((tile, 128), lambda i, m: (i, 0)),
                pl.BlockSpec((count, D), lambda i, m: (0, 0)),
                pl.BlockSpec((tile, 1), lambda i, m: (i, 0)),
                pl.BlockSpec((12, D), lambda i, m: (0, 0)),
            ],
            out_specs=[rows, rows, grads, grads, pl.BlockSpec((8, D), lambda i, m: (0, 0))],
            scratch_shapes=[
                pltpu.VMEM((8, ATTN_TILES, 16, 128), BF),
                pltpu.VMEM((count, D), BF),
                pltpu.VMEM((D, D), BF),
                pltpu.SemaphoreType.DMA,
            ],
        ),
        out_shape=[shape((count, D), F32), shape((count, D), BF)]
        + [shape((4, 1, 6, 6, 16, 128), BF)] * 2
        + [shape((8, D), F32)],
        compiler_params=params(),
        cost_estimate=cost(
            flops=4 * count * D * D, bytes_accessed=count * D * 16, transcendentals=0
        ),
        name="norm_bwd",
    )(me, gw, dy1, n1, rstd, ctx, keep, vec)


def attn_bwd_kernel(
    first, q_ref, k_ref, v_ref, ctx_ref, dctx_ref, lse_ref, segc_ref, segr_ref, d_ref, lse_s,
):
    col = pl.program_id(1) + first

    @pl.when(col == first)
    def _():
        lse_s[...] = lse_ref[...].T

    query, key, value, dctx = q_ref[...], k_ref[...], v_ref[...], dctx_ref[...]
    lane = lax.broadcasted_iota(jnp.int32, (1, 128), 1)
    low = lane < 64
    zero = jnp.zeros((), BF)
    queries = [jnp.where(low, query, zero), jnp.where(low, zero, query)]
    keys = [jnp.where(low, key, zero), jnp.where(low, zero, key)]
    dctxs = [jnp.where(low, dctx, zero), jnp.where(low, zero, dctx)]
    products = (dctx.astype(F32) * ctx_ref[...].astype(F32)).T
    row_dots = [
        jnp.sum(products[:64], axis=0, keepdims=True),
        jnp.sum(products[64:], axis=0, keepdims=True),
    ]
    lses = [lse_s[pl.ds(2 * col + head, 1), :] for head in range(2)]
    seg_row = segr_ref[...]
    dq_t = jnp.zeros((128, SLOTS), F32)
    for block in range(4):
        rows = slice(block * 128, block * 128 + 128)
        allowed = segc_ref[rows, :] == seg_row
        dv = jnp.zeros((128, 128), F32)
        dk = jnp.zeros((128, 128), F32)
        for head in range(2):
            scores = dot(key[rows], queries[head], NT) * 0.125
            prob = jnp.where(allowed, jnp.exp(scores - lses[head]), 0.0)
            dv = dv + dot(prob.astype(BF), dctxs[head], NN)
            dprob = dot(value[rows], dctxs[head], NT)
            dscore = (prob * (dprob - row_dots[head])).astype(BF)
            dk = dk + dot(dscore, queries[head], NN)
            dq_t = dq_t + dot(keys[head][rows], dscore, TN)
        d_ref[1, rows, :] = (dk * 0.125).astype(BF)
        d_ref[2, rows, :] = dv.astype(BF)
    d_ref[0] = (dq_t.T * 0.125).astype(BF)


def attn_bwd(query, key, value, ctx, dctx, lse, segc, segr, first, cols):
    count = query.shape[0]
    rows = count // SLOTS
    part = pl.BlockSpec((SLOTS, 128), lambda r, j: (r, j + first))
    slot = pl.BlockSpec((SLOTS, 1), lambda r, j: (r, 0))
    return pl.pallas_call(
        functools.partial(attn_bwd_kernel, first),
        grid=(rows, cols),
        in_specs=[part] * 5
        + [
            pl.BlockSpec((SLOTS, 128), lambda r, j: (r, 0)),
            slot,
            pl.BlockSpec((None, 1, SLOTS), lambda r, j: (r, 0, 0)),
        ],
        out_specs=pl.BlockSpec((3, SLOTS, 128), lambda r, j: (0, r, j)),
        out_shape=jax.ShapeDtypeStruct((3, count, 128 * cols), BF),
        scratch_shapes=[pltpu.VMEM((128, SLOTS), F32)],
        compiler_params=params(),
        cost_estimate=cost(
            flops=10 * count * D * SLOTS, bytes_accessed=count * D * 16, transcendentals=count * SLOTS * 12
        ),
        name="attn_bwd",
    )(query, key, value, ctx, dctx, lse, segc, segr)


def proj_grad_kernel(me_ref, x_ref, d_ref, dwk_ref, dws_ref, vg_ref, xt_s, r_s):
    step = pl.program_id(0)
    me = me_ref[0]

    @pl.when(step == 0)
    def _():
        xt_s[...] = x_ref[...].T
        vg_ref[...] = jnp.zeros_like(vg_ref)

    grad = d_ref[...]
    vg_ref[pl.ds(step, 1), :] = jnp.sum(grad.astype(F32), axis=0, keepdims=True)
    r_s[...] = dot(xt_s[...], grad, NN).astype(BF)
    split_square(r_s, me & 1, (me >> 1) & 1, (me >> 2) & 1, dwk_ref, dws_ref, 0, r_s.shape[1] // 128)


def proj_grad(me, tokens, grads):
    count, width = grads.shape[1:]
    cols = width // 128
    out = pl.BlockSpec((4, 1, 6, cols, 16, 128), lambda i, m: (0, i, 0, 0, 0, 0))
    shape = jax.ShapeDtypeStruct
    return pl.pallas_call(
        proj_grad_kernel,
        grid_spec=pltpu.PrefetchScalarGridSpec(
            num_scalar_prefetch=1,
            grid=(3,),
            in_specs=[
                pl.BlockSpec((count, D), lambda i, m: (0, 0)),
                pl.BlockSpec((None, count, width), lambda i, m: (i, 0, 0)),
            ],
            out_specs=[out, out, pl.BlockSpec((8, width), lambda i, m: (0, 0))],
            scratch_shapes=[pltpu.VMEM((D, count), BF), pltpu.VMEM((D, width), BF)],
        ),
        out_shape=[shape((4, 3, 6, cols, 16, 128), BF)] * 2 + [shape((8, width), F32)],
        compiler_params=params(),
        cost_estimate=cost(
            flops=6 * count * D * D, bytes_accessed=count * D * 14, transcendentals=0
        ),
        name="proj_grad",
    )(me, tokens, grads)


def input_grad_kernel(gw_ref, dh1_ref, da_ref, db_ref, out_ref, w_s, sems):
    @pl.when(pl.program_id(0) == 0)
    def _():
        copies = [
            pltpu.make_async_copy(
                gw_ref.at[pl.ds(8 * m, 8), pl.ds(FFN_TILES, ATTN_TILES)],
                w_s.at[pl.ds(8 * m, 8)],
                sems.at[m],
            )
            for m in range(3)
        ]
        for copy in copies:
            copy.start()
        for copy in copies:
            copy.wait()

    total = dh1_ref[...]
    for m in range(3):
        grad = jnp.concatenate([da_ref[m], db_ref[m]], axis=1)
        total = total + dot(grad, square(w_s, 8 * m), NT)
    out_ref[...] = total.astype(BF)


def input_grad(gw, dh1, first, second):
    count = dh1.shape[0]
    rows = pl.BlockSpec((MID_TILE, D), lambda i: (i, 0))
    return pl.pallas_call(
        input_grad_kernel,
        grid=(count // MID_TILE,),
        in_specs=[ANY, rows] + [pl.BlockSpec((3, MID_TILE, D // 2), lambda i: (0, i, 0))] * 2,
        out_specs=rows,
        out_shape=jax.ShapeDtypeStruct((count, D), BF),
        scratch_shapes=[
            pltpu.VMEM((24, ATTN_TILES, 16, 128), BF),
            pltpu.SemaphoreType.DMA((3,)),
        ],
        compiler_params=params(),
        cost_estimate=cost(
            flops=6 * count * D * D, bytes_accessed=count * D * 18, transcendentals=0
        ),
        name="input_grad",
    )(gw, dh1, first, second)


def retile(flat, blocks):
    tall = flat.shape[0] // (16 * blocks)
    tiles = flat.reshape(tall, 16, blocks, 128).transpose(0, 2, 1, 3)
    return tiles.reshape(tall * blocks, 16, 128)


def untile(tiles, blocks):
    tall = tiles.shape[0] // blocks
    flat = tiles.reshape(tall, blocks, 16, 128).transpose(0, 2, 1, 3)
    return flat.reshape(tall * blocks * 16, 128)


def gather_tiles(attn, ffn, vectors, size):
    if size == OWNERS:
        upper = lax.axis_index("fsdp") < OWNERS // 2
        ffn_tiles = jnp.where(upper, retile(ffn, 24), retile(ffn, 6))
        vec = jnp.pad(vectors, (0, 2048 - vectors.shape[0])).reshape(1, 16, 128)
        mine = jnp.concatenate([ffn_tiles, retile(attn, 6), vec], axis=0)
        gathered = lax.all_gather(mine, "fsdp", axis=0, tiled=False)
        vec = gathered[:, FFN_TILES + ATTN_TILES].reshape(OWNERS, 2048)[:, : vectors.shape[0]]
        return gathered, vec.astype(F32).reshape(12, D)
    attn = lax.all_gather(attn, "fsdp", axis=0, tiled=True)
    ffn = lax.all_gather(ffn, "fsdp", axis=0, tiled=True)
    vec = lax.all_gather(vectors, "fsdp", axis=0, tiled=True)
    half = ffn.shape[0] // 2
    ffn_tiles = jnp.concatenate([retile(ffn[:half], 24), retile(ffn[half:], 6)], axis=0)
    gathered = jnp.concatenate(
        [
            ffn_tiles.reshape(OWNERS, FFN_TILES, 16, 128),
            retile(attn, 6).reshape(OWNERS, ATTN_TILES, 16, 128),
        ],
        axis=1,
    )
    return gathered, vec.astype(F32).reshape(12, D)


def hop(value, bit):
    pairs = [(i, i ^ bit) for i in range(OWNERS)]
    return lax.ppermute(value, "fsdp", pairs)


def reduce_plain(ffn_terms, attn_terms, vector_terms):
    def absolute(keep, send):
        planes = keep.shape[1]
        both = jnp.stack([keep, send], axis=1)
        return jnp.moveaxis(both, 2, 0).reshape(planes * 8, -1, 16, 128)

    dw1k, dw1s, dw2k, dw2s = ffn_terms
    up = untile(absolute(dw1k, dw1s).reshape(-1, 16, 128), 24)
    down = untile(absolute(dw2k, dw2s).reshape(-1, 16, 128), 6)
    proj = untile(absolute(*attn_terms).reshape(-1, 16, 128), 6)

    def scatter(value):
        return lax.psum_scatter(value.astype(F32), "fsdp", scatter_dimension=0, tiled=True)

    return scatter(proj), scatter(jnp.concatenate([up, down], axis=0)), scatter(vector_terms)


class Reduction:
    def __init__(self, keeps, sends):
        self.keeps = keeps
        self.received = [hop(send, 1) for send in sends]

    def part(self, place, upper):
        pieces = []
        for a, b in zip(self.keeps, self.received, strict=True):
            half = a.shape[1] // 2
            cut = slice(half, None) if upper else slice(0, half)
            piece = a[place, cut].astype(F32) + b[place, cut].astype(F32)
            pieces.append(piece.reshape((-1, 16, 128)))
        return jnp.concatenate(pieces, axis=0)

    def corner(self):
        self.via_x = hop(self.part(3, False).astype(BF), 2)
        self.via_y = hop(self.part(3, True).astype(BF), 4)

    def sides(self):
        to_x = jnp.stack([self.part(1, False), self.part(1, True) + self.via_y.astype(F32)])
        to_y = jnp.stack([self.part(2, False) + self.via_x.astype(F32), self.part(2, True)])
        self.from_x = hop(to_x.astype(BF), 2)
        self.from_y = hop(to_y.astype(BF), 4)

    def planes(self, my_z, arrange):
        own = jnp.stack([self.part(0, False), self.part(0, True)])
        own = arrange(own + self.from_x.astype(F32) + self.from_y.astype(F32))
        self.mine = lax.dynamic_index_in_dim(own, my_z, 0, keepdims=False)
        low = own.astype(BF)
        self.others = [
            hop(lax.dynamic_index_in_dim(low, my_z ^ step, 0, keepdims=False), 8 * step)
            for step in (1, 2, 3)
        ]

    def total(self):
        return self.mine + sum(other.astype(F32) for other in self.others)


def meet(hops, values):
    return lax.optimization_barrier((hops, values))


def tiles_of(array):
    return array.reshape(array.shape[:2] + (-1, 16, 128))


def layer(tokens, attn_matrices, ffn_matrices, vectors, segments, pad_segment, cotangent, size):
    fast = size == OWNERS
    gw, vec = gather_tiles(attn_matrices, ffn_matrices, vectors, size)
    place = lax.axis_index("fsdp") if fast else jnp.zeros((), jnp.int32)
    me = place.reshape(1).astype(jnp.int32)
    my_z = place >> 3
    rows = segments.shape[0]
    segc = segments.reshape(rows * SLOTS, 1)
    segr = segments.reshape(rows, 1, SLOTS)
    keep = (segments != pad_segment[:, None]).astype(F32).reshape(rows * SLOTS, 1)

    query, key, value, ctx, lse = attn_fwd(gw, tokens, vec, segc, segr, keep)
    g, gp, n1, rstd, yb, out, dz, dh2, vg_two = mid_fwd(gw, ctx, tokens, cotangent, vec)
    dw1k, dw1s, dw2k, dw2s, db1, dy1 = ffn_bwd(me, gw, dz, yb, dh2, g, gp)
    if fast:
        ffn_sum = Reduction([tiles_of(dw1k), tiles_of(dw2k)], [tiles_of(dw1s), tiles_of(dw2s)])
    dh1, dctx, dwok, dwos, vg_one = norm_bwd(me, gw, dy1, n1, rstd, ctx, keep, vec)
    if fast:
        ffn_sum.received, dctx = meet(ffn_sum.received, dctx)
        ffn_sum.corner()
    first = attn_bwd(query, key, value, ctx, dctx, lse, segc, segr, 0, 3)
    if fast:
        (ffn_sum.via_x, ffn_sum.via_y), (first, dctx) = meet(
            (ffn_sum.via_x, ffn_sum.via_y), (first, dctx)
        )
        ffn_sum.sides()
    dwak, dwas, vg_a = proj_grad(me, tokens, first)
    second = attn_bwd(query, key, value, ctx, dctx, lse, segc, segr, 3, 3)
    if fast:
        (ffn_sum.from_x, ffn_sum.from_y), second = meet((ffn_sum.from_x, ffn_sum.from_y), second)

        def arrange(own):
            own = own.reshape(2, 2, FFN_TILES, 16, 128).transpose(1, 0, 2, 3, 4)
            return own.reshape(4, FFN_TILES, 16, 128)

        ffn_sum.planes(my_z, arrange)
    dwbk, dwbs, vg_b = proj_grad(me, tokens, second)
    vector_terms = jnp.concatenate(
        [
            vg_a[0],
            vg_b[0],
            vg_a[2],
            vg_b[2],
            vg_one[2],
            vg_one[0],
            vg_one[1],
            db1[0],
            vg_two[2],
            vg_two[0],
            vg_two[1],
        ]
    )
    keeps = jnp.concatenate([jnp.concatenate([dwak, dwbk], axis=3), dwok], axis=1)
    sends = jnp.concatenate([jnp.concatenate([dwas, dwbs], axis=3), dwos], axis=1)
    if not fast:
        dx = input_grad(gw, dh1, first, second)
        return (out, dx) + reduce_plain((dw1k, dw1s, dw2k, dw2s), (keeps, sends), vector_terms)

    each = vector_terms.shape[0] // OWNERS
    terms = vector_terms.reshape(4, 2, 2, 2, each)
    for axis in (1, 2, 3):
        bit = (place >> (3 - axis)) & 1
        terms = jnp.where(bit == 1, jnp.flip(terms, axis), terms)
    terms = jnp.pad(terms, ((0, 0),) * 4 + ((0, 2048 - each),)).astype(BF)
    terms = terms.transpose(3, 1, 2, 0, 4).reshape(2, 4, 4, 1, 16, 128)
    attn_sum = Reduction(
        [jnp.concatenate([tiles_of(keeps), terms[0]], axis=2)],
        [jnp.concatenate([tiles_of(sends), terms[1]], axis=2)],
    )
    attn_sum.corner()
    attn_sum.sides()
    dx = input_grad(gw, dh1, first, second)
    attn_sum.planes(my_z, lambda own: own.reshape(4, ATTN_TILES + 1, 16, 128))
    ffn = ffn_sum.total()
    upper = place < OWNERS // 2
    ffn_grad = jnp.where(upper, untile(ffn, 24), untile(ffn, 6))
    attn = attn_sum.total()
    attn_grad = untile(attn[:ATTN_TILES], 6)
    vector_grad = attn[ATTN_TILES].reshape(2048)[:each]
    return out, dx, attn_grad, ffn_grad, vector_grad


def solution(mesh):
    size = mesh.shape["fsdp"]
    return jax.shard_map(
        functools.partial(layer, size=size),
        mesh=mesh,
        in_specs=(
            P("fsdp", None),
            P("fsdp", None),
            P("fsdp", None),
            P("fsdp"),
            P("fsdp", None),
            P("fsdp"),
            P("fsdp", None),
        ),
        out_specs=(P("fsdp", None), P("fsdp", None), P("fsdp", None), P("fsdp", None), P("fsdp")),
        check_vma=False,
    )
```

```python
import functools

import jax
import jax.numpy as jnp
from jax import lax
from jax.experimental import pallas as pl
from jax.experimental.pallas import tpu as pltpu
from jax.sharding import PartitionSpec as P

D = 768
FF = 3072
SLOTS = 512
BF = jnp.bfloat16
F32 = jnp.float32
NN = ((1,), (0,))
NT = ((1,), (1,))
TN = ((0,), (0,))
OWNERS = 32
ATTN_TILES = 36
FFN_TILES = 72
COST_SCALE = 1
VMEM_LIMIT = 60 * 1024 * 1024

TAIL_SLOPE = 0.39 * 0.5**0.5
TAIL_POLY = (
    0.11766260955586648,
    0.04569420719462487,
    0.32477969950633645,
    -0.3177001395785759,
    0.44333218507090993,
    -0.11376856259852677,
)


def dot(left, right, dims):
    return lax.dot_general(left, right, (dims, ((), ())), preferred_element_type=F32)


def params(**kwargs):
    return pltpu.CompilerParams(vmem_limit_bytes=VMEM_LIMIT, **kwargs)


def cost(flops, bytes_accessed, transcendentals):
    return pl.CostEstimate(
        flops=flops // COST_SCALE,
        bytes_accessed=bytes_accessed // COST_SCALE,
        transcendentals=transcendentals // COST_SCALE,
    )


def whole(shape):
    zeros = (0,) * len(shape)
    return pl.BlockSpec(shape, lambda *_: zeros)


ANY = pl.BlockSpec(memory_space=pl.ANY)
VEC_TILES = 5
VEC_ROWS = 16 * VEC_TILES


def row(vec_ref, index, width=D):
    blocks = width // 128
    return jnp.concatenate([vec_ref[pl.ds(6 * index + i, 1), :] for i in range(blocks)], axis=1)


def put_row(vec_ref, index, value, first=0):
    for i in range(value.shape[1] // 128):
        vec_ref[pl.ds(6 * index + first + i, 1), :] = value[:, 128 * i : 128 * i + 128]


def square_cols(tiles, first, col):
    parts = [tiles[pl.ds(first, 8), i * 6 + col] for i in range(6)]
    return jnp.stack(parts, axis=1).reshape(D, 128)


def square(tiles, first):
    return jnp.concatenate([square_cols(tiles, first, col) for col in range(6)], axis=1)


def up_chunk(tiles, chunk):
    cols = []
    for col in range(6):
        parts = [tiles[:, i * 24 + chunk * 6 + col] for i in range(3)]
        cols.append(jnp.stack(parts, axis=1).reshape(D, 128))
    return jnp.concatenate(cols, axis=1)


def down_chunk(tiles, chunk):
    cols = []
    for col in range(6):
        parts = [tiles[pl.ds(4 * chunk, 4), i * 6 + col] for i in range(12)]
        cols.append(jnp.stack(parts, axis=1).reshape(D, 128))
    return jnp.concatenate(cols, axis=1)


Q_TILES = 24
P_TILES = ATTN_TILES - Q_TILES


def attn_copies(fast, me, refs, w_s, sems):
    if not fast:
        return [pltpu.make_async_copy(refs[0], w_s, sems.at[0])]
    yxc, my_z = me & 7, me >> 3
    copies = []
    for core in range(2):
        for side in range(4):
            place = yxc ^ (2 * side + core)
            across, along = refs[8 * core + side], refs[8 * core + 4 + side]
            for z in range(4):
                copies.append((across.at[my_z ^ z], w_s.at[8 * z + place, pl.ds(0, Q_TILES)]))
            for other in range(4):
                owner = 8 * (my_z ^ side) + (yxc ^ (2 * other + core))
                tiles = along.at[pl.ds(other * P_TILES, P_TILES)]
                copies.append((tiles, w_s.at[owner, pl.ds(Q_TILES, P_TILES)]))
    return [pltpu.make_async_copy(src, dst, sems.at[i]) for i, (src, dst) in enumerate(copies)]


def attn_fwd_kernel(fast, me_ref, *args):
    count = 16 if fast else 1
    refs = args[:count]
    (
        vec_ref, x_ref, segc_ref, segr_ref, keep_ref,
        q_ref, k_ref, v_ref, ctx_ref, lse_ref, wa_ref, vec_out_ref,
        w_s, sems, out_sem,
    ) = args[count:]
    line, col = pl.program_id(0), pl.program_id(1)
    first_step = (line == 0) & (col == 0)
    last_step = (line == pl.num_programs(0) - 1) & (col == pl.num_programs(1) - 1)
    out_copy = pltpu.make_async_copy(w_s, wa_ref, out_sem)

    @pl.when(first_step)
    def _():
        copies = attn_copies(fast, me_ref[0], refs, w_s, sems)
        for copy in copies:
            copy.start()
        vec = vec_ref[0].astype(F32)
        for i in range(1, vec_ref.shape[0]):
            vec = vec + vec_ref[i].astype(F32)
        vec_out_ref[...] = vec.reshape(VEC_ROWS, 128)
        for copy in copies:
            copy.wait()
        out_copy.start()

    @pl.when(last_step)
    def _():
        out_copy.wait()

    weight = jnp.concatenate([square_cols(w_s, 8 * m, col) for m in range(3)], axis=1)
    qkv = dot(x_ref[...], weight, NN)
    query = (qkv[:, :128] + vec_out_ref[pl.ds(col, 1), :]).astype(BF)
    key = qkv[:, 128:256].astype(BF)
    value = (qkv[:, 256:] + vec_out_ref[pl.ds(6 + col, 1), :]).astype(BF)
    q_ref[...] = query
    k_ref[...] = key
    v_ref[...] = value
    lane = lax.broadcasted_iota(jnp.int32, (1, 128), 1)
    low = lane < 64
    zero = jnp.zeros((), BF)
    keys = [jnp.where(low, key, zero), jnp.where(low, zero, key)]
    values = [jnp.where(low, value, zero), jnp.where(low, zero, value)]
    seg_row = segr_ref[...]
    for block in range(4):
        rows = pl.ds(block * 128, 128)
        allowed = segc_ref[rows, :] == seg_row
        q_block = query[block * 128 : block * 128 + 128]
        acc = jnp.zeros((128, 128), F32)
        lse = lse_ref[rows, :]
        for head in range(2):
            scores = dot(q_block, keys[head], NT) * 0.125
            scores = jnp.where(allowed, scores, -1e9)
            top = jnp.max(scores, axis=1, keepdims=True)
            expd = jnp.exp(scores - top)
            total = jnp.sum(expd, axis=1, keepdims=True)
            prob = (expd * (1.0 / total)).astype(BF)
            acc = acc + dot(prob, values[head], NN)
            lse = jnp.where(lane == 2 * col + head, top + jnp.log(total), lse)
        ctx_ref[rows, :] = (acc * keep_ref[rows, :]).astype(BF)
        lse_ref[rows, :] = lse


def attn_fwd(fast, me, pieces, vec, tokens, segc, segr, keep):
    count = tokens.shape[0]
    rows = count // SLOTS
    part = pl.BlockSpec((SLOTS, 128), lambda r, j, m: (r, j))
    slot = pl.BlockSpec((SLOTS, 1), lambda r, j, m: (r, 0))
    shape = jax.ShapeDtypeStruct
    return pl.pallas_call(
        functools.partial(attn_fwd_kernel, fast),
        grid_spec=pltpu.PrefetchScalarGridSpec(
            num_scalar_prefetch=1,
            grid=(rows, 6),
            in_specs=[ANY] * len(pieces)
            + [
                whole(vec.shape),
                pl.BlockSpec((SLOTS, D), lambda r, j, m: (r, 0)),
                slot,
                pl.BlockSpec((None, 1, SLOTS), lambda r, j, m: (r, 0, 0)),
                slot,
            ],
            out_specs=[part] * 4
            + [pl.BlockSpec((SLOTS, 128), lambda r, j, m: (r, 0)), ANY, whole((VEC_ROWS, 128))],
            scratch_shapes=[
                pltpu.VMEM((OWNERS, ATTN_TILES, 16, 128), BF),
                pltpu.SemaphoreType.DMA((64,)),
                pltpu.SemaphoreType.DMA,
            ],
        ),
        out_shape=[shape((count, D), BF)] * 4
        + [
            shape((count, 128), F32),
            shape((OWNERS, ATTN_TILES, 16, 128), BF),
            shape((VEC_ROWS, 128), F32),
        ],
        compiler_params=params(),
        cost_estimate=cost(
            flops=2 * count * D * (3 * D + 4 * SLOTS), bytes_accessed=count * D * 12, transcendentals=count * SLOTS * 12
        ),
        name="attn_fwd",
    )(me, *pieces, vec, tokens, segc, segr, keep)


def norm_parts(hidden):
    mean = jnp.mean(hidden, axis=1, keepdims=True)
    centered = hidden - mean
    var = jnp.mean(centered * centered, axis=1, keepdims=True)
    rstd = lax.rsqrt(var + 1e-12)
    return centered * rstd, rstd


def gelu_parts(u):
    size = jnp.abs(u)
    t = pl.reciprocal(1.0 + TAIL_SLOPE * size)
    poly = jnp.full_like(t, TAIL_POLY[-1])
    for coef in TAIL_POLY[-2::-1]:
        poly = poly * t + coef
    bell = jnp.exp(u * u * -0.5)
    tail = poly * t * bell
    phi_cdf = jnp.where(u > 0, 1.0 - tail, tail)
    return u * phi_cdf, phi_cdf + u * bell * 0.3989422804014327


def mid_copies(gw_ref, w1_s, w2_s, sems):
    copies = []
    for chunk in range(4):
        here = []
        for i in range(3):
            tiles = pl.ds(i * 24 + chunk * 6, 6)
            here.append((gw_ref.at[pl.ds(0, 16), tiles], w1_s.at[:, tiles]))
        owners = pl.ds(4 * chunk, 4)
        here.append((gw_ref.at[pl.ds(16 + 4 * chunk, 4), pl.ds(0, FFN_TILES)], w2_s.at[owners]))
        copies.append(
            [pltpu.make_async_copy(src, dst, sems.at[chunk, i]) for i, (src, dst) in enumerate(here)]
        )
    return copies


MID_TILE = 256


def mid_fwd_kernel(
    gw_ref, wa_ref, ctx_ref, x_ref, cot_ref, vec_ref,
    g_ref, gp_ref, n1_ref, rstd_ref, yb_ref, out_ref, dz_ref, dh2_ref, vg_ref,
    wo_s, w1_s, w2_s, h2_s, sems, wo_sem,
):
    chunk = pl.program_id(0)
    copies = mid_copies(gw_ref, w1_s, w2_s, sems)
    count = x_ref.shape[0]
    steps = count // MID_TILE

    def tile(i):
        return pl.ds(pl.multiple_of(i * MID_TILE, MID_TILE), MID_TILE)

    @pl.when(chunk == 0)
    def _():
        wo_copy = pltpu.make_async_copy(
            wa_ref.at[pl.ds(24, 8)], wo_s, wo_sem
        )
        wo_copy.start()
        for group in copies:
            for copy in group:
                copy.start()
        wo_copy.wait()

        def body(i, carry):
            rows = tile(i)
            hidden = x_ref[rows, :].astype(F32) + dot(ctx_ref[rows, :], square(wo_s, 0), NN)
            hidden = hidden + row(vec_ref, 2)
            normed, rstd = norm_parts(hidden)
            y_one = normed * row(vec_ref, 3) + row(vec_ref, 4)
            n1_ref[rows, :] = normed
            rstd_ref[rows, :] = jnp.broadcast_to(rstd, (MID_TILE, 128))
            yb_ref[rows, :] = y_one.astype(BF)
            h2_s[rows, :] = y_one + row(vec_ref, 9)
            return carry

        lax.fori_loop(0, steps, body, 0)

    for index in range(4):

        @pl.when(chunk == index)
        def _(index=index):
            for copy in copies[index]:
                copy.wait()

    def ffn(i, carry):
        rows = tile(i)
        u = dot(yb_ref[rows, :], up_chunk(w1_s, chunk), NN) + row(vec_ref, 5 + chunk)
        act, slope = gelu_parts(u)
        act = act.astype(BF)
        g_ref[rows, :] = act
        gp_ref[rows, :] = slope.astype(BF)
        h2_s[rows, :] += dot(act, down_chunk(w2_s, chunk), NN)
        return carry

    lax.fori_loop(0, steps, ffn, 0)

    @pl.when(chunk == 3)
    def _():
        def body(i, carry):
            gain_sum, bias_sum, dz_sum = carry
            rows = tile(i)
            normed, rstd = norm_parts(h2_s[rows, :])
            gain = row(vec_ref, 10)
            out_ref[rows, :] = (normed * gain + row(vec_ref, 11)).astype(BF)
            err = cot_ref[rows, :].astype(F32)
            t = gain * err
            mean_t = jnp.mean(t, axis=1, keepdims=True)
            mean_tn = jnp.mean(t * normed, axis=1, keepdims=True)
            dh2 = (t - mean_t - normed * mean_tn) * rstd
            dz = dh2.astype(BF)
            dh2_ref[rows, :] = dh2
            dz_ref[rows, :] = dz
            return (
                gain_sum + jnp.sum(err * normed, axis=0, keepdims=True),
                bias_sum + jnp.sum(err, axis=0, keepdims=True),
                dz_sum + jnp.sum(dz.astype(F32), axis=0, keepdims=True),
            )

        zero = jnp.zeros((1, D), F32)
        gain_sum, bias_sum, dz_sum = lax.fori_loop(0, steps, body, (zero, zero, zero))
        vg_ref[...] = jnp.zeros_like(vg_ref)
        put_row(vg_ref, 9, dz_sum)
        put_row(vg_ref, 10, gain_sum)
        put_row(vg_ref, 11, bias_sum)


def mid_fwd(gw, wa, ctx, tokens, cotangent, vec):
    count = tokens.shape[0]
    full = whole((count, D))
    part = pl.BlockSpec((count, D), lambda c: (0, c))
    shape = jax.ShapeDtypeStruct
    return pl.pallas_call(
        mid_fwd_kernel,
        grid=(4,),
        in_specs=[ANY, ANY, full, full, full, whole((VEC_ROWS, 128))],
        out_specs=[part, part, full, whole((count, 128)), full, full, full, full, whole((VEC_ROWS, 128))],
        out_shape=[
            shape((count, FF), BF),
            shape((count, FF), BF),
            shape((count, D), F32),
            shape((count, 128), F32),
            shape((count, D), BF),
            shape((count, D), BF),
            shape((count, D), BF),
            shape((count, D), F32),
            shape((VEC_ROWS, 128), F32),
        ],
        scratch_shapes=[
            pltpu.VMEM((8, ATTN_TILES, 16, 128), BF),
            pltpu.VMEM((16, FFN_TILES, 16, 128), BF),
            pltpu.VMEM((16, FFN_TILES, 16, 128), BF),
            pltpu.VMEM((count, D), F32),
            pltpu.SemaphoreType.DMA((4, 4)),
            pltpu.SemaphoreType.DMA,
        ],
        compiler_params=params(),
        cost_estimate=cost(
            flops=2 * count * D * (D + 2 * FF), bytes_accessed=count * D * 40, transcendentals=count * FF
        ),
        name="mid_fwd",
    )(gw, wa, ctx, tokens, cotangent, vec)


def pick(mine, even, odd):
    return jnp.where(mine == 0, even, odd), jnp.where(mine == 0, odd, even)


def ffn_bwd_kernel(
    me_ref, gw_ref, dz_ref, yb_ref, dh2_ref, g_ref, gp_ref, vg_in_ref,
    dw1k_ref, dw1s_ref, dw2k_ref, dw2s_ref, vg_ref, dy1_ref,
    w1_s, w2_s, ybt_s, du_s, r_s, sems,
):
    chunk = pl.program_id(0)
    me = me_ref[0]
    core, my_x, my_y = me & 1, (me >> 1) & 1, (me >> 2) & 1
    copies = mid_copies(gw_ref, w1_s, w2_s, sems)
    count = dz_ref.shape[0]
    steps = count // MID_TILE

    @pl.when(chunk == 0)
    def _():
        for group in copies:
            for copy in group:
                copy.start()
        vg_ref[...] = vg_in_ref[...]
        ybt_s[...] = yb_ref[...].T

    for index in range(4):

        @pl.when(chunk == index)
        def _(index=index):
            for copy in copies[index]:
                copy.wait()

    def grad_act(i, total):
        rows = pl.ds(pl.multiple_of(i * MID_TILE, MID_TILE), MID_TILE)
        dg = dot(dz_ref[rows, :], down_chunk(w2_s, chunk), NT)
        du = (gp_ref[rows, :].astype(F32) * dg).astype(BF)
        du_s[rows, :] = du
        back = dot(du, up_chunk(w1_s, chunk), NT)

        @pl.when(chunk == 0)
        def _():
            dy1_ref[rows, :] = dh2_ref[rows, :] + back

        @pl.when(chunk > 0)
        def _():
            dy1_ref[rows, :] += back

        return total + jnp.sum(du.astype(F32), axis=0, keepdims=True)

    db1 = lax.fori_loop(0, steps, grad_act, jnp.zeros((1, D), F32))
    put_row(vg_ref, 5 + chunk, db1)

    r_s[...] = dot(ybt_s[...], du_s[...], NN).astype(BF)
    for pair in range(8):
        even, odd = r_s[pl.ds(pair * 96, 48), :], r_s[pl.ds(pair * 96 + 48, 48), :]
        keep, send = pick(core, even, odd)
        place = ((((pair >> 1) & 1) ^ my_y) << 1) | ((pair & 1) ^ my_x)
        for col in range(6):
            lanes = slice(col * 128, col * 128 + 128)
            dw1k_ref[place, pair >> 2, :, col] = keep[:, lanes].reshape(3, 16, 128)
            dw1s_ref[place, pair >> 2, :, col] = send[:, lanes].reshape(3, 16, 128)

    r_s[...] = dot(g_ref[...], dz_ref[...], TN).astype(BF)
    for pair in range(2):
        even, odd = r_s[pl.ds(pair * 384, 192), :], r_s[pl.ds(pair * 384 + 192, 192), :]
        keep, send = pick(core, even, odd)
        for col in range(6):
            lanes = slice(col * 128, col * 128 + 128)
            dw2k_ref[pair ^ my_x, 0, :, col] = keep[:, lanes].reshape(12, 16, 128)
            dw2s_ref[pair ^ my_x, 0, :, col] = send[:, lanes].reshape(12, 16, 128)


def ffn_bwd(me, gw, dz, yb, dh2, g, gp, vg):
    count = dz.shape[0]
    full = pl.BlockSpec((count, D), lambda c, m: (0, 0))
    part = pl.BlockSpec((count, D), lambda c, m: (0, c))
    up = pl.BlockSpec((4, 2, 3, 6, 16, 128), lambda c, m: (0, 0, 0, c, 0, 0))
    down = pl.BlockSpec(
        (2, 1, 12, 6, 16, 128), lambda c, m: ((c % 2) ^ ((m[0] >> 2) & 1), c // 2, 0, 0, 0, 0)
    )
    shape = jax.ShapeDtypeStruct
    return pl.pallas_call(
        ffn_bwd_kernel,
        grid_spec=pltpu.PrefetchScalarGridSpec(
            num_scalar_prefetch=1,
            grid=(4,),
            in_specs=[ANY, full, full, full, part, part, whole((VEC_ROWS, 128))],
            out_specs=[up, up, down, down, whole((VEC_ROWS, 128)), full],
            scratch_shapes=[
                pltpu.VMEM((16, FFN_TILES, 16, 128), BF),
                pltpu.VMEM((16, FFN_TILES, 16, 128), BF),
                pltpu.VMEM((D, count), BF),
                pltpu.VMEM((count, D), BF),
                pltpu.VMEM((D, D), BF),
                pltpu.SemaphoreType.DMA((4, 4)),
            ],
        ),
        out_shape=[shape((4, 2, 3, 24, 16, 128), BF)] * 2
        + [shape((4, 2, 12, 6, 16, 128), BF)] * 2
        + [shape((VEC_ROWS, 128), F32), shape((count, D), F32)],
        compiler_params=params(),
        cost_estimate=cost(
            flops=8 * count * D * FF, bytes_accessed=count * D * 40, transcendentals=0
        ),
        name="ffn_bwd",
    )(me, gw, dz, yb, dh2, g, gp, vg)


def norm_bwd_kernel(
    wa_ref, dy1_ref, n1_ref, rstd_ref, keep_ref, vec_ref, vg_in_ref,
    dh1_ref, dctx_ref, da_ref, vg_ref,
    wo_s, sums_s, sem,
):
    step = pl.program_id(0)
    copy = pltpu.make_async_copy(wa_ref.at[pl.ds(24, 8)], wo_s, sem)

    @pl.when(step == 0)
    def _():
        copy.start()
        vg_ref[...] = vg_in_ref[...]
        sums_s[...] = jnp.zeros_like(sums_s)

    dy1 = dy1_ref[...]
    normed = n1_ref[...]
    t = dy1 * row(vec_ref, 3)
    mean_t = jnp.mean(t, axis=1, keepdims=True)
    mean_tn = jnp.mean(t * normed, axis=1, keepdims=True)
    dh1 = (t - mean_t - normed * mean_tn) * rstd_ref[:, 0:1]
    dh1_ref[...] = dh1
    da = dh1.astype(BF)
    da_ref[...] = da
    sums_s[0:1, :] += jnp.sum(da.astype(F32), axis=0, keepdims=True)
    sums_s[1:2, :] += jnp.sum(dy1 * normed, axis=0, keepdims=True)
    sums_s[2:3, :] += jnp.sum(dy1, axis=0, keepdims=True)

    @pl.when(step == 0)
    def _():
        copy.wait()

    back = dot(da, square(wo_s, 0), NT).astype(BF).astype(F32)
    dctx_ref[...] = (back * keep_ref[...]).astype(BF)

    @pl.when(step == pl.num_programs(0) - 1)
    def _():
        for i in range(3):
            put_row(vg_ref, 2 + i, sums_s[i : i + 1, :])


def norm_bwd(wa, dy1, n1, rstd, keep, vec, vg):
    count = dy1.shape[0]
    tile = MID_TILE
    rows = pl.BlockSpec((tile, D), lambda i: (i, 0))
    shape = jax.ShapeDtypeStruct
    return pl.pallas_call(
        norm_bwd_kernel,
        grid=(count // tile,),
        in_specs=[
            ANY,
            rows,
            rows,
            pl.BlockSpec((tile, 128), lambda i: (i, 0)),
            pl.BlockSpec((tile, 1), lambda i: (i, 0)),
            whole((VEC_ROWS, 128)),
            whole((VEC_ROWS, 128)),
        ],
        out_specs=[rows, rows, rows, whole((VEC_ROWS, 128))],
        scratch_shapes=[
            pltpu.VMEM((8, ATTN_TILES, 16, 128), BF),
            pltpu.VMEM((8, D), F32),
            pltpu.SemaphoreType.DMA,
        ],
        out_shape=[
            shape((count, D), F32),
            shape((count, D), BF),
            shape((count, D), BF),
            shape((VEC_ROWS, 128), F32),
        ],
        compiler_params=params(),
        cost_estimate=cost(
            flops=2 * count * D * D, bytes_accessed=count * D * 16, transcendentals=0
        ),
        name="norm_bwd",
    )(wa, dy1, n1, rstd, keep, vec, vg)


def attn_bwd_kernel(
    first, q_ref, k_ref, v_ref, ctx_ref, dctx_ref, lse_ref, segc_ref, segr_ref, d_ref, lse_s,
):
    col = pl.program_id(1) + first

    @pl.when(col == first)
    def _():
        lse_s[...] = lse_ref[...].T

    query, key, value, dctx = q_ref[...], k_ref[...], v_ref[...], dctx_ref[...]
    lane = lax.broadcasted_iota(jnp.int32, (1, 128), 1)
    low = lane < 64
    zero = jnp.zeros((), BF)
    queries = [jnp.where(low, query, zero), jnp.where(low, zero, query)]
    keys = [jnp.where(low, key, zero), jnp.where(low, zero, key)]
    dctxs = [jnp.where(low, dctx, zero), jnp.where(low, zero, dctx)]
    products = (dctx.astype(F32) * ctx_ref[...].astype(F32)).T
    row_dots = [
        jnp.sum(products[:64], axis=0, keepdims=True),
        jnp.sum(products[64:], axis=0, keepdims=True),
    ]
    lses = [lse_s[pl.ds(2 * col + head, 1), :] for head in range(2)]
    seg_row = segr_ref[...]
    dq_t = jnp.zeros((128, SLOTS), F32)
    for block in range(4):
        rows = slice(block * 128, block * 128 + 128)
        allowed = segc_ref[rows, :] == seg_row
        dv = jnp.zeros((128, 128), F32)
        dk = jnp.zeros((128, 128), F32)
        for head in range(2):
            scores = dot(key[rows], queries[head], NT) * 0.125
            prob = jnp.where(allowed, jnp.exp(scores - lses[head]), 0.0)
            dv = dv + dot(prob.astype(BF), dctxs[head], NN)
            dprob = dot(value[rows], dctxs[head], NT)
            dscore = (prob * (dprob - row_dots[head])).astype(BF)
            dk = dk + dot(dscore, queries[head], NN)
            dq_t = dq_t + dot(keys[head][rows], dscore, TN)
        d_ref[1, rows, :] = (dk * 0.125).astype(BF)
        d_ref[2, rows, :] = dv.astype(BF)
    d_ref[0] = (dq_t.T * 0.125).astype(BF)


def attn_bwd(query, key, value, ctx, dctx, lse, segc, segr, first, cols):
    count = query.shape[0]
    rows = count // SLOTS
    part = pl.BlockSpec((SLOTS, 128), lambda r, j: (r, j + first))
    slot = pl.BlockSpec((SLOTS, 1), lambda r, j: (r, 0))
    return pl.pallas_call(
        functools.partial(attn_bwd_kernel, first),
        grid=(rows, cols),
        in_specs=[part] * 5
        + [
            pl.BlockSpec((SLOTS, 128), lambda r, j: (r, 0)),
            slot,
            pl.BlockSpec((None, 1, SLOTS), lambda r, j: (r, 0, 0)),
        ],
        out_specs=pl.BlockSpec((3, SLOTS, 128), lambda r, j: (0, r, j)),
        out_shape=jax.ShapeDtypeStruct((3, count, 128 * cols), BF),
        scratch_shapes=[pltpu.VMEM((128, SLOTS), F32)],
        compiler_params=params(),
        cost_estimate=cost(
            flops=10 * count * D * SLOTS, bytes_accessed=count * D * 16, transcendentals=count * SLOTS * 12
        ),
        name="attn_bwd",
    )(query, key, value, ctx, dctx, lse, segc, segr)


def proj_grad_kernel(first, me_ref, x_ref, ctx_ref, d_ref, da_ref, vg_in_ref, dwk_ref, dws_ref, vg_ref, t_s, r_s):
    step = pl.program_id(0)
    me = me_ref[0]
    core, my_x, my_y = me & 1, (me >> 1) & 1, (me >> 2) & 1

    @pl.when(step == 0)
    def _():
        t_s[...] = x_ref[...].T
        vg_ref[...] = vg_in_ref[...]

    @pl.when(step == 3)
    def _():
        t_s[...] = ctx_ref[...].T

    grad = jnp.where(step == 3, da_ref[...], d_ref[...])

    @pl.when((step == 0) | (step == 2))
    def _():
        put_row(vg_ref, step >> 1, jnp.sum(grad.astype(F32), axis=0, keepdims=True), first)

    r_s[...] = dot(t_s[...], grad, NN).astype(BF)
    for pair in range(4):
        even, odd = r_s[pl.ds(pair * 192, 96), :], r_s[pl.ds(pair * 192 + 96, 96), :]
        keep, send = pick(core, even, odd)
        place = (((pair >> 1) ^ my_y) << 1) | ((pair & 1) ^ my_x)
        for col in range(r_s.shape[1] // 128):
            lanes = slice(col * 128, col * 128 + 128)
            dwk_ref[place, 0, :, col] = keep[:, lanes].reshape(6, 16, 128)
            dws_ref[place, 0, :, col] = send[:, lanes].reshape(6, 16, 128)


def proj_grad(me, tokens, ctx, grads, da, vg, first):
    count, width = grads.shape[1:]
    cols = width // 128
    out = pl.BlockSpec((4, 1, 6, cols, 16, 128), lambda i, m: (0, i, 0, 0, 0, 0))
    full = pl.BlockSpec((count, D), lambda i, m: (0, 0))
    shape = jax.ShapeDtypeStruct
    return pl.pallas_call(
        functools.partial(proj_grad_kernel, first),
        grid_spec=pltpu.PrefetchScalarGridSpec(
            num_scalar_prefetch=1,
            grid=(4,),
            in_specs=[
                full,
                full,
                pl.BlockSpec((None, count, width), lambda i, m: (jnp.minimum(i, 2), 0, 0)),
                pl.BlockSpec((count, width), lambda i, m: (0, first // cols)),
                whole((VEC_ROWS, 128)),
            ],
            out_specs=[out, out, whole((VEC_ROWS, 128))],
            scratch_shapes=[pltpu.VMEM((D, count), BF), pltpu.VMEM((D, width), BF)],
        ),
        out_shape=[shape((4, 4, 6, cols, 16, 128), BF)] * 2 + [shape((VEC_ROWS, 128), F32)],
        compiler_params=params(),
        cost_estimate=cost(
            flops=8 * count * D * width, bytes_accessed=count * D * 14, transcendentals=0
        ),
        name="proj_grad",
    )(me, tokens, ctx, grads, da, vg)


def input_grad_kernel(wa_ref, dh1_ref, da_ref, db_ref, out_ref, w_s, sems):
    @pl.when(pl.program_id(0) == 0)
    def _():
        copies = [
            pltpu.make_async_copy(
                wa_ref.at[pl.ds(8 * m, 8)],
                w_s.at[pl.ds(8 * m, 8)],
                sems.at[m],
            )
            for m in range(3)
        ]
        for copy in copies:
            copy.start()
        for copy in copies:
            copy.wait()

    total = dh1_ref[...]
    for m in range(3):
        grad = jnp.concatenate([da_ref[m], db_ref[m]], axis=1)
        total = total + dot(grad, square(w_s, 8 * m), NT)
    out_ref[...] = total.astype(BF)


def input_grad(wa, dh1, first, second):
    count = dh1.shape[0]
    rows = pl.BlockSpec((MID_TILE, D), lambda i: (i, 0))
    return pl.pallas_call(
        input_grad_kernel,
        grid=(count // MID_TILE,),
        in_specs=[ANY, rows] + [pl.BlockSpec((3, MID_TILE, D // 2), lambda i: (0, i, 0))] * 2,
        out_specs=rows,
        out_shape=jax.ShapeDtypeStruct((count, D), BF),
        scratch_shapes=[
            pltpu.VMEM((24, ATTN_TILES, 16, 128), BF),
            pltpu.SemaphoreType.DMA((3,)),
        ],
        compiler_params=params(),
        cost_estimate=cost(
            flops=6 * count * D * D, bytes_accessed=count * D * 18, transcendentals=0
        ),
        name="input_grad",
    )(wa, dh1, first, second)


def retile(flat, blocks):
    tall = flat.shape[0] // (16 * blocks)
    tiles = flat.reshape(tall, 16, blocks, 128).transpose(0, 2, 1, 3)
    return tiles.reshape(tall * blocks, 16, 128)


def untile(tiles, blocks):
    tall = tiles.shape[0] // blocks
    flat = tiles.reshape(tall, blocks, 16, 128).transpose(0, 2, 1, 3)
    return flat.reshape(tall * blocks * 16, 128)


def gather_ffn(ffn, size):
    if size == OWNERS:
        upper = lax.axis_index("fsdp") < OWNERS // 2
        mine = jnp.where(upper, retile(ffn, 24), retile(ffn, 6))
        return lax.all_gather(mine, "fsdp", axis=0, tiled=False)
    ffn = lax.all_gather(ffn, "fsdp", axis=0, tiled=True)
    half = ffn.shape[0] // 2
    tiles = jnp.concatenate([retile(ffn[:half], 24), retile(ffn[half:], 6)], axis=0)
    return tiles.reshape(OWNERS, FFN_TILES, 16, 128)


def pad_vectors(flat):
    return jnp.pad(flat, (0, VEC_ROWS * 128 - flat.shape[0])).reshape(VEC_TILES, 16, 128)


def gather_attn(attn, vectors, size):
    if size != OWNERS:
        attn = lax.all_gather(attn, "fsdp", axis=0, tiled=True)
        vec = lax.all_gather(vectors, "fsdp", axis=0, tiled=True)
        return [retile(attn, 6).reshape(OWNERS, ATTN_TILES, 16, 128)], pad_vectors(vec)[None]
    tiles = retile(attn, 6)
    each = vectors.shape[0]
    flat = jnp.zeros((VEC_ROWS * 128,), BF)
    vec = lax.dynamic_update_slice(flat, vectors, (lax.axis_index("fsdp") * each,))
    vec = vec.reshape(VEC_TILES, 16, 128)
    mine_q, mine_p = tiles[:Q_TILES], jnp.concatenate([tiles[Q_TILES:], vec], axis=0)
    planes = [mine_q] + [hop(mine_q, 8 * step) for step in (1, 2, 3)]
    chips = [mine_p] + [hop(mine_p, 2 * side) for side in (1, 2, 3)]
    across = jnp.stack(planes, axis=0)
    vec = sum(chip[P_TILES:].astype(F32) for chip in chips).astype(BF)
    along = jnp.concatenate([chip[:P_TILES] for chip in chips] + [vec], axis=0)
    arrays = [across] + [hop(across, 2 * side) for side in (1, 2, 3)]
    arrays += [along] + [hop(along, 8 * step) for step in (1, 2, 3)]
    arrays += [hop(array, 1) for array in arrays]
    vecs = [array[4 * P_TILES :] for array in arrays[4:8] + arrays[12:16]]
    return arrays, jnp.stack(vecs, axis=0)


def hop(value, bit):
    pairs = [(i, i ^ bit) for i in range(OWNERS)]
    return lax.ppermute(value, "fsdp", pairs)


def reduce_plain(ffn_terms, attn_terms, vector_terms):
    def absolute(keep, send):
        planes = keep.shape[1]
        both = jnp.stack([keep, send], axis=1)
        return jnp.moveaxis(both, 2, 0).reshape(planes * 8, -1, 16, 128)

    dw1k, dw1s, dw2k, dw2s = ffn_terms
    up = untile(absolute(dw1k, dw1s).reshape(-1, 16, 128), 24)
    down = untile(absolute(dw2k, dw2s).reshape(-1, 16, 128), 6)
    proj = untile(absolute(*attn_terms).reshape(-1, 16, 128), 6)

    def scatter(value):
        return lax.psum_scatter(value.astype(F32), "fsdp", scatter_dimension=0, tiled=True)

    return scatter(proj), scatter(jnp.concatenate([up, down], axis=0)), scatter(vector_terms)


class Reduction:
    def __init__(self, keeps, sends, vec=None):
        self.keeps = keeps
        self.hops = [hop(send, 1) for send in sends]
        self.vec = vec
        if vec is not None:
            self.hops.append(hop(vec.astype(BF), 1))

    def part(self, place, upper):
        pieces = []
        for a, b in zip(self.keeps, self.received, strict=True):
            half = a.shape[1] // 2
            cut = slice(half, None) if upper else slice(0, half)
            piece = a[place, cut].astype(F32) + b[place, cut].astype(F32)
            pieces.append(piece.reshape((-1, 16, 128)))
        return jnp.concatenate(pieces, axis=0) if len(pieces) > 1 else pieces[0]

    def ride(self, message):
        message = message.astype(BF)
        if self.vec is None:
            return message
        return jnp.concatenate([message, self.vec.astype(BF)], axis=0)

    def landed(self, message):
        if self.vec is None:
            return message
        self.vec = self.vec + message[-VEC_TILES:].astype(F32)
        return message[:-VEC_TILES]

    def corner(self):
        self.received = self.hops[: len(self.keeps)]
        if self.vec is not None:
            self.vec = self.vec + self.hops[-1].astype(F32)
        self.hops = [hop(self.ride(self.part(3, False)), 2), hop(self.part(3, True).astype(BF), 4)]

    def sides(self):
        via_x, via_y = self.landed(self.hops[0]), self.hops[1]
        to_x = jnp.concatenate([self.part(1, False), self.part(1, True) + via_y.astype(F32)])
        to_y = jnp.concatenate([self.part(2, False) + via_x.astype(F32), self.part(2, True)])
        self.hops = [hop(to_x.astype(BF), 2), hop(self.ride(to_y), 4)]

    def planes(self, my_z, arrange):
        from_x, from_y = self.hops[0], self.landed(self.hops[1])
        own = jnp.concatenate([self.part(0, False), self.part(0, True)])
        own = arrange(own + from_x.astype(F32) + from_y.astype(F32))
        self.mine = lax.dynamic_index_in_dim(own, my_z, 0, keepdims=False)
        low = own.astype(BF)
        self.hops = [
            hop(self.ride(lax.dynamic_index_in_dim(low, my_z ^ step, 0, keepdims=False)), 8 * step)
            for step in (1, 2, 3)
        ]

    def total(self):
        return self.mine + sum(self.landed(other).astype(F32) for other in self.hops)


def meet(hops, values):
    return lax.optimization_barrier((hops, values))


def tiles_of(array):
    return array.reshape(array.shape[:2] + (-1, 16, 128))


def layer(tokens, attn_matrices, ffn_matrices, vectors, segments, pad_segment, cotangent, size):
    fast = size == OWNERS
    gw = gather_ffn(ffn_matrices, size)
    pieces, vecs = gather_attn(attn_matrices, vectors, size)
    place = lax.axis_index("fsdp") if fast else jnp.zeros((), jnp.int32)
    me = place.reshape(1).astype(jnp.int32)
    my_z = place >> 3
    rows = segments.shape[0]
    segc = segments.reshape(rows * SLOTS, 1)
    segr = segments.reshape(rows, 1, SLOTS)
    keep = (segments != pad_segment[:, None]).astype(F32).reshape(rows * SLOTS, 1)

    query, key, value, ctx, lse, wa, vec = attn_fwd(fast, me, pieces, vecs, tokens, segc, segr, keep)
    g, gp, n1, rstd, yb, out, dz, dh2, vg = mid_fwd(gw, wa, ctx, tokens, cotangent, vec)
    dw1k, dw1s, dw2k, dw2s, vg, dy1 = ffn_bwd(me, gw, dz, yb, dh2, g, gp, vg)
    if not fast:
        dh1, dctx, da, vg = norm_bwd(wa, dy1, n1, rstd, keep, vec, vg)
        first = attn_bwd(query, key, value, ctx, dctx, lse, segc, segr, 0, 3)
        dwak, dwas, vg = proj_grad(me, tokens, ctx, first, da, vg, 0)
        second = attn_bwd(query, key, value, ctx, dctx, lse, segc, segr, 3, 3)
        dwbk, dwbs, vg = proj_grad(me, tokens, ctx, second, da, vg, 3)
        dx = input_grad(wa, dh1, first, second)
        attn_terms = [jnp.concatenate(pair, axis=3) for pair in ((dwak, dwbk), (dwas, dwbs))]
        vector_terms = vg.reshape(-1)[: 12 * D]
        return (out, dx) + reduce_plain((dw1k, dw1s, dw2k, dw2s), attn_terms, vector_terms)

    def arrange_ffn(own):
        own = own.reshape(2, 2, FFN_TILES, 16, 128).transpose(1, 0, 2, 3, 4)
        return own.reshape(4, FFN_TILES, 16, 128)

    def arrange_attn(own):
        return own.reshape(4, ATTN_TILES // 2, 16, 128)

    ffn = Reduction([tiles_of(dw1k), tiles_of(dw2k)], [tiles_of(dw1s), tiles_of(dw2s)])
    dh1, dctx, da, vg = norm_bwd(wa, dy1, n1, rstd, keep, vec, vg)
    ffn.hops, (dh1, dctx, da, vg) = meet(ffn.hops, (dh1, dctx, da, vg))
    ffn.corner()
    first = attn_bwd(query, key, value, ctx, dctx, lse, segc, segr, 0, 3)
    ffn.hops, (first, dctx) = meet(ffn.hops, (first, dctx))
    ffn.sides()
    dwak, dwas, vg = proj_grad(me, tokens, ctx, first, da, vg, 0)
    left = Reduction([tiles_of(dwak)], [tiles_of(dwas)])
    second = attn_bwd(query, key, value, ctx, dctx, lse, segc, segr, 3, 3)
    (ffn.hops, left.hops), second = meet((ffn.hops, left.hops), second)
    ffn.planes(my_z, arrange_ffn)
    left.corner()
    dwbk, dwbs, vg = proj_grad(me, tokens, ctx, second, da, vg, 3)
    left.hops, (dwbk, dwbs, vg) = meet(left.hops, (dwbk, dwbs, vg))
    right = Reduction(
        [tiles_of(dwbk)], [tiles_of(dwbs)], vg.reshape(VEC_TILES, 16, 128)
    )
    left.sides()
    dx = input_grad(wa, dh1, first, second)
    (right.hops, left.hops, ffn.hops), dx = meet((right.hops, left.hops, ffn.hops), dx)
    right.corner()
    left.planes(my_z, arrange_attn)
    right.sides()
    right.planes(my_z, arrange_attn)

    upper = place < OWNERS // 2
    ffn_sum = ffn.total()
    ffn_grad = jnp.where(upper, untile(ffn_sum, 24), untile(ffn_sum, 6))
    halves = [r.total().reshape(6, 3, 16, 128) for r in (left, right)]
    attn_grad = untile(jnp.concatenate(halves, axis=1).reshape(ATTN_TILES, 16, 128), 6)
    each = vectors.shape[0]
    vector_grad = lax.dynamic_slice(right.vec.reshape(-1), (place * each,), (each,))
    return out, dx, attn_grad, ffn_grad, vector_grad


def solution(mesh):
    size = mesh.shape["fsdp"]
    return jax.shard_map(
        functools.partial(layer, size=size),
        mesh=mesh,
        in_specs=(
            P("fsdp", None),
            P("fsdp", None),
            P("fsdp", None),
            P("fsdp"),
            P("fsdp", None),
            P("fsdp"),
            P("fsdp", None),
        ),
        out_specs=(P("fsdp", None), P("fsdp", None), P("fsdp", None), P("fsdp", None), P("fsdp")),
        check_vma=False,
    )
```

```python
import functools

import jax
import jax.numpy as jnp
from jax import lax
from jax.experimental import pallas as pl
from jax.experimental.pallas import tpu as pltpu
from jax.sharding import PartitionSpec as P

D = 768
FF = 3072
SLOTS = 512
BF = jnp.bfloat16
F32 = jnp.float32
NN = ((1,), (0,))
NT = ((1,), (1,))
TN = ((0,), (0,))
OWNERS = 32
ATTN_TILES = 36
FFN_TILES = 72
COST_SCALE = 1
VMEM_LIMIT = 60 * 1024 * 1024

TAIL_SLOPE = 0.39 * 0.5**0.5
TAIL_POLY = (
    0.11766260955586648,
    0.04569420719462487,
    0.32477969950633645,
    -0.3177001395785759,
    0.44333218507090993,
    -0.11376856259852677,
)


def dot(left, right, dims):
    return lax.dot_general(left, right, (dims, ((), ())), preferred_element_type=F32)


def params(**kwargs):
    return pltpu.CompilerParams(vmem_limit_bytes=VMEM_LIMIT, **kwargs)


def cost(flops, bytes_accessed, transcendentals):
    return pl.CostEstimate(
        flops=flops // COST_SCALE,
        bytes_accessed=bytes_accessed // COST_SCALE,
        transcendentals=transcendentals // COST_SCALE,
    )


def whole(shape):
    zeros = (0,) * len(shape)
    return pl.BlockSpec(shape, lambda *_: zeros)


ANY = pl.BlockSpec(memory_space=pl.ANY)
VEC_TILES = 5
VEC_ROWS = 16 * VEC_TILES


def row(vec_ref, index, width=D):
    blocks = width // 128
    return jnp.concatenate([vec_ref[pl.ds(6 * index + i, 1), :] for i in range(blocks)], axis=1)


def put_row(vec_ref, index, value, first=0):
    for i in range(value.shape[1] // 128):
        vec_ref[pl.ds(6 * index + first + i, 1), :] = value[:, 128 * i : 128 * i + 128]


def square_cols(tiles, first, col):
    parts = [tiles[pl.ds(first, 8), i * 6 + col] for i in range(6)]
    return jnp.stack(parts, axis=1).reshape(D, 128)


def square(tiles, first):
    return jnp.concatenate([square_cols(tiles, first, col) for col in range(6)], axis=1)


def up_chunk(tiles, chunk):
    cols = []
    for col in range(6):
        parts = [tiles[:, i * 24 + chunk * 6 + col] for i in range(3)]
        cols.append(jnp.stack(parts, axis=1).reshape(D, 128))
    return jnp.concatenate(cols, axis=1)


def down_chunk(tiles, chunk):
    cols = []
    for col in range(6):
        parts = [tiles[pl.ds(4 * chunk, 4), i * 6 + col] for i in range(12)]
        cols.append(jnp.stack(parts, axis=1).reshape(D, 128))
    return jnp.concatenate(cols, axis=1)


Q_TILES = 24
P_TILES = ATTN_TILES - Q_TILES


def attn_copies(fast, me, refs, w_s, sems):
    if not fast:
        return [pltpu.make_async_copy(refs[0], w_s, sems.at[0])]
    yxc, my_z = me & 7, me >> 3
    copies = []
    for core in range(2):
        for side in range(4):
            place = yxc ^ (2 * side + core)
            across, along = refs[8 * core + side], refs[8 * core + 4 + side]
            for z in range(4):
                copies.append((across.at[my_z ^ z], w_s.at[8 * z + place, pl.ds(0, Q_TILES)]))
            for other in range(4):
                owner = 8 * (my_z ^ side) + (yxc ^ (2 * other + core))
                tiles = along.at[pl.ds(other * P_TILES, P_TILES)]
                copies.append((tiles, w_s.at[owner, pl.ds(Q_TILES, P_TILES)]))
    return [pltpu.make_async_copy(src, dst, sems.at[i]) for i, (src, dst) in enumerate(copies)]


def attn_fwd_kernel(fast, me_ref, span_ref, *args):
    count = 16 if fast else 1
    refs = args[:count]
    (
        vec_ref, x_ref, segc_ref, segr_ref,
        q_ref, k_ref, v_ref, ctx_ref, lse_ref, wa_ref, vec_out_ref,
        w_s, vt_s, sems, out_sem,
    ) = args[count:]
    line, col = pl.program_id(0), pl.program_id(1)
    first_step = (line == 0) & (col == 0)
    last_step = (line == pl.num_programs(0) - 1) & (col == pl.num_programs(1) - 1)
    out_copy = pltpu.make_async_copy(w_s, wa_ref, out_sem)

    @pl.when(first_step)
    def _():
        copies = attn_copies(fast, me_ref[0], refs, w_s, sems)
        for copy in copies:
            copy.start()
        vec = vec_ref[0].astype(F32)
        for i in range(1, vec_ref.shape[0]):
            vec = vec + vec_ref[i].astype(F32)
        vec_out_ref[...] = vec.reshape(VEC_ROWS, 128)
        for copy in copies:
            copy.wait()
        out_copy.start()

    @pl.when(last_step)
    def _():
        out_copy.wait()

    cols = [2 * col, 2 * col + 1]
    weight = jnp.concatenate([square_cols(w_s, 8 * m, c) for m in range(3) for c in cols], axis=1)
    qkv = dot(x_ref[...], weight, NN)
    bias_q = jnp.concatenate([vec_out_ref[pl.ds(c, 1), :] for c in cols], axis=1)
    bias_v = jnp.concatenate([vec_out_ref[pl.ds(6 + c, 1), :] for c in cols], axis=1)
    q_ref[...] = (qkv[:, :256] + bias_q).astype(BF) * 0.125
    k_ref[...] = qkv[:, 256:512].astype(BF)
    v_ref[...] = (qkv[:, 512:] + bias_v).astype(BF)
    lane = lax.broadcasted_iota(jnp.int32, (1, 128), 1)
    low = lane < 64
    zero = jnp.zeros((), BF)

    for pair in range(2):
        vt_s[pl.ds(128 * pair, 128), :] = v_ref[:, 128 * pair : 128 * pair + 128].T

    def attend(block, carry):
        rows = pl.ds(pl.multiple_of(block * 128, 128), 128)
        start, count = span_ref[line, 2 * block], span_ref[line, 2 * block + 1]

        @pl.when(count == 0)
        def _():
            ctx_ref[rows, :] = jnp.zeros((128, 256), BF)
            lse_ref[:, rows] = jnp.zeros((4, 128), F32)

        def window(size):
            @pl.when(count == size)
            def _():
                seen = pl.ds(pl.multiple_of(start * 128, 128), 128 * size)
                seg_row = segr_ref[:, rows]
                blocked = jnp.where(segc_ref[seen, :] == seg_row, 0.0, -1e30)
                keep = jnp.where(jnp.broadcast_to(seg_row, (64, 128)) < 0, 0.0, 1.0)
                scores = []
                for head in range(4):
                    lanes = slice(128 * (head // 2), 128 * (head // 2) + 128)
                    query = q_ref[rows, lanes]
                    query = jnp.where(low, query, zero) if head % 2 == 0 else jnp.where(low, zero, query)
                    scores.append(dot(k_ref[seen, lanes], query, NT) + blocked)
                tops = [jnp.max(score, axis=0, keepdims=True) for score in scores]
                expds = [jnp.exp(score - top) for score, top in zip(scores, tops)]
                totals = [jnp.sum(expd, axis=0, keepdims=True) for expd in expds]
                outs = []
                for head in range(4):
                    values = vt_s[pl.ds(64 * head, 64), seen]
                    out = dot(values, expds[head].astype(BF), NN)
                    outs.append(out * (1.0 / totals[head]) * keep)
                    lse_ref[pl.ds(head, 1), rows] = tops[head] + jnp.log(totals[head])
                ctx_ref[rows, :] = jnp.concatenate(outs, axis=0).T.astype(BF)

        for size in range(1, 5):
            window(size)
        return carry

    lax.fori_loop(0, 4, attend, 0)


def attn_fwd(fast, me, span, pieces, vec, tokens, segc, segr):
    count = tokens.shape[0]
    rows = count // SLOTS
    part = pl.BlockSpec((SLOTS, 256), lambda r, j, m, s: (r, j))
    slot = pl.BlockSpec((SLOTS, 1), lambda r, j, m, s: (r, 0))
    shape = jax.ShapeDtypeStruct
    return pl.pallas_call(
        functools.partial(attn_fwd_kernel, fast),
        grid_spec=pltpu.PrefetchScalarGridSpec(
            num_scalar_prefetch=2,
            grid=(rows, 3),
            in_specs=[ANY] * len(pieces)
            + [
                whole(vec.shape),
                pl.BlockSpec((SLOTS, D), lambda r, j, m, s: (r, 0)),
                slot,
                pl.BlockSpec((None, 1, SLOTS), lambda r, j, m, s: (r, 0, 0)),
            ],
            out_specs=[part] * 4
            + [pl.BlockSpec((None, None, 4, SLOTS), lambda r, j, m, s: (r, j, 0, 0)), ANY, whole((VEC_ROWS, 128))],
            scratch_shapes=[
                pltpu.VMEM((OWNERS, ATTN_TILES, 16, 128), BF),
                pltpu.VMEM((256, SLOTS), BF),
                pltpu.SemaphoreType.DMA((64,)),
                pltpu.SemaphoreType.DMA,
            ],
        ),
        out_shape=[shape((count, D), BF)] * 4
        + [
            shape((rows, 3, 4, SLOTS), F32),
            shape((OWNERS, ATTN_TILES, 16, 128), BF),
            shape((VEC_ROWS, 128), F32),
        ],
        compiler_params=params(),
        cost_estimate=cost(
            flops=2 * count * D * (3 * D + 4 * SLOTS), bytes_accessed=count * D * 12, transcendentals=count * SLOTS * 12
        ),
        name="attn_fwd",
    )(me, span, *pieces, vec, tokens, segc, segr)


def norm_parts(hidden):
    mean = jnp.mean(hidden, axis=1, keepdims=True)
    centered = hidden - mean
    var = jnp.mean(centered * centered, axis=1, keepdims=True)
    rstd = lax.rsqrt(var + 1e-12)
    return centered * rstd, rstd


def gelu_parts(u):
    size = jnp.abs(u)
    t = pl.reciprocal(1.0 + TAIL_SLOPE * size)
    poly = jnp.full_like(t, TAIL_POLY[-1])
    for coef in TAIL_POLY[-2::-1]:
        poly = poly * t + coef
    bell = jnp.exp(u * u * -0.5)
    tail = poly * t * bell
    phi_cdf = jnp.where(u > 0, 1.0 - tail, tail)
    return u * phi_cdf, phi_cdf + u * bell * 0.3989422804014327


NORM_TILE = 256


def norm_fwd_kernel(wa_ref, ctx_ref, x_ref, vec_ref, n1_ref, rstd_ref, wo_s, sem):
    copy = pltpu.make_async_copy(wa_ref.at[pl.ds(24, 8)], wo_s, sem)

    @pl.when(pl.program_id(0) == 0)
    def _():
        copy.start()
        copy.wait()

    hidden = x_ref[...].astype(F32) + dot(ctx_ref[...], square(wo_s, 0), NN) + row(vec_ref, 2)
    normed, rstd = norm_parts(hidden)
    n1_ref[...] = normed
    rstd_ref[...] = jnp.broadcast_to(rstd, rstd_ref.shape)


def norm_fwd(wa, ctx, tokens, vec):
    count = tokens.shape[0]
    rows = pl.BlockSpec((NORM_TILE, D), lambda i: (i, 0))
    slim = pl.BlockSpec((NORM_TILE, 128), lambda i: (i, 0))
    shape = jax.ShapeDtypeStruct
    return pl.pallas_call(
        norm_fwd_kernel,
        grid=(count // NORM_TILE,),
        in_specs=[ANY, rows, rows, whole((VEC_ROWS, 128))],
        out_specs=[rows, slim],
        out_shape=[shape((count, D), F32), shape((count, 128), F32)],
        scratch_shapes=[pltpu.VMEM((8, ATTN_TILES, 16, 128), BF), pltpu.SemaphoreType.DMA],
        compiler_params=params(),
        cost_estimate=cost(
            flops=2 * count * D * D, bytes_accessed=count * D * 9, transcendentals=0
        ),
        name="norm_fwd",
    )(wa, ctx, tokens, vec)


def ffn_copies(gw_ref, w1_s, w2_s, sems):
    copies = []
    for chunk in range(4):
        here = []
        for i in range(3):
            tiles = pl.ds(i * 24 + chunk * 6, 6)
            here.append((gw_ref.at[pl.ds(0, 16), tiles], w1_s.at[:, tiles]))
        owners = pl.ds(4 * chunk, 4)
        here.append((gw_ref.at[pl.ds(16 + 4 * chunk, 4)], w2_s.at[owners]))
        copies.append(
            [pltpu.make_async_copy(src, dst, sems.at[chunk, i]) for i, (src, dst) in enumerate(here)]
        )
    return copies


MID_TILE = 1024


def pick(mine, even, odd):
    return jnp.where(mine == 0, even, odd), jnp.where(mine == 0, odd, even)


def ffn_kernel(
    me_ref, gw_ref, n1_ref, cot_ref, vec_ref,
    out_ref, dw1k_ref, dw1s_ref, dw2k_ref, dw2s_ref, vg_ref, dy1_ref,
    w1_s, w2_s, g_s, gp_s, yb_s, ybt_s, dz_s, du_s, r_s, sems,
):
    step = pl.program_id(0)
    me = me_ref[0]
    core, my_x, my_y = me & 1, (me >> 1) & 1, (me >> 2) & 1
    copies = ffn_copies(gw_ref, w1_s, w2_s, sems)
    count = n1_ref.shape[0]
    tiles = count // MID_TILE

    def tile(i):
        return pl.ds(pl.multiple_of(i * MID_TILE, MID_TILE), MID_TILE)

    @pl.when(step == 0)
    def _():
        for group in copies:
            for copy in group:
                copy.start()

        def body(i, carry):
            rows = tile(i)
            y_one = n1_ref[rows, :] * row(vec_ref, 3) + row(vec_ref, 4)
            yb_s[rows, :] = y_one.astype(BF)
            dy1_ref[rows, :] = y_one + row(vec_ref, 9)
            return carry

        lax.fori_loop(0, tiles, body, 0)
        ybt_s[...] = yb_s[...].T

    for index in range(4):

        @pl.when(step == index)
        def _(index=index):
            for copy in copies[index]:
                copy.wait()

    @pl.when(step < 4)
    def _():
        def body(i, carry):
            rows = tile(i)
            u = dot(yb_s[rows, :], up_chunk(w1_s, step), NN) + row(vec_ref, 5 + step)
            act, slope = gelu_parts(u)
            act = act.astype(BF)
            g_s[step, rows, :] = act
            gp_s[step, rows, :] = slope.astype(BF)
            dy1_ref[rows, :] += dot(act, down_chunk(w2_s, step), NN)
            return carry

        lax.fori_loop(0, tiles, body, 0)

    @pl.when(step == 3)
    def _():
        def body(i, carry):
            gain_sum, bias_sum, dz_sum = carry
            rows = pl.ds(pl.multiple_of(i * NORM_TILE, NORM_TILE), NORM_TILE)
            normed, rstd = norm_parts(dy1_ref[rows, :])
            gain = row(vec_ref, 10)
            out_ref[rows, :] = (normed * gain + row(vec_ref, 11)).astype(BF)
            err = cot_ref[rows, :].astype(F32)
            t = gain * err
            mean_t = jnp.mean(t, axis=1, keepdims=True)
            mean_tn = jnp.mean(t * normed, axis=1, keepdims=True)
            dh2 = (t - mean_t - normed * mean_tn) * rstd
            dz = dh2.astype(BF)
            dy1_ref[rows, :] = dh2
            dz_s[rows, :] = dz
            return (
                gain_sum + jnp.sum(err * normed, axis=0, keepdims=True),
                bias_sum + jnp.sum(err, axis=0, keepdims=True),
                dz_sum + jnp.sum(dz.astype(F32), axis=0, keepdims=True),
            )

        zero = jnp.zeros((1, D), F32)
        sums = lax.fori_loop(0, count // NORM_TILE, body, (zero, zero, zero))
        vg_ref[...] = jnp.zeros_like(vg_ref)
        put_row(vg_ref, 9, sums[2])
        put_row(vg_ref, 10, sums[0])
        put_row(vg_ref, 11, sums[1])

    @pl.when(step >= 4)
    def _():
        chunk = step - 4

        def body(i, total):
            rows = tile(i)
            dg = dot(dz_s[rows, :], down_chunk(w2_s, chunk), NT)
            du = (gp_s[chunk, rows, :].astype(F32) * dg).astype(BF)
            du_s[rows, :] = du
            dy1_ref[rows, :] += dot(du, up_chunk(w1_s, chunk), NT)
            return total + jnp.sum(du.astype(F32), axis=0, keepdims=True)

        db1 = lax.fori_loop(0, tiles, body, jnp.zeros((1, D), F32))
        put_row(vg_ref, 5 + chunk, db1)

        r_s[...] = dot(ybt_s[...], du_s[...], NN).astype(BF)
        for pair in range(8):
            even, odd = r_s[pl.ds(pair * 96, 48), :], r_s[pl.ds(pair * 96 + 48, 48), :]
            keep, send = pick(core, even, odd)
            place = ((((pair >> 1) & 1) ^ my_y) << 1) | ((pair & 1) ^ my_x)
            for col in range(6):
                lanes = slice(col * 128, col * 128 + 128)
                dw1k_ref[place, pair >> 2, :, col] = keep[:, lanes].reshape(3, 16, 128)
                dw1s_ref[place, pair >> 2, :, col] = send[:, lanes].reshape(3, 16, 128)

        r_s[...] = dot(g_s[chunk], dz_s[...], TN).astype(BF)
        for pair in range(2):
            even, odd = r_s[pl.ds(pair * 384, 192), :], r_s[pl.ds(pair * 384 + 192, 192), :]
            keep, send = pick(core, even, odd)
            for col in range(6):
                lanes = slice(col * 128, col * 128 + 128)
                dw2k_ref[pair ^ my_x, 0, :, col] = keep[:, lanes].reshape(12, 16, 128)
                dw2s_ref[pair ^ my_x, 0, :, col] = send[:, lanes].reshape(12, 16, 128)


def ffn_layer(me, gw, n1, cotangent, vec):
    count = n1.shape[0]
    full = whole((count, D))
    up = pl.BlockSpec(
        (4, 2, 3, 6, 16, 128), lambda s, m: (0, 0, 0, jnp.maximum(s - 4, 0), 0, 0)
    )

    def down_index(s, m):
        chunk = jnp.maximum(s - 4, 0)
        return ((chunk % 2) ^ ((m[0] >> 2) & 1), chunk // 2, 0, 0, 0, 0)

    down = pl.BlockSpec((2, 1, 12, 6, 16, 128), down_index)
    shape = jax.ShapeDtypeStruct
    return pl.pallas_call(
        ffn_kernel,
        grid_spec=pltpu.PrefetchScalarGridSpec(
            num_scalar_prefetch=1,
            grid=(8,),
            in_specs=[ANY, full, full, whole((VEC_ROWS, 128))],
            out_specs=[full, up, up, down, down, whole((VEC_ROWS, 128)), full],
            scratch_shapes=[
                pltpu.VMEM((16, FFN_TILES, 16, 128), BF),
                pltpu.VMEM((16, FFN_TILES, 16, 128), BF),
                pltpu.VMEM((4, count, D), BF),
                pltpu.VMEM((4, count, D), BF),
                pltpu.VMEM((count, D), BF),
                pltpu.VMEM((D, count), BF),
                pltpu.VMEM((count, D), BF),
                pltpu.VMEM((count, D), BF),
                pltpu.VMEM((D, D), BF),
                pltpu.SemaphoreType.DMA((4, 4)),
            ],
        ),
        out_shape=[shape((count, D), BF)]
        + [shape((4, 2, 3, 24, 16, 128), BF)] * 2
        + [shape((4, 2, 12, 6, 16, 128), BF)] * 2
        + [shape((VEC_ROWS, 128), F32), shape((count, D), F32)],
        compiler_params=params(),
        cost_estimate=cost(
            flops=12 * count * D * FF, bytes_accessed=count * D * 30, transcendentals=count * FF
        ),
        name="ffn_layer",
    )(me, gw, n1, cotangent, vec)


def norm_bwd_kernel(
    wa_ref, dy1_ref, n1_ref, rstd_ref, keep_ref, vec_ref, vg_in_ref,
    dh1_ref, dctx_ref, da_ref, vg_ref,
    wo_s, sums_s, sem,
):
    step = pl.program_id(0)
    copy = pltpu.make_async_copy(wa_ref.at[pl.ds(24, 8)], wo_s, sem)

    @pl.when(step == 0)
    def _():
        copy.start()
        vg_ref[...] = vg_in_ref[...]
        sums_s[...] = jnp.zeros_like(sums_s)

    dy1 = dy1_ref[...]
    normed = n1_ref[...]
    t = dy1 * row(vec_ref, 3)
    mean_t = jnp.mean(t, axis=1, keepdims=True)
    mean_tn = jnp.mean(t * normed, axis=1, keepdims=True)
    dh1 = (t - mean_t - normed * mean_tn) * rstd_ref[:, 0:1]
    dh1_ref[...] = dh1
    da = dh1.astype(BF)
    da_ref[...] = da
    sums_s[0:1, :] += jnp.sum(da.astype(F32), axis=0, keepdims=True)
    sums_s[1:2, :] += jnp.sum(dy1 * normed, axis=0, keepdims=True)
    sums_s[2:3, :] += jnp.sum(dy1, axis=0, keepdims=True)

    @pl.when(step == 0)
    def _():
        copy.wait()

    back = dot(da, square(wo_s, 0), NT).astype(BF).astype(F32)
    dctx_ref[...] = (back * keep_ref[...]).astype(BF)

    @pl.when(step == pl.num_programs(0) - 1)
    def _():
        for i in range(3):
            put_row(vg_ref, 2 + i, sums_s[i : i + 1, :])


def norm_bwd(wa, dy1, n1, rstd, keep, vec, vg):
    count = dy1.shape[0]
    tile = NORM_TILE
    rows = pl.BlockSpec((tile, D), lambda i: (i, 0))
    shape = jax.ShapeDtypeStruct
    return pl.pallas_call(
        norm_bwd_kernel,
        grid=(count // tile,),
        in_specs=[
            ANY,
            rows,
            rows,
            pl.BlockSpec((tile, 128), lambda i: (i, 0)),
            pl.BlockSpec((tile, 1), lambda i: (i, 0)),
            whole((VEC_ROWS, 128)),
            whole((VEC_ROWS, 128)),
        ],
        out_specs=[rows, rows, rows, whole((VEC_ROWS, 128))],
        scratch_shapes=[
            pltpu.VMEM((8, ATTN_TILES, 16, 128), BF),
            pltpu.VMEM((8, D), F32),
            pltpu.SemaphoreType.DMA,
        ],
        out_shape=[
            shape((count, D), F32),
            shape((count, D), BF),
            shape((count, D), BF),
            shape((VEC_ROWS, 128), F32),
        ],
        compiler_params=params(),
        cost_estimate=cost(
            flops=2 * count * D * D, bytes_accessed=count * D * 16, transcendentals=0
        ),
        name="norm_bwd",
    )(wa, dy1, n1, rstd, keep, vec, vg)


def attn_bwd_kernel(
    first, span_ref, q_ref, k_ref, v_ref, ctx_ref, dctx_ref, lse_ref, segc_ref, segr_ref, d_ref, dqt_s, dots_s
):
    line = pl.program_id(0)
    pairs = q_ref.shape[1] // 128
    lane = lax.broadcasted_iota(jnp.int32, (1, 128), 1)
    low = lane < 64
    zero = jnp.zeros((), BF)
    spots = [slice(128 * pair, 128 * pair + 128) for pair in range(pairs)]
    for pair, lanes in enumerate(spots):
        products = (dctx_ref[:, lanes].astype(F32) * ctx_ref[:, lanes].astype(F32)).T
        for head in range(2):
            place = slice(4 * pair + head, 4 * pair + head + 1)
            dots_s[place, :] = jnp.sum(products[64 * head : 64 * head + 64], axis=0, keepdims=True)
            index = 2 * (first + pair) + head
            place = slice(4 * pair + 2 + head, 4 * pair + 3 + head)
            dots_s[place, :] = lse_ref[index // 4, index % 4 : index % 4 + 1, :]
    dqt_s[...] = jnp.zeros_like(dqt_s)

    def both(value):
        return jnp.concatenate([jnp.where(low, value, zero), jnp.where(low, zero, value)], axis=0)

    def block_step(block, carry):
        rows = pl.ds(pl.multiple_of(block * 128, 128), 128)
        start, count = span_ref[line, 2 * block], span_ref[line, 2 * block + 1]

        @pl.when(count == 0)
        def _():
            d_ref[1, rows, :] = jnp.zeros((128, 128 * pairs), BF)
            d_ref[2, rows, :] = jnp.zeros((128, 128 * pairs), BF)

        def window(size):
            @pl.when(count == size)
            def _():
                seen = pl.ds(pl.multiple_of(start * 128, 128), 128 * size)
                seg_row = segr_ref[:, seen]
                allowed = segc_ref[rows, :] == jnp.where(seg_row < 0, -2, seg_row)
                allowed = jnp.concatenate([allowed, allowed], axis=0)

                def spread(pair, offset):
                    lines = [dots_s[4 * pair + offset + h : 4 * pair + offset + h + 1, seen] for h in range(2)]
                    return jnp.concatenate([jnp.broadcast_to(r, (128, 128 * size)) for r in lines], axis=0)

                keys = [both(k_ref[rows, lanes]) for lanes in spots]
                queries = [q_ref[seen, lanes] for lanes in spots]
                dctxs = [dctx_ref[seen, lanes] for lanes in spots]
                scores = [dot(k, q, NT) for k, q in zip(keys, queries)]
                dprobs = [dot(both(v_ref[rows, lanes]), dctx, NT) for lanes, dctx in zip(spots, dctxs)]
                probs = [
                    jnp.where(allowed, jnp.exp(score - spread(pair, 2)), 0.0)
                    for pair, score in enumerate(scores)
                ]
                dscores = [
                    (prob * (dprob - spread(pair, 0))).astype(BF)
                    for pair, (prob, dprob) in enumerate(zip(probs, dprobs))
                ]
                dvs = [dot(prob.astype(BF), dctx, NN) for prob, dctx in zip(probs, dctxs)]
                dks = [dot(dscore, query, NN) for dscore, query in zip(dscores, queries)]
                dqs = [dot(key, dscore, TN) for key, dscore in zip(keys, dscores)]
                for pair, lanes in enumerate(spots):
                    dqt_s[lanes, seen] += dqs[pair]
                    d_ref[1, rows, lanes] = jnp.where(low, dks[pair][:128], dks[pair][128:]).astype(BF)
                    d_ref[2, rows, lanes] = jnp.where(low, dvs[pair][:128], dvs[pair][128:]).astype(BF)

        for size in range(1, 5):
            window(size)
        return carry

    lax.fori_loop(0, 4, block_step, 0)
    d_ref[0] = (dqt_s[...].T * 0.125).astype(BF)


def attn_bwd(span, query, key, value, ctx, dctx, lse, segc, segr, first, cols):
    count = query.shape[0]
    rows = count // SLOTS
    width = 128 * cols
    part = pl.BlockSpec((SLOTS, width), lambda r, s: (r, first // cols))
    return pl.pallas_call(
        functools.partial(attn_bwd_kernel, first),
        grid_spec=pltpu.PrefetchScalarGridSpec(
            num_scalar_prefetch=1,
            grid=(rows,),
            in_specs=[part] * 5
            + [
                pl.BlockSpec((None, 3, 4, SLOTS), lambda r, s: (r, 0, 0, 0)),
                pl.BlockSpec((SLOTS, 1), lambda r, s: (r, 0)),
                pl.BlockSpec((None, 1, SLOTS), lambda r, s: (r, 0, 0)),
            ],
            out_specs=pl.BlockSpec((3, SLOTS, width), lambda r, s: (0, r, 0)),
            scratch_shapes=[pltpu.VMEM((width, SLOTS), F32), pltpu.VMEM((4 * cols, SLOTS), F32)],
        ),
        out_shape=jax.ShapeDtypeStruct((3, count, width), BF),
        compiler_params=params(),
        cost_estimate=cost(
            flops=10 * count * D * SLOTS, bytes_accessed=count * D * 16, transcendentals=count * SLOTS * 12
        ),
        name="attn_bwd",
    )(span, query, key, value, ctx, dctx, lse, segc, segr)


def proj_grad_kernel(first, me_ref, x_ref, ctx_ref, d_ref, da_ref, vg_in_ref, dwk_ref, dws_ref, vg_ref, t_s, r_s):
    step = pl.program_id(0)
    me = me_ref[0]
    core, my_x, my_y = me & 1, (me >> 1) & 1, (me >> 2) & 1

    @pl.when(step == 0)
    def _():
        t_s[...] = x_ref[...].T
        vg_ref[...] = vg_in_ref[...]

    @pl.when(step == 3)
    def _():
        t_s[...] = ctx_ref[...].T

    grad = jnp.where(step == 3, da_ref[...], d_ref[...])

    @pl.when((step == 0) | (step == 2))
    def _():
        put_row(vg_ref, step >> 1, jnp.sum(grad.astype(F32), axis=0, keepdims=True), first)

    r_s[...] = dot(t_s[...], grad, NN).astype(BF)
    for pair in range(4):
        even, odd = r_s[pl.ds(pair * 192, 96), :], r_s[pl.ds(pair * 192 + 96, 96), :]
        keep, send = pick(core, even, odd)
        place = (((pair >> 1) ^ my_y) << 1) | ((pair & 1) ^ my_x)
        for col in range(r_s.shape[1] // 128):
            lanes = slice(col * 128, col * 128 + 128)
            dwk_ref[place, 0, :, col] = keep[:, lanes].reshape(6, 16, 128)
            dws_ref[place, 0, :, col] = send[:, lanes].reshape(6, 16, 128)


def proj_grad(me, tokens, ctx, grads, da, vg, first):
    count, width = grads.shape[1:]
    cols = width // 128
    out = pl.BlockSpec((4, 1, 6, cols, 16, 128), lambda i, m: (0, i, 0, 0, 0, 0))
    full = pl.BlockSpec((count, D), lambda i, m: (0, 0))
    shape = jax.ShapeDtypeStruct
    return pl.pallas_call(
        functools.partial(proj_grad_kernel, first),
        grid_spec=pltpu.PrefetchScalarGridSpec(
            num_scalar_prefetch=1,
            grid=(4,),
            in_specs=[
                full,
                full,
                pl.BlockSpec((None, count, width), lambda i, m: (jnp.minimum(i, 2), 0, 0)),
                pl.BlockSpec((count, width), lambda i, m: (0, first // cols)),
                whole((VEC_ROWS, 128)),
            ],
            out_specs=[out, out, whole((VEC_ROWS, 128))],
            scratch_shapes=[pltpu.VMEM((D, count), BF), pltpu.VMEM((D, width), BF)],
        ),
        out_shape=[shape((4, 4, 6, cols, 16, 128), BF)] * 2 + [shape((VEC_ROWS, 128), F32)],
        compiler_params=params(),
        cost_estimate=cost(
            flops=8 * count * D * width, bytes_accessed=count * D * 14, transcendentals=0
        ),
        name="proj_grad",
    )(me, tokens, ctx, grads, da, vg)


def input_grad_kernel(wa_ref, dh1_ref, da_ref, db_ref, out_ref, w_s, sems):
    @pl.when(pl.program_id(0) == 0)
    def _():
        copies = [
            pltpu.make_async_copy(
                wa_ref.at[pl.ds(8 * m, 8)],
                w_s.at[pl.ds(8 * m, 8)],
                sems.at[m],
            )
            for m in range(3)
        ]
        for copy in copies:
            copy.start()
        for copy in copies:
            copy.wait()

    total = dh1_ref[...]
    for m in range(3):
        grad = jnp.concatenate([da_ref[m], db_ref[m]], axis=1)
        total = total + dot(grad, square(w_s, 8 * m), NT)
    out_ref[...] = total.astype(BF)


def input_grad(wa, dh1, first, second):
    count = dh1.shape[0]
    rows = pl.BlockSpec((NORM_TILE, D), lambda i: (i, 0))
    return pl.pallas_call(
        input_grad_kernel,
        grid=(count // NORM_TILE,),
        in_specs=[ANY, rows] + [pl.BlockSpec((3, NORM_TILE, D // 2), lambda i: (0, i, 0))] * 2,
        out_specs=rows,
        out_shape=jax.ShapeDtypeStruct((count, D), BF),
        scratch_shapes=[
            pltpu.VMEM((24, ATTN_TILES, 16, 128), BF),
            pltpu.SemaphoreType.DMA((3,)),
        ],
        compiler_params=params(),
        cost_estimate=cost(
            flops=6 * count * D * D, bytes_accessed=count * D * 18, transcendentals=0
        ),
        name="input_grad",
    )(wa, dh1, first, second)


def retile(flat, blocks):
    tall = flat.shape[0] // (16 * blocks)
    tiles = flat.reshape(tall, 16, blocks, 128).transpose(0, 2, 1, 3)
    return tiles.reshape(tall * blocks, 16, 128)


def untile(tiles, blocks):
    tall = tiles.shape[0] // blocks
    flat = tiles.reshape(tall, blocks, 16, 128).transpose(0, 2, 1, 3)
    return flat.reshape(tall * blocks * 16, 128)


def gather_ffn(ffn, size):
    if size == OWNERS:
        upper = lax.axis_index("fsdp") < OWNERS // 2
        mine = jnp.where(upper, retile(ffn, 24), retile(ffn, 6))
        return lax.all_gather(mine, "fsdp", axis=0, tiled=False)
    ffn = lax.all_gather(ffn, "fsdp", axis=0, tiled=True)
    half = ffn.shape[0] // 2
    tiles = jnp.concatenate([retile(ffn[:half], 24), retile(ffn[half:], 6)], axis=0)
    return tiles.reshape(OWNERS, FFN_TILES, 16, 128)


def pad_vectors(flat):
    return jnp.pad(flat, (0, VEC_ROWS * 128 - flat.shape[0])).reshape(VEC_TILES, 16, 128)


def gather_attn(attn, vectors, size):
    if size != OWNERS:
        attn = lax.all_gather(attn, "fsdp", axis=0, tiled=True)
        vec = lax.all_gather(vectors, "fsdp", axis=0, tiled=True)
        return [retile(attn, 6).reshape(OWNERS, ATTN_TILES, 16, 128)], pad_vectors(vec)[None]
    tiles = retile(attn, 6)
    each = vectors.shape[0]
    flat = jnp.zeros((VEC_ROWS * 128,), BF)
    vec = lax.dynamic_update_slice(flat, vectors, (lax.axis_index("fsdp") * each,))
    vec = vec.reshape(VEC_TILES, 16, 128)
    mine_q, mine_p = tiles[:Q_TILES], jnp.concatenate([tiles[Q_TILES:], vec], axis=0)
    planes = [mine_q] + [hop(mine_q, 8 * step) for step in (1, 2, 3)]
    chips = [mine_p] + [hop(mine_p, 2 * side) for side in (1, 2, 3)]
    across = jnp.stack(planes, axis=0)
    vec = sum(chip[P_TILES:].astype(F32) for chip in chips).astype(BF)
    along = jnp.concatenate([chip[:P_TILES] for chip in chips] + [vec], axis=0)
    arrays = [across] + [hop(across, 2 * side) for side in (1, 2, 3)]
    arrays += [along] + [hop(along, 8 * step) for step in (1, 2, 3)]
    arrays += [hop(array, 1) for array in arrays]
    vecs = [array[4 * P_TILES :] for array in arrays[4:8] + arrays[12:16]]
    return arrays, jnp.stack(vecs, axis=0)


def hop(value, bit):
    pairs = [(i, i ^ bit) for i in range(OWNERS)]
    return lax.ppermute(value, "fsdp", pairs)


def reduce_plain(ffn_terms, attn_terms, vector_terms):
    def absolute(keep, send):
        planes = keep.shape[1]
        both = jnp.stack([keep, send], axis=1)
        return jnp.moveaxis(both, 2, 0).reshape(planes * 8, -1, 16, 128)

    dw1k, dw1s, dw2k, dw2s = ffn_terms
    up = untile(absolute(dw1k, dw1s).reshape(-1, 16, 128), 24)
    down = untile(absolute(dw2k, dw2s).reshape(-1, 16, 128), 6)
    proj = untile(absolute(*attn_terms).reshape(-1, 16, 128), 6)

    def scatter(value):
        return lax.psum_scatter(value.astype(F32), "fsdp", scatter_dimension=0, tiled=True)

    return scatter(proj), scatter(jnp.concatenate([up, down], axis=0)), scatter(vector_terms)


class Reduction:
    def __init__(self, keeps, sends, vec=None):
        self.keeps = keeps
        self.hops = [hop(send, 1) for send in sends]
        self.vec = vec
        if vec is not None:
            self.hops.append(hop(vec.astype(BF), 1))

    def part(self, place, upper):
        pieces = []
        for a, b in zip(self.keeps, self.received, strict=True):
            half = a.shape[1] // 2
            cut = slice(half, None) if upper else slice(0, half)
            piece = a[place, cut].astype(F32) + b[place, cut].astype(F32)
            pieces.append(piece.reshape((-1, 16, 128)))
        return jnp.concatenate(pieces, axis=0) if len(pieces) > 1 else pieces[0]

    def ride(self, message):
        message = message.astype(BF)
        if self.vec is None:
            return message
        return jnp.concatenate([message, self.vec.astype(BF)], axis=0)

    def landed(self, message):
        if self.vec is None:
            return message
        self.vec = self.vec + message[-VEC_TILES:].astype(F32)
        return message[:-VEC_TILES]

    def corner(self):
        self.received = self.hops[: len(self.keeps)]
        if self.vec is not None:
            self.vec = self.vec + self.hops[-1].astype(F32)
        self.hops = [hop(self.ride(self.part(3, False)), 2), hop(self.part(3, True).astype(BF), 4)]

    def sides(self):
        via_x, via_y = self.landed(self.hops[0]), self.hops[1]
        to_x = jnp.concatenate([self.part(1, False), self.part(1, True) + via_y.astype(F32)])
        to_y = jnp.concatenate([self.part(2, False) + via_x.astype(F32), self.part(2, True)])
        self.hops = [hop(to_x.astype(BF), 2), hop(self.ride(to_y), 4)]

    def planes(self, my_z, arrange):
        from_x, from_y = self.hops[0], self.landed(self.hops[1])
        own = jnp.concatenate([self.part(0, False), self.part(0, True)])
        own = arrange(own + from_x.astype(F32) + from_y.astype(F32))
        self.mine = lax.dynamic_index_in_dim(own, my_z, 0, keepdims=False)
        low = own.astype(BF)
        self.hops = [
            hop(self.ride(lax.dynamic_index_in_dim(low, my_z ^ step, 0, keepdims=False)), 8 * step)
            for step in (1, 2, 3)
        ]

    def total(self):
        return self.mine + sum(self.landed(other).astype(F32) for other in self.hops)


def meet(hops, values):
    return lax.optimization_barrier((hops, values))


def tiles_of(array):
    return array.reshape(array.shape[:2] + (-1, 16, 128))


def spans(segments, pad_segment):
    pad = pad_segment[:, None]
    seen = jnp.where(segments == pad, -1, segments)
    first, last = segments[:, ::128], segments[:, 127::128]
    last = jnp.minimum(last, pad - 1)
    below = jnp.sum(segments[:, None, :] < first[:, :, None], axis=2)
    upto = jnp.sum(segments[:, None, :] <= last[:, :, None], axis=2)
    start = below // 128
    count = jnp.where(first == pad, 0, (upto + 127) // 128 - start)
    both = jnp.stack([jnp.where(count == 0, 0, start), count], axis=2)
    return seen, both.reshape(segments.shape[0], 8).astype(jnp.int32)


def layer(tokens, attn_matrices, ffn_matrices, vectors, segments, pad_segment, cotangent, size):
    fast = size == OWNERS
    gw = gather_ffn(ffn_matrices, size)
    pieces, vecs = gather_attn(attn_matrices, vectors, size)
    place = lax.axis_index("fsdp") if fast else jnp.zeros((), jnp.int32)
    me = place.reshape(1).astype(jnp.int32)
    my_z = place >> 3
    rows = segments.shape[0]
    seen, span = spans(segments, pad_segment)
    segc = seen.reshape(rows * SLOTS, 1)
    segr = seen.reshape(rows, 1, SLOTS)
    keep = (segments != pad_segment[:, None]).astype(F32).reshape(rows * SLOTS, 1)

    query, key, value, ctx, lse, wa, vec = attn_fwd(
        fast, me, span, pieces, vecs, tokens, segc, segr
    )
    n1, rstd = norm_fwd(wa, ctx, tokens, vec)
    out, dw1k, dw1s, dw2k, dw2s, vg, dy1 = ffn_layer(me, gw, n1, cotangent, vec)
    if not fast:
        dh1, dctx, da, vg = norm_bwd(wa, dy1, n1, rstd, keep, vec, vg)
        first = attn_bwd(span, query, key, value, ctx, dctx, lse, segc, segr, 0, 3)
        dwak, dwas, vg = proj_grad(me, tokens, ctx, first, da, vg, 0)
        second = attn_bwd(span, query, key, value, ctx, dctx, lse, segc, segr, 3, 3)
        dwbk, dwbs, vg = proj_grad(me, tokens, ctx, second, da, vg, 3)
        dx = input_grad(wa, dh1, first, second)
        attn_terms = [jnp.concatenate(pair, axis=3) for pair in ((dwak, dwbk), (dwas, dwbs))]
        vector_terms = vg.reshape(-1)[: 12 * D]
        return (out, dx) + reduce_plain((dw1k, dw1s, dw2k, dw2s), attn_terms, vector_terms)

    def arrange_ffn(own):
        own = own.reshape(2, 2, FFN_TILES, 16, 128).transpose(1, 0, 2, 3, 4)
        return own.reshape(4, FFN_TILES, 16, 128)

    def arrange_attn(own):
        return own.reshape(4, ATTN_TILES // 2, 16, 128)

    ffn = Reduction([tiles_of(dw1k), tiles_of(dw2k)], [tiles_of(dw1s), tiles_of(dw2s)])
    dh1, dctx, da, vg = norm_bwd(wa, dy1, n1, rstd, keep, vec, vg)
    ffn.hops, (dh1, dctx, da, vg) = meet(ffn.hops, (dh1, dctx, da, vg))
    ffn.corner()
    first = attn_bwd(span, query, key, value, ctx, dctx, lse, segc, segr, 0, 3)
    ffn.hops, (first, dctx) = meet(ffn.hops, (first, dctx))
    ffn.sides()
    dwak, dwas, vg = proj_grad(me, tokens, ctx, first, da, vg, 0)
    left = Reduction([tiles_of(dwak)], [tiles_of(dwas)])
    second = attn_bwd(span, query, key, value, ctx, dctx, lse, segc, segr, 3, 3)
    (ffn.hops, left.hops), second = meet((ffn.hops, left.hops), second)
    ffn.planes(my_z, arrange_ffn)
    left.corner()
    dwbk, dwbs, vg = proj_grad(me, tokens, ctx, second, da, vg, 3)
    left.hops, (dwbk, dwbs, vg) = meet(left.hops, (dwbk, dwbs, vg))
    right = Reduction(
        [tiles_of(dwbk)], [tiles_of(dwbs)], vg.reshape(VEC_TILES, 16, 128)
    )
    left.sides()
    dx = input_grad(wa, dh1, first, second)
    (right.hops, left.hops, ffn.hops), dx = meet((right.hops, left.hops, ffn.hops), dx)
    right.corner()
    left.planes(my_z, arrange_attn)
    right.sides()
    right.planes(my_z, arrange_attn)

    upper = place < OWNERS // 2
    ffn_sum = ffn.total()
    ffn_grad = jnp.where(upper, untile(ffn_sum, 24), untile(ffn_sum, 6))
    halves = [r.total().reshape(6, 3, 16, 128) for r in (left, right)]
    attn_grad = untile(jnp.concatenate(halves, axis=1).reshape(ATTN_TILES, 16, 128), 6)
    each = vectors.shape[0]
    vector_grad = lax.dynamic_slice(right.vec.reshape(-1), (place * each,), (each,))
    return out, dx, attn_grad, ffn_grad, vector_grad


def solution(mesh):
    size = mesh.shape["fsdp"]
    return jax.shard_map(
        functools.partial(layer, size=size),
        mesh=mesh,
        in_specs=(
            P("fsdp", None),
            P("fsdp", None),
            P("fsdp", None),
            P("fsdp"),
            P("fsdp", None),
            P("fsdp"),
            P("fsdp", None),
        ),
        out_specs=(P("fsdp", None), P("fsdp", None), P("fsdp", None), P("fsdp", None), P("fsdp")),
        check_vma=False,
    )
```

```python
import functools

import jax
import jax.numpy as jnp
from jax import lax
from jax.experimental import pallas as pl
from jax.experimental.pallas import tpu as pltpu
from jax.sharding import PartitionSpec as P

D = 768
FF = 3072
SLOTS = 512
BF = jnp.bfloat16
F32 = jnp.float32
NN = ((1,), (0,))
NT = ((1,), (1,))
TN = ((0,), (0,))
OWNERS = 32
ATTN_TILES = 36
FFN_TILES = 72
COST_SCALE = 1
VMEM_LIMIT = 60 * 1024 * 1024

TAIL_SLOPE = 0.39 * 0.5**0.5
TAIL_POLY = (
    0.11766260955586648,
    0.04569420719462487,
    0.32477969950633645,
    -0.3177001395785759,
    0.44333218507090993,
    -0.11376856259852677,
)


def dot(left, right, dims):
    return lax.dot_general(left, right, (dims, ((), ())), preferred_element_type=F32)


def params(**kwargs):
    return pltpu.CompilerParams(vmem_limit_bytes=VMEM_LIMIT, **kwargs)


def cost(flops, bytes_accessed, transcendentals):
    return pl.CostEstimate(
        flops=flops // COST_SCALE,
        bytes_accessed=bytes_accessed // COST_SCALE,
        transcendentals=transcendentals // COST_SCALE,
    )


def whole(shape):
    zeros = (0,) * len(shape)
    return pl.BlockSpec(shape, lambda *_: zeros)


ANY = pl.BlockSpec(memory_space=pl.ANY)
VEC_TILES = 5
VEC_ROWS = 16 * VEC_TILES


def row(vec_ref, index, width=D):
    blocks = width // 128
    return jnp.concatenate([vec_ref[pl.ds(6 * index + i, 1), :] for i in range(blocks)], axis=1)


def put_row(vec_ref, index, value, first=0):
    for i in range(value.shape[1] // 128):
        vec_ref[pl.ds(6 * index + first + i, 1), :] = value[:, 128 * i : 128 * i + 128]


def square_cols(tiles, first, col):
    parts = [tiles[pl.ds(first, 8), i * 6 + col] for i in range(6)]
    return jnp.stack(parts, axis=1).reshape(D, 128)


def square(tiles, first):
    return jnp.concatenate([square_cols(tiles, first, col) for col in range(6)], axis=1)


def up_col(tiles, col):
    parts = [tiles[:, i * 24 + col] for i in range(3)]
    return jnp.stack(parts, axis=1).reshape(D, 128)


def up_chunk(tiles, chunk):
    return jnp.concatenate([up_col(tiles, chunk * 6 + col) for col in range(6)], axis=1)


def down_chunk(tiles, chunk):
    cols = []
    for col in range(6):
        parts = [tiles[pl.ds(4 * chunk, 4), i * 6 + col] for i in range(12)]
        cols.append(jnp.stack(parts, axis=1).reshape(D, 128))
    return jnp.concatenate(cols, axis=1)


PIECES = 10


def piece_copies(me, refs, tiles, planes, dst):
    yxc, my_z = me & 7, me >> 3
    half = tiles // 2
    copies = []
    for core in range(2):
        own, over_x, over_y, low, high = refs[5 * core : 5 * core + 5]
        for z in planes:
            plane = my_z ^ z
            for side, ref in ((0, own), (1, over_x), (2, over_y)):
                owner = 8 * z + (yxc ^ (2 * side + core))
                copies.append((ref.at[pl.ds(plane * tiles, tiles)], dst(owner, pl.ds(0, tiles))))
            owner = 8 * z + (yxc ^ (6 + core))
            for part, ref in ((0, low), (1, high)):
                copies.append((ref.at[plane], dst(owner, pl.ds(part * half, half))))
    return copies


def attn_copies(fast, me, refs, w_s, sems):
    if not fast:
        return [pltpu.make_async_copy(refs[0], w_s, sems.at[0])]
    copies = piece_copies(me, refs, ATTN_TILES, range(4), lambda owner, tiles: w_s.at[owner, tiles])
    return [pltpu.make_async_copy(src, dst, sems.at[i]) for i, (src, dst) in enumerate(copies)]


def attn_fwd_kernel(fast, me_ref, span_ref, *args):
    count = PIECES if fast else 1
    refs = args[:count]
    (
        vec_ref, x_ref, segc_ref, segr_ref,
        q_ref, k_ref, v_ref, ctx_ref, lse_ref, wa_ref, vec_out_ref,
        w_s, vt_s, sems, out_sem,
    ) = args[count:]
    line, col = pl.program_id(0), pl.program_id(1)
    first_step = (line == 0) & (col == 0)
    last_step = (line == pl.num_programs(0) - 1) & (col == pl.num_programs(1) - 1)
    out_copy = pltpu.make_async_copy(w_s, wa_ref, out_sem)

    @pl.when(first_step)
    def _():
        copies = attn_copies(fast, me_ref[0], refs, w_s, sems)
        for copy in copies:
            copy.start()
        vec = vec_ref[0].astype(F32)
        for i in range(1, vec_ref.shape[0]):
            vec = vec + vec_ref[i].astype(F32)
        vec_out_ref[...] = vec.reshape(VEC_ROWS, 128)
        for copy in copies:
            copy.wait()
        out_copy.start()

    @pl.when(last_step)
    def _():
        out_copy.wait()

    cols = [2 * col, 2 * col + 1]
    weight = jnp.concatenate([square_cols(w_s, 8 * m, c) for m in range(3) for c in cols], axis=1)
    qkv = dot(x_ref[...], weight, NN)
    bias_q = jnp.concatenate([vec_out_ref[pl.ds(c, 1), :] for c in cols], axis=1)
    bias_v = jnp.concatenate([vec_out_ref[pl.ds(6 + c, 1), :] for c in cols], axis=1)
    q_ref[...] = (qkv[:, :256] + bias_q).astype(BF) * 0.125
    k_ref[...] = qkv[:, 256:512].astype(BF)
    v_ref[...] = (qkv[:, 512:] + bias_v).astype(BF)
    lane = lax.broadcasted_iota(jnp.int32, (1, 128), 1)
    low = lane < 64
    zero = jnp.zeros((), BF)

    for pair in range(2):
        vt_s[pl.ds(128 * pair, 128), :] = v_ref[:, 128 * pair : 128 * pair + 128].T

    def attend(block, carry):
        rows = pl.ds(pl.multiple_of(block * 128, 128), 128)
        start, count = span_ref[line, 2 * block], span_ref[line, 2 * block + 1]

        @pl.when(count == 0)
        def _():
            ctx_ref[rows, :] = jnp.zeros((128, 256), BF)
            lse_ref[:, rows] = jnp.zeros((4, 128), F32)

        def window(size):
            @pl.when(count == size)
            def _():
                seen = pl.ds(pl.multiple_of(start * 128, 128), 128 * size)
                seg_row = segr_ref[:, rows]
                blocked = jnp.where(segc_ref[seen, :] == seg_row, 0.0, -1e30)
                keep = jnp.where(jnp.broadcast_to(seg_row, (64, 128)) < 0, 0.0, 1.0)
                scores = []
                for head in range(4):
                    lanes = slice(128 * (head // 2), 128 * (head // 2) + 128)
                    query = q_ref[rows, lanes]
                    query = jnp.where(low, query, zero) if head % 2 == 0 else jnp.where(low, zero, query)
                    scores.append(dot(k_ref[seen, lanes], query, NT) + blocked)
                tops = [jnp.max(score, axis=0, keepdims=True) for score in scores]
                expds = [jnp.exp(score - top) for score, top in zip(scores, tops)]
                totals = [jnp.sum(expd, axis=0, keepdims=True) for expd in expds]
                outs = []
                for head in range(4):
                    values = vt_s[pl.ds(64 * head, 64), seen]
                    out = dot(values, expds[head].astype(BF), NN)
                    outs.append(out * (1.0 / totals[head]) * keep)
                    lse_ref[pl.ds(head, 1), rows] = tops[head] + jnp.log(totals[head])
                ctx_ref[rows, :] = jnp.concatenate(outs, axis=0).T.astype(BF)

        for size in range(1, 5):
            window(size)
        return carry

    lax.fori_loop(0, 4, attend, 0)


def attn_fwd(fast, me, span, pieces, vec, tokens, segc, segr):
    count = tokens.shape[0]
    rows = count // SLOTS
    part = pl.BlockSpec((SLOTS, 256), lambda r, j, m, s: (r, j))
    slot = pl.BlockSpec((SLOTS, 1), lambda r, j, m, s: (r, 0))
    shape = jax.ShapeDtypeStruct
    return pl.pallas_call(
        functools.partial(attn_fwd_kernel, fast),
        grid_spec=pltpu.PrefetchScalarGridSpec(
            num_scalar_prefetch=2,
            grid=(rows, 3),
            in_specs=[ANY] * len(pieces)
            + [
                whole(vec.shape),
                pl.BlockSpec((SLOTS, D), lambda r, j, m, s: (r, 0)),
                slot,
                pl.BlockSpec((None, 1, SLOTS), lambda r, j, m, s: (r, 0, 0)),
            ],
            out_specs=[part] * 4
            + [pl.BlockSpec((None, None, 4, SLOTS), lambda r, j, m, s: (r, j, 0, 0)), ANY, whole((VEC_ROWS, 128))],
            scratch_shapes=[
                pltpu.VMEM((OWNERS, ATTN_TILES, 16, 128), BF),
                pltpu.VMEM((256, SLOTS), BF),
                pltpu.SemaphoreType.DMA((160,)),
                pltpu.SemaphoreType.DMA,
            ],
        ),
        out_shape=[shape((count, D), BF)] * 4
        + [
            shape((rows, 3, 4, SLOTS), F32),
            shape((OWNERS, ATTN_TILES, 16, 128), BF),
            shape((VEC_ROWS, 128), F32),
        ],
        compiler_params=params(),
        cost_estimate=cost(
            flops=2 * count * D * (3 * D + 4 * SLOTS), bytes_accessed=count * D * 12, transcendentals=count * SLOTS * 12
        ),
        name="attn_fwd",
    )(me, span, *pieces, vec, tokens, segc, segr)


def norm_parts(hidden):
    mean = jnp.mean(hidden, axis=1, keepdims=True)
    centered = hidden - mean
    var = jnp.mean(centered * centered, axis=1, keepdims=True)
    rstd = lax.rsqrt(var + 1e-12)
    return centered * rstd, rstd


def gelu_parts(u):
    size = jnp.abs(u)
    t = pl.reciprocal(1.0 + TAIL_SLOPE * size)
    poly = jnp.full_like(t, TAIL_POLY[-1])
    for coef in TAIL_POLY[-2::-1]:
        poly = poly * t + coef
    bell = jnp.exp(u * u * -0.5)
    tail = poly * t * bell
    phi_cdf = jnp.where(u > 0, 1.0 - tail, tail)
    return u * phi_cdf, phi_cdf + u * bell * 0.3989422804014327


NORM_TILE = 256


def norm_fwd_kernel(wa_ref, ctx_ref, x_ref, vec_ref, n1_ref, rstd_ref, wo_s, sem):
    copy = pltpu.make_async_copy(wa_ref.at[pl.ds(24, 8)], wo_s, sem)

    @pl.when(pl.program_id(0) == 0)
    def _():
        copy.start()
        copy.wait()

    hidden = x_ref[...].astype(F32) + dot(ctx_ref[...], square(wo_s, 0), NN) + row(vec_ref, 2)
    normed, rstd = norm_parts(hidden)
    n1_ref[...] = normed
    rstd_ref[...] = jnp.broadcast_to(rstd, rstd_ref.shape)


def norm_fwd(wa, ctx, tokens, vec):
    count = tokens.shape[0]
    rows = pl.BlockSpec((NORM_TILE, D), lambda i: (i, 0))
    slim = pl.BlockSpec((NORM_TILE, 128), lambda i: (i, 0))
    shape = jax.ShapeDtypeStruct
    return pl.pallas_call(
        norm_fwd_kernel,
        grid=(count // NORM_TILE,),
        in_specs=[ANY, rows, rows, whole((VEC_ROWS, 128))],
        out_specs=[rows, slim],
        out_shape=[shape((count, D), F32), shape((count, 128), F32)],
        scratch_shapes=[pltpu.VMEM((8, ATTN_TILES, 16, 128), BF), pltpu.SemaphoreType.DMA],
        compiler_params=params(),
        cost_estimate=cost(
            flops=2 * count * D * D, bytes_accessed=count * D * 9, transcendentals=0
        ),
        name="norm_fwd",
    )(wa, ctx, tokens, vec)


def ffn_copies(fast, me, refs, w1_s, w2_s, sems):
    if not fast:
        pairs = [[(refs[0].at[pl.ds(0, 16)], w1_s)], [(refs[0].at[pl.ds(16, 16)], w2_s)]]
    else:
        pairs = [
            piece_copies(me, refs, FFN_TILES, planes, lambda o, t, d=dst, f=first: d.at[o - f, t])
            for planes, dst, first in ((range(2), w1_s, 0), (range(2, 4), w2_s, 16))
        ]
    return [
        [pltpu.make_async_copy(src, dst, sems.at[m, i]) for i, (src, dst) in enumerate(group)]
        for m, group in enumerate(pairs)
    ]


MID_TILE = 512


def pick(mine, even, odd):
    return jnp.where(mine == 0, even, odd), jnp.where(mine == 0, odd, even)


def norm_grad(normed, rstd, t):
    mean_t = jnp.mean(t, axis=1, keepdims=True)
    mean_tn = jnp.mean(t * normed, axis=1, keepdims=True)
    return (t - mean_t - normed * mean_tn) * rstd


def column_sum(value):
    return jnp.sum(value.astype(F32), axis=0, keepdims=True)


def ffn_kernel(fast, me_ref, *args):
    pieces = PIECES if fast else 1
    (
        wa_ref, n1_ref, rstd_ref, cot_ref, seg_ref, vec_ref,
        out_ref, dw1k_ref, dw1s_ref, dw2k_ref, dw2s_ref, vg_ref, dh1_ref, da_ref, dctx_ref,
        w1_s, w2_s, wo_s, g_s, gp_s, yb_s, ybt_s, dz_s, du_s, r_s, sems, wo_sem,
    ) = args[pieces:]
    step = pl.program_id(0)
    me = me_ref[0]
    core, my_x, my_y = me & 1, (me >> 1) & 1, (me >> 2) & 1
    copies = ffn_copies(fast, me, args[:pieces], w1_s, w2_s, sems)
    wo_copy = pltpu.make_async_copy(wa_ref.at[pl.ds(24, 8)], wo_s, wo_sem)
    count = n1_ref.shape[0]

    def tile(i, size):
        return pl.ds(pl.multiple_of(i * size, size), size)

    @pl.when(step == 0)
    def _():
        for group in copies:
            for copy in group:
                copy.start()
        wo_copy.start()

        def body(i, carry):
            rows = tile(i, NORM_TILE)
            y_one = n1_ref[rows, :] * row(vec_ref, 3) + row(vec_ref, 4)
            yb_s[rows, :] = y_one.astype(BF)
            dh1_ref[rows, :] = y_one + row(vec_ref, 9)
            return carry

        lax.fori_loop(0, count // NORM_TILE, body, 0)
        ybt_s[...] = yb_s[...].T
        for copy in copies[0]:
            copy.wait()

    @pl.when(step < 4)
    def _():
        def widen(sub, carry):
            lanes = tile(sub, 256)
            weight = jnp.concatenate([up_col(w1_s, step * 6 + 2 * sub + i) for i in range(2)], axis=1)
            first = 6 * (5 + step) + 2 * sub
            bias = jnp.concatenate([vec_ref[pl.ds(first + i, 1), :] for i in range(2)], axis=1)
            act, slope = gelu_parts(dot(yb_s[...], weight, NN) + bias)
            g_s[step, :, lanes] = act.astype(BF)
            gp_s[step, :, lanes] = slope.astype(BF)
            return carry

        lax.fori_loop(0, 3, widen, 0)

        @pl.when(step == 0)
        def _():
            for copy in copies[1]:
                copy.wait()

        def narrow(i, carry):
            rows = tile(i, MID_TILE)
            dh1_ref[rows, :] += dot(g_s[step, rows, :], down_chunk(w2_s, step), NN)
            return carry

        lax.fori_loop(0, count // MID_TILE, narrow, 0)

    @pl.when(step == 3)
    def _():
        def body(i, sums):
            rows = tile(i, NORM_TILE)
            normed, rstd = norm_parts(dh1_ref[rows, :])
            gain = row(vec_ref, 10)
            out_ref[rows, :] = (normed * gain + row(vec_ref, 11)).astype(BF)
            err = cot_ref[rows, :].astype(F32)
            dh2 = norm_grad(normed, rstd, gain * err)
            dz = dh2.astype(BF)
            dh1_ref[rows, :] = dh2
            dz_s[rows, :] = dz
            return (
                sums[0] + column_sum(dz),
                sums[1] + column_sum(err * normed),
                sums[2] + column_sum(err),
            )

        zero = jnp.zeros((1, D), F32)
        sums = lax.fori_loop(0, count // NORM_TILE, body, (zero, zero, zero))
        vg_ref[...] = jnp.zeros_like(vg_ref)
        for i in range(3):
            put_row(vg_ref, 9 + i, sums[i])

    @pl.when(step >= 4)
    def _():
        chunk = step - 4

        def back(i, total):
            rows = tile(i, MID_TILE)
            dg = dot(dz_s[rows, :], down_chunk(w2_s, chunk), NT)
            du = (gp_s[chunk, rows, :].astype(F32) * dg).astype(BF)
            du_s[rows, :] = du
            dh1_ref[rows, :] += dot(du, up_chunk(w1_s, chunk), NT)
            return total + column_sum(du)

        put_row(vg_ref, 5 + chunk, lax.fori_loop(0, count // MID_TILE, back, jnp.zeros((1, D), F32)))

        def weights(half, carry):
            lanes = tile(half, 384)
            r_s[...] = dot(ybt_s[lanes, :], du_s[...], NN).astype(BF)
            for pair in range(4):
                even, odd = r_s[pl.ds(pair * 96, 48), :], r_s[pl.ds(pair * 96 + 48, 48), :]
                keep, send = pick(core, even, odd)
                place = (((pair >> 1) ^ my_y) << 1) | ((pair & 1) ^ my_x)
                for col in range(6):
                    spot = slice(col * 128, col * 128 + 128)
                    dw1k_ref[place, half, :, col] = keep[:, spot].reshape(3, 16, 128)
                    dw1s_ref[place, half, :, col] = send[:, spot].reshape(3, 16, 128)
            r_s[...] = dot(g_s[chunk, :, lanes], dz_s[...], TN).astype(BF)
            keep, send = pick(core, r_s[:192, :], r_s[192:, :])
            for col in range(6):
                spot = slice(col * 128, col * 128 + 128)
                dw2k_ref[half ^ my_x, 0, :, col] = keep[:, spot].reshape(12, 16, 128)
                dw2s_ref[half ^ my_x, 0, :, col] = send[:, spot].reshape(12, 16, 128)
            return carry

        lax.fori_loop(0, 2, weights, 0)

    @pl.when(step == 7)
    def _():
        wo_copy.wait()

        def body(i, sums):
            rows = tile(i, NORM_TILE)
            dy1, normed = dh1_ref[rows, :], n1_ref[rows, :]
            dh1 = norm_grad(normed, rstd_ref[rows, 0:1], dy1 * row(vec_ref, 3))
            da = dh1.astype(BF)
            dh1_ref[rows, :] = dh1
            da_ref[rows, :] = da
            back = dot(da, square(wo_s, 0), NT)
            dctx_ref[rows, :] = jnp.where(seg_ref[rows, :] >= 0, back, 0.0).astype(BF)
            return (
                sums[0] + column_sum(da),
                sums[1] + column_sum(dy1 * normed),
                sums[2] + column_sum(dy1),
            )

        zero = jnp.zeros((1, D), F32)
        sums = lax.fori_loop(0, count // NORM_TILE, body, (zero, zero, zero))
        for i in range(3):
            put_row(vg_ref, 2 + i, sums[i])


def ffn_layer(fast, me, pieces, wa, n1, rstd, cotangent, segc, vec):
    count = n1.shape[0]
    once = pl.Buffered(1)

    def single(shape):
        zeros = (0,) * len(shape)
        return pl.BlockSpec(shape, lambda *_: zeros, pipeline_mode=once)

    full = whole((count, D))
    up = pl.BlockSpec(
        (4, 2, 3, 6, 16, 128), lambda s, m: (0, 0, 0, jnp.maximum(s - 4, 0), 0, 0)
    )

    def down_index(s, m):
        chunk = jnp.maximum(s - 4, 0)
        return ((chunk % 2) ^ ((m[0] >> 2) & 1), chunk // 2, 0, 0, 0, 0)

    down = pl.BlockSpec((2, 1, 12, 6, 16, 128), down_index)
    shape = jax.ShapeDtypeStruct
    return pl.pallas_call(
        functools.partial(ffn_kernel, fast),
        grid_spec=pltpu.PrefetchScalarGridSpec(
            num_scalar_prefetch=1,
            grid=(8,),
            in_specs=[ANY] * len(pieces)
            + [
                ANY,
                single((count, D)),
                single((count, 128)),
                single((count, D)),
                single((count, 1)),
                single((VEC_ROWS, 128)),
            ],
            out_specs=[full, up, up, down, down, whole((VEC_ROWS, 128)), full, full, full],
            scratch_shapes=[
                pltpu.VMEM((16, FFN_TILES, 16, 128), BF),
                pltpu.VMEM((16, FFN_TILES, 16, 128), BF),
                pltpu.VMEM((8, ATTN_TILES, 16, 128), BF),
                pltpu.VMEM((4, count, D), BF),
                pltpu.VMEM((4, count, D), BF),
                pltpu.VMEM((count, D), BF),
                pltpu.VMEM((D, count), BF),
                pltpu.VMEM((count, D), BF),
                pltpu.VMEM((count, D), BF),
                pltpu.VMEM((D // 2, D), BF),
                pltpu.SemaphoreType.DMA((2, 40)),
                pltpu.SemaphoreType.DMA,
            ],
        ),
        out_shape=[shape((count, D), BF)]
        + [shape((4, 2, 3, 24, 16, 128), BF)] * 2
        + [shape((4, 2, 12, 6, 16, 128), BF)] * 2
        + [shape((VEC_ROWS, 128), F32), shape((count, D), F32)]
        + [shape((count, D), BF)] * 2,
        compiler_params=params(),
        cost_estimate=cost(
            flops=12 * count * D * FF, bytes_accessed=count * D * 30, transcendentals=count * FF
        ),
        name="ffn_layer",
    )(me, *pieces, wa, n1, rstd, cotangent, segc, vec)


def attn_bwd_kernel(
    first, span_ref, q_ref, k_ref, v_ref, ctx_ref, dctx_ref, lse_ref, segc_ref, segr_ref, d_ref, dqt_s, dots_s
):
    line = pl.program_id(0)
    pairs = q_ref.shape[1] // 128
    lane = lax.broadcasted_iota(jnp.int32, (1, 128), 1)
    low = lane < 64
    zero = jnp.zeros((), BF)
    spots = [slice(128 * pair, 128 * pair + 128) for pair in range(pairs)]
    for pair, lanes in enumerate(spots):
        products = (dctx_ref[:, lanes].astype(F32) * ctx_ref[:, lanes].astype(F32)).T
        for head in range(2):
            place = slice(4 * pair + head, 4 * pair + head + 1)
            dots_s[place, :] = jnp.sum(products[64 * head : 64 * head + 64], axis=0, keepdims=True)
            index = 2 * (first + pair) + head
            place = slice(4 * pair + 2 + head, 4 * pair + 3 + head)
            dots_s[place, :] = lse_ref[index // 4, index % 4 : index % 4 + 1, :]
    dqt_s[...] = jnp.zeros_like(dqt_s)

    def both(value):
        return jnp.concatenate([jnp.where(low, value, zero), jnp.where(low, zero, value)], axis=0)

    def block_step(block, carry):
        rows = pl.ds(pl.multiple_of(block * 128, 128), 128)
        start, count = span_ref[line, 2 * block], span_ref[line, 2 * block + 1]

        @pl.when(count == 0)
        def _():
            d_ref[1, rows, :] = jnp.zeros((128, 128 * pairs), BF)
            d_ref[2, rows, :] = jnp.zeros((128, 128 * pairs), BF)

        def window(size):
            @pl.when(count == size)
            def _():
                seen = pl.ds(pl.multiple_of(start * 128, 128), 128 * size)
                seg_row = segr_ref[:, seen]
                allowed = segc_ref[rows, :] == jnp.where(seg_row < 0, -2, seg_row)
                allowed = jnp.concatenate([allowed, allowed], axis=0)

                def spread(pair, offset):
                    lines = [dots_s[4 * pair + offset + h : 4 * pair + offset + h + 1, seen] for h in range(2)]
                    return jnp.concatenate([jnp.broadcast_to(r, (128, 128 * size)) for r in lines], axis=0)

                keys = [both(k_ref[rows, lanes]) for lanes in spots]
                queries = [q_ref[seen, lanes] for lanes in spots]
                dctxs = [dctx_ref[seen, lanes] for lanes in spots]
                scores = [dot(k, q, NT) for k, q in zip(keys, queries)]
                dprobs = [dot(both(v_ref[rows, lanes]), dctx, NT) for lanes, dctx in zip(spots, dctxs)]
                probs = [
                    jnp.where(allowed, jnp.exp(score - spread(pair, 2)), 0.0)
                    for pair, score in enumerate(scores)
                ]
                dscores = [
                    (prob * (dprob - spread(pair, 0))).astype(BF)
                    for pair, (prob, dprob) in enumerate(zip(probs, dprobs))
                ]
                dvs = [dot(prob.astype(BF), dctx, NN) for prob, dctx in zip(probs, dctxs)]
                dks = [dot(dscore, query, NN) for dscore, query in zip(dscores, queries)]
                dqs = [dot(key, dscore, TN) for key, dscore in zip(keys, dscores)]
                for pair, lanes in enumerate(spots):
                    dqt_s[lanes, seen] += dqs[pair]
                    d_ref[1, rows, lanes] = jnp.where(low, dks[pair][:128], dks[pair][128:]).astype(BF)
                    d_ref[2, rows, lanes] = jnp.where(low, dvs[pair][:128], dvs[pair][128:]).astype(BF)

        for size in range(1, 5):
            window(size)
        return carry

    lax.fori_loop(0, 4, block_step, 0)
    d_ref[0] = (dqt_s[...].T * 0.125).astype(BF)


def attn_bwd(span, query, key, value, ctx, dctx, lse, segc, segr, first, cols):
    count = query.shape[0]
    rows = count // SLOTS
    width = 128 * cols
    part = pl.BlockSpec((SLOTS, width), lambda r, s: (r, first // cols))
    return pl.pallas_call(
        functools.partial(attn_bwd_kernel, first),
        grid_spec=pltpu.PrefetchScalarGridSpec(
            num_scalar_prefetch=1,
            grid=(rows,),
            in_specs=[part] * 5
            + [
                pl.BlockSpec((None, 3, 4, SLOTS), lambda r, s: (r, 0, 0, 0)),
                pl.BlockSpec((SLOTS, 1), lambda r, s: (r, 0)),
                pl.BlockSpec((None, 1, SLOTS), lambda r, s: (r, 0, 0)),
            ],
            out_specs=pl.BlockSpec((3, SLOTS, width), lambda r, s: (0, r, 0)),
            scratch_shapes=[pltpu.VMEM((width, SLOTS), F32), pltpu.VMEM((4 * cols, SLOTS), F32)],
        ),
        out_shape=jax.ShapeDtypeStruct((3, count, width), BF),
        compiler_params=params(),
        cost_estimate=cost(
            flops=10 * count * D * SLOTS, bytes_accessed=count * D * 16, transcendentals=count * SLOTS * 12
        ),
        name="attn_bwd",
    )(span, query, key, value, ctx, dctx, lse, segc, segr)


def proj_grad_kernel(me_ref, x_ref, ctx_ref, first_ref, second_ref, da_ref, vg_in_ref, dwk_ref, dws_ref, vg_ref, r_s):
    step = pl.program_id(0)
    me = me_ref[0]
    core, my_x, my_y = me & 1, (me >> 1) & 1, (me >> 2) & 1

    @pl.when(step == 0)
    def _():
        vg_ref[...] = vg_in_ref[...]

    @pl.when(step < 3)
    def _():
        grad = jnp.concatenate([first_ref[...], second_ref[...]], axis=1)
        r_s[...] = dot(x_ref[...], grad, TN).astype(BF)

        @pl.when(step != 1)
        def _():
            put_row(vg_ref, step >> 1, column_sum(grad))

    @pl.when(step == 3)
    def _():
        r_s[...] = dot(ctx_ref[...], da_ref[...], TN).astype(BF)

    for pair in range(4):
        even, odd = r_s[pl.ds(pair * 192, 96), :], r_s[pl.ds(pair * 192 + 96, 96), :]
        keep, send = pick(core, even, odd)
        place = (((pair >> 1) ^ my_y) << 1) | ((pair & 1) ^ my_x)
        for col in range(6):
            lanes = slice(col * 128, col * 128 + 128)
            dwk_ref[place, 0, :, col] = keep[:, lanes].reshape(6, 16, 128)
            dws_ref[place, 0, :, col] = send[:, lanes].reshape(6, 16, 128)


def proj_grad(me, tokens, ctx, first, second, da, vg):
    count, width = first.shape[1:]
    out = pl.BlockSpec((4, 1, 6, 6, 16, 128), lambda i, m: (0, i, 0, 0, 0, 0))
    full = whole((count, D))
    part = pl.BlockSpec((None, count, width), lambda i, m: (jnp.minimum(i, 2), 0, 0))
    shape = jax.ShapeDtypeStruct
    return pl.pallas_call(
        proj_grad_kernel,
        grid_spec=pltpu.PrefetchScalarGridSpec(
            num_scalar_prefetch=1,
            grid=(4,),
            in_specs=[full, full, part, part, full, whole((VEC_ROWS, 128))],
            out_specs=[out, out, whole((VEC_ROWS, 128))],
            scratch_shapes=[pltpu.VMEM((D, D), BF)],
        ),
        out_shape=[shape((4, 4, 6, 6, 16, 128), BF)] * 2 + [shape((VEC_ROWS, 128), F32)],
        compiler_params=params(),
        cost_estimate=cost(
            flops=8 * count * D * D, bytes_accessed=count * D * 20, transcendentals=0
        ),
        name="proj_grad",
    )(me, tokens, ctx, first, second, da, vg)


def input_grad_kernel(wa_ref, dh1_ref, da_ref, db_ref, out_ref, w_s, sems):
    @pl.when(pl.program_id(0) == 0)
    def _():
        copies = [
            pltpu.make_async_copy(
                wa_ref.at[pl.ds(8 * m, 8)],
                w_s.at[pl.ds(8 * m, 8)],
                sems.at[m],
            )
            for m in range(3)
        ]
        for copy in copies:
            copy.start()
        for copy in copies:
            copy.wait()

    total = dh1_ref[...]
    for m in range(3):
        grad = jnp.concatenate([da_ref[m], db_ref[m]], axis=1)
        total = total + dot(grad, square(w_s, 8 * m), NT)
    out_ref[...] = total.astype(BF)


def input_grad(wa, dh1, first, second):
    count = dh1.shape[0]
    rows = pl.BlockSpec((NORM_TILE, D), lambda i: (i, 0))
    return pl.pallas_call(
        input_grad_kernel,
        grid=(count // NORM_TILE,),
        in_specs=[ANY, rows] + [pl.BlockSpec((3, NORM_TILE, D // 2), lambda i: (0, i, 0))] * 2,
        out_specs=rows,
        out_shape=jax.ShapeDtypeStruct((count, D), BF),
        scratch_shapes=[
            pltpu.VMEM((24, ATTN_TILES, 16, 128), BF),
            pltpu.SemaphoreType.DMA((3,)),
        ],
        compiler_params=params(),
        cost_estimate=cost(
            flops=6 * count * D * D, bytes_accessed=count * D * 18, transcendentals=0
        ),
        name="input_grad",
    )(wa, dh1, first, second)


def retile(flat, blocks):
    tall = flat.shape[0] // (16 * blocks)
    tiles = flat.reshape(tall, 16, blocks, 128).transpose(0, 2, 1, 3)
    return tiles.reshape(tall * blocks, 16, 128)


def untile(tiles, blocks):
    tall = tiles.shape[0] // blocks
    flat = tiles.reshape(tall, blocks, 16, 128).transpose(0, 2, 1, 3)
    return flat.reshape(tall * blocks * 16, 128)


def pad_vectors(flat):
    return jnp.pad(flat, (0, VEC_ROWS * 128 - flat.shape[0])).reshape(VEC_TILES, 16, 128)


def gather_plain(attn, ffn, vectors):
    attn = lax.all_gather(attn, "fsdp", axis=0, tiled=True)
    ffn = lax.all_gather(ffn, "fsdp", axis=0, tiled=True)
    vec = lax.all_gather(vectors, "fsdp", axis=0, tiled=True)
    half = ffn.shape[0] // 2
    tiles = jnp.concatenate([retile(ffn[:half], 24), retile(ffn[half:], 6)], axis=0)
    attn_tiles = retile(attn, 6).reshape(OWNERS, ATTN_TILES, 16, 128)
    return attn_tiles, tiles.reshape(OWNERS, FFN_TILES, 16, 128), pad_vectors(vec)[None]


class Gather:
    def __init__(self, tiles, vec=None):
        self.own, self.tiles, self.vec = tiles, tiles.shape[0], vec

    def ride(self, message):
        return message if self.vec is None else jnp.concatenate([message, self.vec], axis=0)

    def landed(self, messages, size):
        if self.vec is None:
            return messages
        total = self.vec.astype(F32) + sum(m[size:].astype(F32) for m in messages)
        self.vec = total.astype(BF)
        return [m[:size] for m in messages]

    def planes(self):
        message = self.ride(self.own)
        self.hops = [hop(message, 8 * step) for step in (1, 2, 3)]

    def sides(self):
        self.own = jnp.concatenate([self.own] + self.landed(self.hops, self.tiles), axis=0)
        self.hops = [hop(self.ride(self.own), 2), hop(self.own, 4)]
        self.mirror = [hop(self.own, 1)]

    def corner(self):
        (self.over_x,) = self.landed(self.hops[:1], 4 * self.tiles)
        self.over_y = self.hops[1]
        shape = (4, self.tiles, 16, 128)
        half = self.tiles // 2
        low = self.over_y.reshape(shape)[:, :half].reshape(-1, 16, 128)
        high = self.over_x.reshape(shape)[:, half:].reshape(-1, 16, 128)
        self.hops = [hop(low, 2), hop(self.ride(high), 4)]
        self.mirror += [hop(self.over_x, 1), hop(self.over_y, 1)]

    def pieces(self):
        half = self.tiles // 2
        (high,) = self.landed(self.hops[1:], 4 * half)
        corners = [part.reshape(4, half, 16, 128) for part in (self.hops[0], high)]
        mirror = self.mirror + [hop(part, 1) for part in corners]
        return [self.own, self.over_x, self.over_y] + corners + mirror

    def vectors(self):
        return jnp.stack([self.vec, hop(self.vec, 1)], axis=0)


def hop(value, bit):
    pairs = [(i, i ^ bit) for i in range(OWNERS)]
    return lax.ppermute(value, "fsdp", pairs)


def reduce_plain(ffn_terms, attn_terms, vector_terms):
    def absolute(keep, send):
        planes = keep.shape[1]
        both = jnp.stack([keep, send], axis=1)
        return jnp.moveaxis(both, 2, 0).reshape(planes * 8, -1, 16, 128)

    dw1k, dw1s, dw2k, dw2s = ffn_terms
    up = untile(absolute(dw1k, dw1s).reshape(-1, 16, 128), 24)
    down = untile(absolute(dw2k, dw2s).reshape(-1, 16, 128), 6)
    proj = untile(absolute(*attn_terms).reshape(-1, 16, 128), 6)

    def scatter(value):
        return lax.psum_scatter(value.astype(F32), "fsdp", scatter_dimension=0, tiled=True)

    return scatter(proj), scatter(jnp.concatenate([up, down], axis=0)), scatter(vector_terms)


def get(message, index, tiles):
    if len(message.shape) == 3:
        return message[pl.ds(index * tiles, tiles)].astype(F32)
    return message[index].astype(F32)


def put(message, index, tiles, value):
    if len(message.shape) == 3:
        message[pl.ds(index * tiles, tiles)] = value.astype(message.dtype)
    else:
        message[index] = value.astype(message.dtype)


def take_terms(refs, spots, leaves):
    terms = {}
    for spot in spots:
        planes = []
        for _ in range(leaves):
            keep, other = refs.pop(0), refs.pop(0)
            planes += [(keep, other, p) for p in range(keep.shape[1])]
        terms[spot] = planes

    def term(spot, index):
        keep, other, plane = terms[spot][index]
        return keep[0, plane].astype(F32) + other[0, plane].astype(F32)

    return term, terms[spots[0]][0][0].shape[2]


def take_vec(refs, vec):
    if not vec:
        return None
    state, arrival = refs.pop(0), refs.pop(0)
    return state[...] + arrival[pl.ds(arrival.shape[0] - VEC_TILES, VEC_TILES)].astype(F32)


def put_tail(message, total):
    message[pl.ds(message.shape[0] - VEC_TILES, VEC_TILES)] = total.astype(BF)


def corner_kernel(leaves, vec, *refs):
    refs = list(refs)
    term, tiles = take_terms(refs, [(3, 0), (3, 1), (1, 0), (2, 1)], leaves)
    total = take_vec(refs, vec)
    to_x, to_y = refs[:2]
    for i in range(2):
        put(to_x, i, tiles, term((3, 0), i))
        put(to_x, 2 + i, tiles, term((1, 0), i))
        put(to_y, i, tiles, term((3, 1), i))
        put(to_y, 2 + i, tiles, term((2, 1), i))
    if vec:
        put_tail(to_x, total)
        refs[2][...] = total


def side_kernel(leaves, vec, *refs):
    refs = list(refs)
    term, tiles = take_terms(refs, [(1, 1), (2, 0)], leaves)
    from_x, from_y = refs.pop(0), refs.pop(0)
    total = take_vec(refs, vec)
    to_x, to_y = refs[:2]
    for i in range(2):
        put(to_x, i, tiles, term((1, 1), i) + get(from_y, i, tiles))
        put(to_y, i, tiles, term((2, 0), i) + get(from_x, i, tiles))
    if vec:
        put_tail(to_y, total)
        refs[2][...] = total


def plane_kernel(leaves, vec, me_ref, *refs):
    refs = list(refs)
    term, tiles = take_terms(refs, [(0, 0), (0, 1)], leaves)
    from_x, from_y, from_x_two, from_y_two = (refs.pop(0) for _ in range(4))
    total = take_vec(refs, vec)
    mine, outs, own = refs[0], refs[1:4], refs[-1]
    for i in range(2):
        lower = term((0, 0), i) + get(from_x, 2 + i, tiles) + get(from_y_two, i, tiles)
        upper = term((0, 1), i) + get(from_y, 2 + i, tiles) + get(from_x_two, i, tiles)
        own[2 * i if leaves == 2 else i] = lower
        own[2 * i + 1 if leaves == 2 else 2 + i] = upper
    my_z = me_ref[0] >> 3
    mine[...] = own[my_z]
    for step in range(3):
        if vec:
            outs[step][pl.ds(0, tiles)] = own[my_z ^ (step + 1)].astype(BF)
            put_tail(outs[step], total)
        else:
            outs[step][...] = own[my_z ^ (step + 1)].astype(BF)
    if vec:
        refs[4][...] = total


class Reduction:
    def __init__(self, keeps, sends, me, vec=None):
        self.keeps, self.me, self.vec = keeps, me, vec
        self.hops = [hop(send, 1) for send in sends]
        if vec is not None:
            self.hops.append(hop(vec.astype(BF), 1))
        self.tiles = keeps[0].shape[2]
        self.steps = 3 if vec is None else 1

    def run(self, kernel, spots, arrivals, outs, name, place=False):
        leaves, tiles, block = len(self.keeps), self.tiles, self.tiles // self.steps
        carries = self.vec is not None
        arrays, in_specs = [], []
        for spot, half in spots:
            for keep, other in zip(self.keeps, self.received, strict=True):
                spec = pl.BlockSpec(
                    (1, keep.shape[1] // 2, block, 16, 128),
                    lambda t, *_, spot=spot, half=half: (spot, half, t, 0, 0),
                )
                arrays += [keep, other]
                in_specs += [spec, spec]

        def message_spec(shape):
            if len(shape) == 4:
                return pl.BlockSpec((shape[0], block, 16, 128), lambda t, *_: (0, t, 0, 0))
            if carries:
                return whole(shape)
            return pl.BlockSpec((block, 16, 128), lambda t, *_: (t, 0, 0))

        for array in arrivals:
            arrays.append(array)
            in_specs.append(message_spec(array.shape))
        if carries:
            arrays += [self.vec, self.vec_arrival]
            in_specs += [whole(self.vec.shape), whole(self.vec_arrival.shape)]
        out_shape = []
        for planes, dtype, tail in outs:
            tail = VEC_TILES if tail and carries else 0
            if carries:
                dims = (planes * tiles + tail, 16, 128)
            else:
                dims = (planes, tiles, 16, 128) if planes > 1 else (tiles, 16, 128)
            out_shape.append(jax.ShapeDtypeStruct(dims, dtype))
        out_specs = [message_spec(shape.shape) for shape in out_shape]
        if carries:
            out_shape.append(jax.ShapeDtypeStruct(self.vec.shape, F32))
            out_specs.append(whole(self.vec.shape))
        result = pl.pallas_call(
            functools.partial(kernel, leaves, carries),
            grid_spec=pltpu.PrefetchScalarGridSpec(
                num_scalar_prefetch=1 if place else 0,
                grid=(self.steps,),
                in_specs=in_specs,
                out_specs=out_specs,
                scratch_shapes=[pltpu.VMEM((4, block, 16, 128), F32)] if place else [],
            ),
            out_shape=out_shape,
            compiler_params=params(),
            cost_estimate=cost(flops=0, bytes_accessed=tiles * 4096 * 16, transcendentals=0),
            name=name,
        )(*([self.me] if place else []), *arrays)
        if carries:
            *result, self.vec = result
        return result

    def corner(self):
        self.received = self.hops[: len(self.keeps)]
        self.vec_arrival = self.hops[-1]
        to_x, to_y = self.run(
            corner_kernel, [(3, 0), (3, 1), (1, 0), (2, 1)], [], [(4, BF, True), (4, BF, False)], "corner"
        )
        self.hops = [hop(to_x, 2), hop(to_y, 4)]

    def sides(self):
        self.early = self.hops
        self.vec_arrival = self.hops[0]
        to_x, to_y = self.run(
            side_kernel, [(1, 1), (2, 0)], self.early, [(2, BF, False), (2, BF, True)], "sides"
        )
        self.hops = [hop(to_x, 2), hop(to_y, 4)]

    def planes(self):
        self.vec_arrival = self.hops[1]
        outs = [(1, F32, False)] + [(1, BF, True)] * 3
        self.mine, *messages = self.run(
            plane_kernel, [(0, 0), (0, 1)], self.early + self.hops, outs, "planes", place=True
        )
        self.hops = messages

    def cross(self):
        self.hops = [hop(message, 8 * (i + 1)) for i, message in enumerate(self.hops)]

    def total(self):
        tiles = self.tiles
        if self.vec is not None:
            self.vec = self.vec + sum(other[tiles:].astype(F32) for other in self.hops)
        return self.mine + sum(other[:tiles].astype(F32) for other in self.hops)


def meet(hops, values):
    return lax.optimization_barrier((hops, values))


def tiles_of(array):
    return array.reshape(array.shape[:2] + (-1, 16, 128))


def spans(segments, pad_segment):
    pad = pad_segment[:, None]
    seen = jnp.where(segments == pad, -1, segments)
    first, last = segments[:, ::128], segments[:, 127::128]
    last = jnp.minimum(last, pad - 1)
    below = jnp.sum(segments[:, None, :] < first[:, :, None], axis=2)
    upto = jnp.sum(segments[:, None, :] <= last[:, :, None], axis=2)
    start = below // 128
    count = jnp.where(first == pad, 0, (upto + 127) // 128 - start)
    both = jnp.stack([jnp.where(count == 0, 0, start), count], axis=2)
    return seen, both.reshape(segments.shape[0], 8).astype(jnp.int32)


def layer(tokens, attn_matrices, ffn_matrices, vectors, segments, pad_segment, cotangent, size):
    fast = size == OWNERS
    each = vectors.shape[0]
    place = lax.axis_index("fsdp") if fast else jnp.zeros((), jnp.int32)
    me = place.reshape(1).astype(jnp.int32)
    my_z = place >> 3
    rows = segments.shape[0]
    seen, span = spans(segments, pad_segment)
    segc = seen.reshape(rows * SLOTS, 1)
    segr = seen.reshape(rows, 1, SLOTS)

    if fast:
        lower = place < OWNERS // 2
        flat = jnp.zeros((VEC_ROWS * 128,), BF)
        mine = lax.dynamic_update_slice(flat, vectors, (place * each,)).reshape(VEC_TILES, 16, 128)
        attn_in = Gather(retile(attn_matrices, 6), mine)
        ffn_in = Gather(jnp.where(lower, retile(ffn_matrices, 24), retile(ffn_matrices, 6)))
        attn_in.planes()
        attn_in.hops, ffn_in.own = meet(attn_in.hops, ffn_in.own)
        ffn_in.planes()
        attn_in.sides()
        attn_in.corner()
        pieces, vecs = attn_in.pieces(), attn_in.vectors()
        ffn_in.hops, pieces = meet(ffn_in.hops, pieces)
        ffn_in.sides()
    else:
        gathered, ffn_tiles, vecs = gather_plain(attn_matrices, ffn_matrices, vectors)
        pieces = [gathered]
    query, key, value, ctx, lse, wa, vec = attn_fwd(
        fast, me, span, pieces, vecs, tokens, segc, segr
    )
    if fast:
        ffn_in.hops, (ctx, wa, vec) = meet(ffn_in.hops, (ctx, wa, vec))
        ffn_in.corner()
    n1, rstd = norm_fwd(wa, ctx, tokens, vec)
    if fast:
        ffn_in.hops, (n1, rstd) = meet(ffn_in.hops, (n1, rstd))
        ffn_pieces = ffn_in.pieces()
    else:
        ffn_pieces = [ffn_tiles]
    out, dw1k, dw1s, dw2k, dw2s, vg, dh1, da, dctx = ffn_layer(
        fast, me, ffn_pieces, wa, n1, rstd, cotangent, segc, vec
    )
    if not fast:
        first = attn_bwd(span, query, key, value, ctx, dctx, lse, segc, segr, 0, 3)
        second = attn_bwd(span, query, key, value, ctx, dctx, lse, segc, segr, 3, 3)
        dwk, dws, vg = proj_grad(me, tokens, ctx, first, second, da, vg)
        dx = input_grad(wa, dh1, first, second)
        vector_terms = vg.reshape(-1)[: 12 * D]
        return (out, dx) + reduce_plain((dw1k, dw1s, dw2k, dw2s), (dwk, dws), vector_terms)

    ffn = Reduction([tiles_of(dw1k), tiles_of(dw2k)], [tiles_of(dw1s), tiles_of(dw2s)], me)
    first = attn_bwd(span, query, key, value, ctx, dctx, lse, segc, segr, 0, 3)
    ffn.hops, (first, dctx) = meet(ffn.hops, (first, dctx))
    ffn.corner()
    second = attn_bwd(span, query, key, value, ctx, dctx, lse, segc, segr, 3, 3)
    dwk, dws, vg = proj_grad(me, tokens, ctx, first, second, da, vg)
    ffn.hops, (dwk, dws, vg, first) = meet(ffn.hops, (dwk, dws, vg, first))
    ffn.sides()
    attn = Reduction([tiles_of(dwk)], [tiles_of(dws)], me, vg.reshape(VEC_TILES, 16, 128))
    dx = input_grad(wa, dh1, first, second)
    (ffn.hops, attn.hops), dx = meet((ffn.hops, attn.hops), dx)
    ffn.planes()
    ffn.hops, attn.hops = meet(ffn.hops, attn.hops)
    ffn.cross()
    attn.corner()
    ffn.hops[:2], attn.hops = meet(ffn.hops[:2], attn.hops)
    attn.sides()
    ffn.hops[2:], attn.hops = meet(ffn.hops[2:], attn.hops)
    attn.planes()
    attn.cross()
    ffn.hops, attn.hops = meet(ffn.hops, attn.hops)

    ffn_sum = ffn.total()
    ffn_grad = jnp.where(lower, untile(ffn_sum, 24), untile(ffn_sum, 6))
    attn_grad = untile(attn.total(), 6)
    vector_grad = lax.dynamic_slice(attn.vec.reshape(-1), (place * each,), (each,))
    return out, dx, attn_grad, ffn_grad, vector_grad


def solution(mesh):
    size = mesh.shape["fsdp"]
    return jax.shard_map(
        functools.partial(layer, size=size),
        mesh=mesh,
        in_specs=(
            P("fsdp", None),
            P("fsdp", None),
            P("fsdp", None),
            P("fsdp"),
            P("fsdp", None),
            P("fsdp"),
            P("fsdp", None),
        ),
        out_specs=(P("fsdp", None), P("fsdp", None), P("fsdp", None), P("fsdp", None), P("fsdp")),
        check_vma=False,
    )
```

```python
import functools

import jax
import jax.numpy as jnp
from jax import lax
from jax.experimental import pallas as pl
from jax.experimental.pallas import tpu as pltpu
from jax.sharding import PartitionSpec as P

D = 768
FF = 3072
SLOTS = 512
BF = jnp.bfloat16
F32 = jnp.float32
NN = ((1,), (0,))
NT = ((1,), (1,))
TN = ((0,), (0,))
OWNERS = 32
ATTN_TILES = 36
FFN_TILES = 72
COST_SCALE = 1
VMEM_LIMIT = 64 * 1024 * 1024

TAIL_SLOPE = 0.39 * 0.5**0.5
TAIL_POLY = (
    0.11766260955586648,
    0.04569420719462487,
    0.32477969950633645,
    -0.3177001395785759,
    0.44333218507090993,
    -0.11376856259852677,
)


def dot(left, right, dims):
    return lax.dot_general(left, right, (dims, ((), ())), preferred_element_type=F32)


def params(**kwargs):
    return pltpu.CompilerParams(vmem_limit_bytes=VMEM_LIMIT, **kwargs)


def cost(flops, bytes_accessed, transcendentals):
    return pl.CostEstimate(
        flops=flops // COST_SCALE,
        bytes_accessed=bytes_accessed // COST_SCALE,
        transcendentals=transcendentals // COST_SCALE,
    )


def whole(shape):
    zeros = (0,) * len(shape)
    return pl.BlockSpec(shape, lambda *_: zeros)


ANY = pl.BlockSpec(memory_space=pl.ANY)
VEC_TILES = 5
VEC_ROWS = 16 * VEC_TILES


def row(vec_ref, index, width=D):
    blocks = width // 128
    return jnp.concatenate([vec_ref[pl.ds(6 * index + i, 1), :] for i in range(blocks)], axis=1)


def put_row(vec_ref, index, value, first=0):
    for i in range(value.shape[1] // 128):
        vec_ref[pl.ds(6 * index + first + i, 1), :] = value[:, 128 * i : 128 * i + 128]


def square_cols(tiles, first, col):
    parts = [tiles[pl.ds(first, 8), i * 6 + col] for i in range(6)]
    return jnp.stack(parts, axis=1).reshape(D, 128)


def square(tiles, first):
    return jnp.concatenate([square_cols(tiles, first, col) for col in range(6)], axis=1)


def up_col(tiles, col):
    parts = [tiles[:, i * 24 + col] for i in range(3)]
    return jnp.stack(parts, axis=1).reshape(D, 128)


def up_chunk(tiles, chunk):
    return jnp.concatenate([up_col(tiles, chunk * 6 + col) for col in range(6)], axis=1)


def down_chunk(tiles, chunk):
    cols = []
    for col in range(6):
        parts = [tiles[pl.ds(4 * chunk, 4), i * 6 + col] for i in range(12)]
        cols.append(jnp.stack(parts, axis=1).reshape(D, 128))
    return jnp.concatenate(cols, axis=1)


PIECES = 10


def piece_copies(me, refs, tiles, planes, dst):
    yxc, my_z = me & 7, me >> 3
    half = tiles // 2
    copies = []
    for core in range(2):
        own, over_x, over_y, low, high = refs[5 * core : 5 * core + 5]
        for z in planes:
            plane = my_z ^ z
            for side, ref in ((0, own), (1, over_x), (2, over_y)):
                owner = 8 * z + (yxc ^ (2 * side + core))
                copies.append((ref.at[pl.ds(plane * tiles, tiles)], dst(owner, pl.ds(0, tiles))))
            owner = 8 * z + (yxc ^ (6 + core))
            for part, ref in ((0, low), (1, high)):
                copies.append((ref.at[plane], dst(owner, pl.ds(part * half, half))))
    return copies


def attn_copies(fast, me, refs, w_s, sems):
    if not fast:
        return [pltpu.make_async_copy(refs[0], w_s, sems.at[0])]
    copies = piece_copies(me, refs, ATTN_TILES, range(4), lambda owner, tiles: w_s.at[owner, tiles])
    return [pltpu.make_async_copy(src, dst, sems.at[i]) for i, (src, dst) in enumerate(copies)]


def attn_fwd_kernel(fast, me_ref, span_ref, *args):
    count = PIECES if fast else 1
    refs = args[:count]
    (
        vec_ref, x_ref, segc_ref, segr_ref,
        q_ref, k_ref, v_ref, ctx_ref, lse_ref, wa_ref, vec_out_ref,
        w_s, vt_s, sems, out_sem,
    ) = args[count:]
    line, col = pl.program_id(0), pl.program_id(1)
    first_step = (line == 0) & (col == 0)
    last_step = (line == pl.num_programs(0) - 1) & (col == pl.num_programs(1) - 1)
    out_copy = pltpu.make_async_copy(w_s, wa_ref, out_sem)

    @pl.when(first_step)
    def _():
        copies = attn_copies(fast, me_ref[0], refs, w_s, sems)
        for copy in copies:
            copy.start()
        vec = vec_ref[0].astype(F32)
        for i in range(1, vec_ref.shape[0]):
            vec = vec + vec_ref[i].astype(F32)
        vec_out_ref[...] = vec.reshape(VEC_ROWS, 128)
        for copy in copies:
            copy.wait()
        out_copy.start()

    @pl.when(last_step)
    def _():
        out_copy.wait()

    cols = [2 * col, 2 * col + 1]
    weight = jnp.concatenate([square_cols(w_s, 8 * m, c) for m in range(3) for c in cols], axis=1)
    qkv = dot(x_ref[...], weight, NN)
    bias_q = jnp.concatenate([vec_out_ref[pl.ds(c, 1), :] for c in cols], axis=1)
    bias_v = jnp.concatenate([vec_out_ref[pl.ds(6 + c, 1), :] for c in cols], axis=1)
    q_ref[...] = (qkv[:, :256] + bias_q).astype(BF) * 0.125
    k_ref[...] = qkv[:, 256:512].astype(BF)
    v_ref[...] = (qkv[:, 512:] + bias_v).astype(BF)
    lane = lax.broadcasted_iota(jnp.int32, (1, 128), 1)
    low = lane < 64
    zero = jnp.zeros((), BF)

    for pair in range(2):
        vt_s[pl.ds(128 * pair, 128), :] = v_ref[:, 128 * pair : 128 * pair + 128].T

    def attend(block, carry):
        rows = pl.ds(pl.multiple_of(block * 128, 128), 128)
        start, count = span_ref[line, 2 * block], span_ref[line, 2 * block + 1]

        @pl.when(count == 0)
        def _():
            ctx_ref[rows, :] = jnp.zeros((128, 256), BF)
            lse_ref[:, rows] = jnp.zeros((4, 128), F32)

        def window(size):
            @pl.when(count == size)
            def _():
                seen = pl.ds(pl.multiple_of(start * 128, 128), 128 * size)
                seg_row = segr_ref[:, rows]
                blocked = jnp.where(segc_ref[seen, :] == seg_row, 0.0, -1e30)
                keep = jnp.where(jnp.broadcast_to(seg_row, (64, 128)) < 0, 0.0, 1.0)
                scores = []
                for head in range(4):
                    lanes = slice(128 * (head // 2), 128 * (head // 2) + 128)
                    query = q_ref[rows, lanes]
                    query = jnp.where(low, query, zero) if head % 2 == 0 else jnp.where(low, zero, query)
                    scores.append(dot(k_ref[seen, lanes], query, NT) + blocked)
                tops = [jnp.max(score, axis=0, keepdims=True) for score in scores]
                expds = [jnp.exp(score - top) for score, top in zip(scores, tops)]
                totals = [jnp.sum(expd, axis=0, keepdims=True) for expd in expds]
                outs = []
                for head in range(4):
                    values = vt_s[pl.ds(64 * head, 64), seen]
                    out = dot(values, expds[head].astype(BF), NN)
                    outs.append(out * (1.0 / totals[head]) * keep)
                    lse_ref[pl.ds(head, 1), rows] = tops[head] + jnp.log(totals[head])
                ctx_ref[rows, :] = jnp.concatenate(outs, axis=0).T.astype(BF)

        for size in range(1, 5):
            window(size)
        return carry

    lax.fori_loop(0, 4, attend, 0)


def attn_fwd(fast, me, span, pieces, vec, tokens, segc, segr):
    count = tokens.shape[0]
    rows = count // SLOTS
    part = pl.BlockSpec((SLOTS, 256), lambda r, j, m, s: (r, j))
    slot = pl.BlockSpec((SLOTS, 1), lambda r, j, m, s: (r, 0))
    shape = jax.ShapeDtypeStruct
    return pl.pallas_call(
        functools.partial(attn_fwd_kernel, fast),
        grid_spec=pltpu.PrefetchScalarGridSpec(
            num_scalar_prefetch=2,
            grid=(rows, 3),
            in_specs=[ANY] * len(pieces)
            + [
                whole(vec.shape),
                pl.BlockSpec((SLOTS, D), lambda r, j, m, s: (r, 0)),
                slot,
                pl.BlockSpec((None, 1, SLOTS), lambda r, j, m, s: (r, 0, 0)),
            ],
            out_specs=[part] * 4
            + [pl.BlockSpec((None, None, 4, SLOTS), lambda r, j, m, s: (r, j, 0, 0)), ANY, whole((VEC_ROWS, 128))],
            scratch_shapes=[
                pltpu.VMEM((OWNERS, ATTN_TILES, 16, 128), BF),
                pltpu.VMEM((256, SLOTS), BF),
                pltpu.SemaphoreType.DMA((160,)),
                pltpu.SemaphoreType.DMA,
            ],
        ),
        out_shape=[shape((count, D), BF)] * 4
        + [
            shape((rows, 3, 4, SLOTS), F32),
            shape((OWNERS, ATTN_TILES, 16, 128), BF),
            shape((VEC_ROWS, 128), F32),
        ],
        compiler_params=params(),
        cost_estimate=cost(
            flops=2 * count * D * (3 * D + 4 * SLOTS), bytes_accessed=count * D * 12, transcendentals=count * SLOTS * 12
        ),
        name="attn_fwd",
    )(me, span, *pieces, vec, tokens, segc, segr)


def norm_parts(hidden):
    mean = jnp.mean(hidden, axis=1, keepdims=True)
    centered = hidden - mean
    var = jnp.mean(centered * centered, axis=1, keepdims=True)
    rstd = lax.rsqrt(var + 1e-12)
    return centered * rstd, rstd


def gelu_parts(u):
    size = jnp.abs(u)
    t = pl.reciprocal(1.0 + TAIL_SLOPE * size)
    poly = jnp.full_like(t, TAIL_POLY[-1])
    for coef in TAIL_POLY[-2::-1]:
        poly = poly * t + coef
    bell = jnp.exp(u * u * -0.5)
    tail = poly * t * bell
    phi_cdf = jnp.where(u > 0, 1.0 - tail, tail)
    return u * phi_cdf, phi_cdf + u * bell * 0.3989422804014327


NORM_TILE = 256


def norm_fwd_kernel(wa_ref, ctx_ref, x_ref, vec_ref, n1_ref, rstd_ref, wo_s, sem):
    copy = pltpu.make_async_copy(wa_ref.at[pl.ds(24, 8)], wo_s, sem)

    @pl.when(pl.program_id(0) == 0)
    def _():
        copy.start()
        copy.wait()

    hidden = x_ref[...].astype(F32) + dot(ctx_ref[...], square(wo_s, 0), NN) + row(vec_ref, 2)
    normed, rstd = norm_parts(hidden)
    n1_ref[...] = normed
    rstd_ref[...] = jnp.broadcast_to(rstd, rstd_ref.shape)


def norm_fwd(wa, ctx, tokens, vec):
    count = tokens.shape[0]
    rows = pl.BlockSpec((NORM_TILE, D), lambda i: (i, 0))
    slim = pl.BlockSpec((NORM_TILE, 128), lambda i: (i, 0))
    shape = jax.ShapeDtypeStruct
    return pl.pallas_call(
        norm_fwd_kernel,
        grid=(count // NORM_TILE,),
        in_specs=[ANY, rows, rows, whole((VEC_ROWS, 128))],
        out_specs=[rows, slim],
        out_shape=[shape((count, D), F32), shape((count, 128), F32)],
        scratch_shapes=[pltpu.VMEM((8, ATTN_TILES, 16, 128), BF), pltpu.SemaphoreType.DMA],
        compiler_params=params(),
        cost_estimate=cost(
            flops=2 * count * D * D, bytes_accessed=count * D * 9, transcendentals=0
        ),
        name="norm_fwd",
    )(wa, ctx, tokens, vec)


def ffn_copies(fast, me, refs, w1_s, w2_s, sems):
    if not fast:
        pairs = [[(refs[0].at[pl.ds(0, 16)], w1_s)], [(refs[0].at[pl.ds(16, 16)], w2_s)]]
    else:
        pairs = [
            piece_copies(me, refs, FFN_TILES, planes, lambda o, t, d=dst, f=first: d.at[o - f, t])
            for planes, dst, first in ((range(2), w1_s, 0), (range(2, 4), w2_s, 16))
        ]
    return [
        [pltpu.make_async_copy(src, dst, sems.at[m, i]) for i, (src, dst) in enumerate(group)]
        for m, group in enumerate(pairs)
    ]


MID_TILE = 1024


def pick(mine, even, odd):
    return jnp.where(mine == 0, even, odd), jnp.where(mine == 0, odd, even)


def norm_grad(normed, rstd, t):
    mean_t = jnp.mean(t, axis=1, keepdims=True)
    mean_tn = jnp.mean(t * normed, axis=1, keepdims=True)
    return (t - mean_t - normed * mean_tn) * rstd


def column_sum(value):
    return jnp.sum(value.astype(F32), axis=0, keepdims=True)


def ffn_kernel(fast, me_ref, *args):
    pieces = PIECES if fast else 1
    (
        wa_ref, n1_ref, rstd_ref, cot_ref, seg_ref, vec_ref,
        out_ref, dw1k_ref, dw1s_ref, dw2k_ref, dw2s_ref, vg_ref, dh1_ref, da_ref, dctx_ref,
        w1_s, w2_s, wo_s, g_s, gp_s, yb_s, ybt_s, dz_s, du_s, r_s, ua_s, ub_s, sems, wo_sem,
    ) = args[pieces:]
    step = pl.program_id(0)
    me = me_ref[0]
    core, my_x, my_y = me & 1, (me >> 1) & 1, (me >> 2) & 1
    copies = ffn_copies(fast, me, args[:pieces], w1_s, w2_s, sems)
    wo_copy = pltpu.make_async_copy(wa_ref.at[pl.ds(24, 8)], wo_s, wo_sem)
    count = n1_ref.shape[0]

    def tile(i, size):
        return pl.ds(pl.multiple_of(i * size, size), size)

    @pl.when(step == 0)
    def _():
        for group in copies:
            for copy in group:
                copy.start()
        wo_copy.start()

        def body(i, carry):
            rows = tile(i, NORM_TILE)
            y_one = n1_ref[rows, :] * row(vec_ref, 3) + row(vec_ref, 4)
            yb_s[rows, :] = y_one.astype(BF)
            dh1_ref[rows, :] = y_one + row(vec_ref, 9)
            return carry

        lax.fori_loop(0, count // NORM_TILE, body, 0)
        ybt_s[...] = yb_s[...].T
        for copy in copies[0]:
            copy.wait()

    @pl.when(step == 0)
    def _():
        def weights_of(sub):
            weight = jnp.concatenate([up_col(w1_s, 2 * sub + i) for i in range(2)], axis=1)
            bias = jnp.concatenate([vec_ref[pl.ds(30 + 2 * sub + i, 1), :] for i in range(2)], axis=1)
            return weight, bias

        def advance(new_ref, new_sub, old_ref, old_sub):
            weight, bias = weights_of(new_sub)
            chunk = lax.div(old_sub, 3)
            lanes = tile(old_sub - 3 * chunk, 256)
            for first in range(0, count, 128):
                rows = slice(first, first + 128)
                new_ref[rows, :] = dot(yb_s[rows, :], weight, NN) + bias
                act, slope = gelu_parts(old_ref[rows, :])
                g_s[chunk, rows, lanes] = act.astype(BF)
                gp_s[chunk, rows, lanes] = slope.astype(BF)

        weight, bias = weights_of(0)
        ua_s[...] = dot(yb_s[...], weight, NN) + bias

        def widen(i, carry):
            advance(ub_s, 2 * i + 1, ua_s, 2 * i)
            advance(ua_s, jnp.minimum(2 * i + 2, 11), ub_s, 2 * i + 1)
            return carry

        lax.fori_loop(0, 6, widen, 0)
        for copy in copies[1]:
            copy.wait()

        def narrow(i, carry):
            rows = tile(i, MID_TILE)
            total = dh1_ref[rows, :]
            for chunk in range(4):
                total = total + dot(g_s[chunk, rows, :], down_chunk(w2_s, chunk), NN)
            dh1_ref[rows, :] = total
            return carry

        lax.fori_loop(0, count // MID_TILE, narrow, 0)

    @pl.when(step == 0)
    def _():
        def body(i, sums):
            rows = tile(i, NORM_TILE)
            normed, rstd = norm_parts(dh1_ref[rows, :])
            gain = row(vec_ref, 10)
            out_ref[rows, :] = (normed * gain + row(vec_ref, 11)).astype(BF)
            err = cot_ref[rows, :].astype(F32)
            dh2 = norm_grad(normed, rstd, gain * err)
            dz = dh2.astype(BF)
            dh1_ref[rows, :] = dh2
            dz_s[rows, :] = dz
            return (
                sums[0] + column_sum(dz),
                sums[1] + column_sum(err * normed),
                sums[2] + column_sum(err),
            )

        zero = jnp.zeros((1, D), F32)
        sums = lax.fori_loop(0, count // NORM_TILE, body, (zero, zero, zero))
        vg_ref[...] = jnp.zeros_like(vg_ref)
        for i in range(3):
            put_row(vg_ref, 9 + i, sums[i])

    @pl.when(step >= 1)
    def _():
        chunk = step - 1

        def back(i, total):
            rows = tile(i, MID_TILE)
            dg = dot(dz_s[rows, :], down_chunk(w2_s, chunk), NT)
            du = (gp_s[chunk, rows, :].astype(F32) * dg).astype(BF)
            du_s[rows, :] = du
            dh1_ref[rows, :] += dot(du, up_chunk(w1_s, chunk), NT)
            return total + column_sum(du)

        put_row(vg_ref, 5 + chunk, lax.fori_loop(0, count // MID_TILE, back, jnp.zeros((1, D), F32)))

        def weights(half, carry):
            lanes = tile(half, 384)
            r_s[...] = dot(ybt_s[lanes, :], du_s[...], NN).astype(BF)
            for pair in range(4):
                even, odd = r_s[pl.ds(pair * 96, 48), :], r_s[pl.ds(pair * 96 + 48, 48), :]
                keep, send = pick(core, even, odd)
                place = (((pair >> 1) ^ my_y) << 1) | ((pair & 1) ^ my_x)
                for col in range(6):
                    spot = slice(col * 128, col * 128 + 128)
                    dw1k_ref[place, half, :, col] = keep[:, spot].reshape(3, 16, 128)
                    dw1s_ref[place, half, :, col] = send[:, spot].reshape(3, 16, 128)
            r_s[...] = dot(g_s[chunk, :, lanes], dz_s[...], TN).astype(BF)
            keep, send = pick(core, r_s[:192, :], r_s[192:, :])
            for col in range(6):
                spot = slice(col * 128, col * 128 + 128)
                dw2k_ref[half ^ my_x, 0, :, col] = keep[:, spot].reshape(12, 16, 128)
                dw2s_ref[half ^ my_x, 0, :, col] = send[:, spot].reshape(12, 16, 128)
            return carry

        lax.fori_loop(0, 2, weights, 0)

    @pl.when(step == 4)
    def _():
        wo_copy.wait()

        def body(i, sums):
            rows = tile(i, NORM_TILE)
            dy1, normed = dh1_ref[rows, :], n1_ref[rows, :]
            dh1 = norm_grad(normed, rstd_ref[rows, 0:1], dy1 * row(vec_ref, 3))
            da = dh1.astype(BF)
            dh1_ref[rows, :] = dh1
            da_ref[rows, :] = da
            back = dot(da, square(wo_s, 0), NT)
            dctx_ref[rows, :] = jnp.where(seg_ref[rows, :] >= 0, back, 0.0).astype(BF)
            return (
                sums[0] + column_sum(da),
                sums[1] + column_sum(dy1 * normed),
                sums[2] + column_sum(dy1),
            )

        zero = jnp.zeros((1, D), F32)
        sums = lax.fori_loop(0, count // NORM_TILE, body, (zero, zero, zero))
        for i in range(3):
            put_row(vg_ref, 2 + i, sums[i])


def ffn_layer(fast, me, pieces, wa, n1, rstd, cotangent, segc, vec):
    count = n1.shape[0]
    once = pl.Buffered(1)

    def single(shape):
        zeros = (0,) * len(shape)
        return pl.BlockSpec(shape, lambda *_: zeros, pipeline_mode=once)

    full = whole((count, D))
    up = pl.BlockSpec(
        (4, 2, 3, 6, 16, 128), lambda s, m: (0, 0, 0, jnp.maximum(s - 1, 0), 0, 0)
    )

    def down_index(s, m):
        chunk = jnp.maximum(s - 1, 0)
        return ((chunk % 2) ^ ((m[0] >> 2) & 1), chunk // 2, 0, 0, 0, 0)

    down = pl.BlockSpec((2, 1, 12, 6, 16, 128), down_index)
    shape = jax.ShapeDtypeStruct
    return pl.pallas_call(
        functools.partial(ffn_kernel, fast),
        grid_spec=pltpu.PrefetchScalarGridSpec(
            num_scalar_prefetch=1,
            grid=(5,),
            in_specs=[ANY] * len(pieces)
            + [
                ANY,
                single((count, D)),
                single((count, 128)),
                single((count, D)),
                single((count, 1)),
                single((VEC_ROWS, 128)),
            ],
            out_specs=[full, up, up, down, down, whole((VEC_ROWS, 128)), full, full, full],
            scratch_shapes=[
                pltpu.VMEM((16, FFN_TILES, 16, 128), BF),
                pltpu.VMEM((16, FFN_TILES, 16, 128), BF),
                pltpu.VMEM((8, ATTN_TILES, 16, 128), BF),
                pltpu.VMEM((4, count, D), BF),
                pltpu.VMEM((4, count, D), BF),
                pltpu.VMEM((count, D), BF),
                pltpu.VMEM((D, count), BF),
                pltpu.VMEM((count, D), BF),
                pltpu.VMEM((count, D), BF),
                pltpu.VMEM((D // 2, D), BF),
                pltpu.VMEM((count, 256), F32),
                pltpu.VMEM((count, 256), F32),
                pltpu.SemaphoreType.DMA((2, 40)),
                pltpu.SemaphoreType.DMA,
            ],
        ),
        out_shape=[shape((count, D), BF)]
        + [shape((4, 2, 3, 24, 16, 128), BF)] * 2
        + [shape((4, 2, 12, 6, 16, 128), BF)] * 2
        + [shape((VEC_ROWS, 128), F32), shape((count, D), F32)]
        + [shape((count, D), BF)] * 2,
        compiler_params=params(),
        cost_estimate=cost(
            flops=12 * count * D * FF, bytes_accessed=count * D * 30, transcendentals=count * FF
        ),
        name="ffn_layer",
    )(me, *pieces, wa, n1, rstd, cotangent, segc, vec)


def attn_bwd_kernel(
    first, span_ref, q_ref, k_ref, v_ref, ctx_ref, dctx_ref, lse_ref, segc_ref, segr_ref, d_ref, dqt_s, dots_s
):
    line = pl.program_id(0)
    pairs = q_ref.shape[1] // 128
    lane = lax.broadcasted_iota(jnp.int32, (1, 128), 1)
    low = lane < 64
    zero = jnp.zeros((), BF)
    spots = [slice(128 * pair, 128 * pair + 128) for pair in range(pairs)]
    for pair, lanes in enumerate(spots):
        products = (dctx_ref[:, lanes].astype(F32) * ctx_ref[:, lanes].astype(F32)).T
        for head in range(2):
            place = slice(4 * pair + head, 4 * pair + head + 1)
            dots_s[place, :] = jnp.sum(products[64 * head : 64 * head + 64], axis=0, keepdims=True)
            index = 2 * (first + pair) + head
            place = slice(4 * pair + 2 + head, 4 * pair + 3 + head)
            dots_s[place, :] = lse_ref[index // 4, index % 4 : index % 4 + 1, :]
    dqt_s[...] = jnp.zeros_like(dqt_s)

    def both(value):
        return jnp.concatenate([jnp.where(low, value, zero), jnp.where(low, zero, value)], axis=0)

    def block_step(block, carry):
        rows = pl.ds(pl.multiple_of(block * 128, 128), 128)
        start, count = span_ref[line, 2 * block], span_ref[line, 2 * block + 1]

        @pl.when(count == 0)
        def _():
            d_ref[1, rows, :] = jnp.zeros((128, 128 * pairs), BF)
            d_ref[2, rows, :] = jnp.zeros((128, 128 * pairs), BF)

        def window(size):
            @pl.when(count == size)
            def _():
                seen = pl.ds(pl.multiple_of(start * 128, 128), 128 * size)
                seg_row = segr_ref[:, seen]
                allowed = segc_ref[rows, :] == jnp.where(seg_row < 0, -2, seg_row)
                allowed = jnp.concatenate([allowed, allowed], axis=0)

                def spread(pair, offset):
                    lines = [dots_s[4 * pair + offset + h : 4 * pair + offset + h + 1, seen] for h in range(2)]
                    return jnp.concatenate([jnp.broadcast_to(r, (128, 128 * size)) for r in lines], axis=0)

                keys = [both(k_ref[rows, lanes]) for lanes in spots]
                queries = [q_ref[seen, lanes] for lanes in spots]
                dctxs = [dctx_ref[seen, lanes] for lanes in spots]
                scores = [dot(k, q, NT) for k, q in zip(keys, queries)]
                dprobs = [dot(both(v_ref[rows, lanes]), dctx, NT) for lanes, dctx in zip(spots, dctxs)]
                probs = [
                    jnp.where(allowed, jnp.exp(score - spread(pair, 2)), 0.0)
                    for pair, score in enumerate(scores)
                ]
                dscores = [
                    (prob * (dprob - spread(pair, 0))).astype(BF)
                    for pair, (prob, dprob) in enumerate(zip(probs, dprobs))
                ]
                dvs = [dot(prob.astype(BF), dctx, NN) for prob, dctx in zip(probs, dctxs)]
                dks = [dot(dscore, query, NN) for dscore, query in zip(dscores, queries)]
                dqs = [dot(key, dscore, TN) for key, dscore in zip(keys, dscores)]
                for pair, lanes in enumerate(spots):
                    dqt_s[lanes, seen] += dqs[pair]
                    d_ref[1, rows, lanes] = jnp.where(low, dks[pair][:128], dks[pair][128:]).astype(BF)
                    d_ref[2, rows, lanes] = jnp.where(low, dvs[pair][:128], dvs[pair][128:]).astype(BF)

        for size in range(1, 5):
            window(size)
        return carry

    lax.fori_loop(0, 4, block_step, 0)
    d_ref[0] = (dqt_s[...].T * 0.125).astype(BF)


def attn_bwd(span, query, key, value, ctx, dctx, lse, segc, segr, first, cols):
    count = query.shape[0]
    rows = count // SLOTS
    width = 128 * cols
    part = pl.BlockSpec((SLOTS, width), lambda r, s: (r, first // cols))
    return pl.pallas_call(
        functools.partial(attn_bwd_kernel, first),
        grid_spec=pltpu.PrefetchScalarGridSpec(
            num_scalar_prefetch=1,
            grid=(rows,),
            in_specs=[part] * 5
            + [
                pl.BlockSpec((None, 3, 4, SLOTS), lambda r, s: (r, 0, 0, 0)),
                pl.BlockSpec((SLOTS, 1), lambda r, s: (r, 0)),
                pl.BlockSpec((None, 1, SLOTS), lambda r, s: (r, 0, 0)),
            ],
            out_specs=pl.BlockSpec((3, SLOTS, width), lambda r, s: (0, r, 0)),
            scratch_shapes=[pltpu.VMEM((width, SLOTS), F32), pltpu.VMEM((4 * cols, SLOTS), F32)],
        ),
        out_shape=jax.ShapeDtypeStruct((3, count, width), BF),
        compiler_params=params(),
        cost_estimate=cost(
            flops=10 * count * D * SLOTS, bytes_accessed=count * D * 16, transcendentals=count * SLOTS * 12
        ),
        name="attn_bwd",
    )(span, query, key, value, ctx, dctx, lse, segc, segr)


def proj_grad_kernel(me_ref, x_ref, ctx_ref, first_ref, second_ref, da_ref, vg_in_ref, dwk_ref, dws_ref, vg_ref, r_s):
    step = pl.program_id(0)
    me = me_ref[0]
    core, my_x, my_y = me & 1, (me >> 1) & 1, (me >> 2) & 1

    @pl.when(step == 0)
    def _():
        vg_ref[...] = vg_in_ref[...]

    @pl.when(step < 3)
    def _():
        grad = jnp.concatenate([first_ref[...], second_ref[...]], axis=1)
        r_s[...] = dot(x_ref[...], grad, TN).astype(BF)

        @pl.when(step != 1)
        def _():
            put_row(vg_ref, step >> 1, column_sum(grad))

    @pl.when(step == 3)
    def _():
        r_s[...] = dot(ctx_ref[...], da_ref[...], TN).astype(BF)

    for pair in range(4):
        even, odd = r_s[pl.ds(pair * 192, 96), :], r_s[pl.ds(pair * 192 + 96, 96), :]
        keep, send = pick(core, even, odd)
        place = (((pair >> 1) ^ my_y) << 1) | ((pair & 1) ^ my_x)
        for col in range(6):
            lanes = slice(col * 128, col * 128 + 128)
            dwk_ref[place, 0, :, col] = keep[:, lanes].reshape(6, 16, 128)
            dws_ref[place, 0, :, col] = send[:, lanes].reshape(6, 16, 128)


def proj_grad(me, tokens, ctx, first, second, da, vg):
    count, width = first.shape[1:]
    out = pl.BlockSpec((4, 1, 6, 6, 16, 128), lambda i, m: (0, i, 0, 0, 0, 0))
    full = whole((count, D))
    part = pl.BlockSpec((None, count, width), lambda i, m: (jnp.minimum(i, 2), 0, 0))
    shape = jax.ShapeDtypeStruct
    return pl.pallas_call(
        proj_grad_kernel,
        grid_spec=pltpu.PrefetchScalarGridSpec(
            num_scalar_prefetch=1,
            grid=(4,),
            in_specs=[full, full, part, part, full, whole((VEC_ROWS, 128))],
            out_specs=[out, out, whole((VEC_ROWS, 128))],
            scratch_shapes=[pltpu.VMEM((D, D), BF)],
        ),
        out_shape=[shape((4, 4, 6, 6, 16, 128), BF)] * 2 + [shape((VEC_ROWS, 128), F32)],
        compiler_params=params(),
        cost_estimate=cost(
            flops=8 * count * D * D, bytes_accessed=count * D * 20, transcendentals=0
        ),
        name="proj_grad",
    )(me, tokens, ctx, first, second, da, vg)


def input_grad_kernel(wa_ref, dh1_ref, da_ref, db_ref, out_ref, w_s, sems):
    @pl.when(pl.program_id(0) == 0)
    def _():
        copies = [
            pltpu.make_async_copy(
                wa_ref.at[pl.ds(8 * m, 8)],
                w_s.at[pl.ds(8 * m, 8)],
                sems.at[m],
            )
            for m in range(3)
        ]
        for copy in copies:
            copy.start()
        for copy in copies:
            copy.wait()

    total = dh1_ref[...]
    for m in range(3):
        grad = jnp.concatenate([da_ref[m], db_ref[m]], axis=1)
        total = total + dot(grad, square(w_s, 8 * m), NT)
    out_ref[...] = total.astype(BF)


def input_grad(wa, dh1, first, second):
    count = dh1.shape[0]
    rows = pl.BlockSpec((NORM_TILE, D), lambda i: (i, 0))
    return pl.pallas_call(
        input_grad_kernel,
        grid=(count // NORM_TILE,),
        in_specs=[ANY, rows] + [pl.BlockSpec((3, NORM_TILE, D // 2), lambda i: (0, i, 0))] * 2,
        out_specs=rows,
        out_shape=jax.ShapeDtypeStruct((count, D), BF),
        scratch_shapes=[
            pltpu.VMEM((24, ATTN_TILES, 16, 128), BF),
            pltpu.SemaphoreType.DMA((3,)),
        ],
        compiler_params=params(),
        cost_estimate=cost(
            flops=6 * count * D * D, bytes_accessed=count * D * 18, transcendentals=0
        ),
        name="input_grad",
    )(wa, dh1, first, second)


def retile(flat, blocks):
    tall = flat.shape[0] // (16 * blocks)
    tiles = flat.reshape(tall, 16, blocks, 128).transpose(0, 2, 1, 3)
    return tiles.reshape(tall * blocks, 16, 128)


def untile(tiles, blocks):
    tall = tiles.shape[0] // blocks
    flat = tiles.reshape(tall, blocks, 16, 128).transpose(0, 2, 1, 3)
    return flat.reshape(tall * blocks * 16, 128)


def pad_vectors(flat):
    return jnp.pad(flat, (0, VEC_ROWS * 128 - flat.shape[0])).reshape(VEC_TILES, 16, 128)


def gather_plain(attn, ffn, vectors):
    attn = lax.all_gather(attn, "fsdp", axis=0, tiled=True)
    ffn = lax.all_gather(ffn, "fsdp", axis=0, tiled=True)
    vec = lax.all_gather(vectors, "fsdp", axis=0, tiled=True)
    half = ffn.shape[0] // 2
    tiles = jnp.concatenate([retile(ffn[:half], 24), retile(ffn[half:], 6)], axis=0)
    attn_tiles = retile(attn, 6).reshape(OWNERS, ATTN_TILES, 16, 128)
    return attn_tiles, tiles.reshape(OWNERS, FFN_TILES, 16, 128), pad_vectors(vec)[None]


class Gather:
    def __init__(self, tiles, vec=None):
        self.own, self.tiles, self.vec = tiles, tiles.shape[0], vec

    def ride(self, message):
        return message if self.vec is None else jnp.concatenate([message, self.vec], axis=0)

    def landed(self, messages, size):
        if self.vec is None:
            return messages
        total = self.vec.astype(F32) + sum(m[size:].astype(F32) for m in messages)
        self.vec = total.astype(BF)
        return [m[:size] for m in messages]

    def planes(self):
        message = self.ride(self.own)
        self.hops = [hop(message, 8 * step) for step in (1, 2, 3)]

    def sides(self):
        self.own = jnp.concatenate([self.own] + self.landed(self.hops, self.tiles), axis=0)
        self.hops = [hop(self.ride(self.own), 2), hop(self.own, 4)]
        self.mirror = [hop(self.own, 1)]

    def corner(self):
        (self.over_x,) = self.landed(self.hops[:1], 4 * self.tiles)
        self.over_y = self.hops[1]
        shape = (4, self.tiles, 16, 128)
        half = self.tiles // 2
        low = self.over_y.reshape(shape)[:, :half].reshape(-1, 16, 128)
        high = self.over_x.reshape(shape)[:, half:].reshape(-1, 16, 128)
        self.hops = [hop(low, 2), hop(self.ride(high), 4)]
        self.mirror += [hop(self.over_x, 1), hop(self.over_y, 1)]

    def pieces(self):
        half = self.tiles // 2
        (high,) = self.landed(self.hops[1:], 4 * half)
        corners = [part.reshape(4, half, 16, 128) for part in (self.hops[0], high)]
        mirror = self.mirror + [hop(part, 1) for part in corners]
        return [self.own, self.over_x, self.over_y] + corners + mirror

    def vectors(self):
        return jnp.stack([self.vec, hop(self.vec, 1)], axis=0)


def hop(value, bit):
    pairs = [(i, i ^ bit) for i in range(OWNERS)]
    return lax.ppermute(value, "fsdp", pairs)


def reduce_plain(ffn_terms, attn_terms, vector_terms):
    def absolute(keep, send):
        planes = keep.shape[1]
        both = jnp.stack([keep, send], axis=1)
        return jnp.moveaxis(both, 2, 0).reshape(planes * 8, -1, 16, 128)

    dw1k, dw1s, dw2k, dw2s = ffn_terms
    up = untile(absolute(dw1k, dw1s).reshape(-1, 16, 128), 24)
    down = untile(absolute(dw2k, dw2s).reshape(-1, 16, 128), 6)
    proj = untile(absolute(*attn_terms).reshape(-1, 16, 128), 6)

    def scatter(value):
        return lax.psum_scatter(value.astype(F32), "fsdp", scatter_dimension=0, tiled=True)

    return scatter(proj), scatter(jnp.concatenate([up, down], axis=0)), scatter(vector_terms)


def get(message, index, tiles):
    if len(message.shape) == 3:
        return message[pl.ds(index * tiles, tiles)].astype(F32)
    return message[index].astype(F32)


def put(message, index, tiles, value):
    if len(message.shape) == 3:
        message[pl.ds(index * tiles, tiles)] = value.astype(message.dtype)
    else:
        message[index] = value.astype(message.dtype)


def take_terms(refs, spots, leaves):
    terms = {}
    for spot in spots:
        planes = []
        for _ in range(leaves):
            keep, other = refs.pop(0), refs.pop(0)
            planes += [(keep, other, p) for p in range(keep.shape[1])]
        terms[spot] = planes

    def term(spot, index):
        keep, other, plane = terms[spot][index]
        return keep[0, plane].astype(F32) + other[0, plane].astype(F32)

    return term, terms[spots[0]][0][0].shape[2]


def take_vec(refs, vec):
    if not vec:
        return None
    state, arrival = refs.pop(0), refs.pop(0)
    return state[...] + arrival[pl.ds(arrival.shape[0] - VEC_TILES, VEC_TILES)].astype(F32)


def put_tail(message, total):
    message[pl.ds(message.shape[0] - VEC_TILES, VEC_TILES)] = total.astype(BF)


def corner_kernel(leaves, vec, *refs):
    refs = list(refs)
    term, tiles = take_terms(refs, [(3, 0), (3, 1), (1, 0), (2, 1)], leaves)
    total = take_vec(refs, vec)
    to_x, to_y = refs[:2]
    for i in range(2):
        put(to_x, i, tiles, term((3, 0), i))
        put(to_x, 2 + i, tiles, term((1, 0), i))
        put(to_y, i, tiles, term((3, 1), i))
        put(to_y, 2 + i, tiles, term((2, 1), i))
    if vec:
        put_tail(to_x, total)
        refs[2][...] = total


def side_kernel(leaves, vec, *refs):
    refs = list(refs)
    term, tiles = take_terms(refs, [(1, 1), (2, 0)], leaves)
    from_x, from_y = refs.pop(0), refs.pop(0)
    total = take_vec(refs, vec)
    to_x, to_y = refs[:2]
    for i in range(2):
        put(to_x, i, tiles, term((1, 1), i) + get(from_y, i, tiles))
        put(to_y, i, tiles, term((2, 0), i) + get(from_x, i, tiles))
    if vec:
        put_tail(to_y, total)
        refs[2][...] = total


def plane_kernel(leaves, vec, me_ref, *refs):
    refs = list(refs)
    term, tiles = take_terms(refs, [(0, 0), (0, 1)], leaves)
    from_x, from_y, from_x_two, from_y_two = (refs.pop(0) for _ in range(4))
    total = take_vec(refs, vec)
    mine, outs, own = refs[0], refs[1:4], refs[-1]
    for i in range(2):
        lower = term((0, 0), i) + get(from_x, 2 + i, tiles) + get(from_y_two, i, tiles)
        upper = term((0, 1), i) + get(from_y, 2 + i, tiles) + get(from_x_two, i, tiles)
        own[2 * i if leaves == 2 else i] = lower
        own[2 * i + 1 if leaves == 2 else 2 + i] = upper
    my_z = me_ref[0] >> 3
    mine[...] = own[my_z]
    for step in range(3):
        if vec:
            outs[step][pl.ds(0, tiles)] = own[my_z ^ (step + 1)].astype(BF)
            put_tail(outs[step], total)
        else:
            outs[step][...] = own[my_z ^ (step + 1)].astype(BF)
    if vec:
        refs[4][...] = total


class Reduction:
    def __init__(self, keeps, sends, me, vec=None):
        self.keeps, self.me, self.vec = keeps, me, vec
        self.hops = [hop(send, 1) for send in sends]
        if vec is not None:
            self.hops.append(hop(vec.astype(BF), 1))
        self.tiles = keeps[0].shape[2]
        self.steps = 3 if vec is None else 1

    def run(self, kernel, spots, arrivals, outs, name, place=False):
        leaves, tiles, block = len(self.keeps), self.tiles, self.tiles // self.steps
        carries = self.vec is not None
        arrays, in_specs = [], []
        for spot, half in spots:
            for keep, other in zip(self.keeps, self.received, strict=True):
                spec = pl.BlockSpec(
                    (1, keep.shape[1] // 2, block, 16, 128),
                    lambda t, *_, spot=spot, half=half: (spot, half, t, 0, 0),
                )
                arrays += [keep, other]
                in_specs += [spec, spec]

        def message_spec(shape):
            if len(shape) == 4:
                return pl.BlockSpec((shape[0], block, 16, 128), lambda t, *_: (0, t, 0, 0))
            if carries:
                return whole(shape)
            return pl.BlockSpec((block, 16, 128), lambda t, *_: (t, 0, 0))

        for array in arrivals:
            arrays.append(array)
            in_specs.append(message_spec(array.shape))
        if carries:
            arrays += [self.vec, self.vec_arrival]
            in_specs += [whole(self.vec.shape), whole(self.vec_arrival.shape)]
        out_shape = []
        for planes, dtype, tail in outs:
            tail = VEC_TILES if tail and carries else 0
            if carries:
                dims = (planes * tiles + tail, 16, 128)
            else:
                dims = (planes, tiles, 16, 128) if planes > 1 else (tiles, 16, 128)
            out_shape.append(jax.ShapeDtypeStruct(dims, dtype))
        out_specs = [message_spec(shape.shape) for shape in out_shape]
        if carries:
            out_shape.append(jax.ShapeDtypeStruct(self.vec.shape, F32))
            out_specs.append(whole(self.vec.shape))
        result = pl.pallas_call(
            functools.partial(kernel, leaves, carries),
            grid_spec=pltpu.PrefetchScalarGridSpec(
                num_scalar_prefetch=1 if place else 0,
                grid=(self.steps,),
                in_specs=in_specs,
                out_specs=out_specs,
                scratch_shapes=[pltpu.VMEM((4, block, 16, 128), F32)] if place else [],
            ),
            out_shape=out_shape,
            compiler_params=params(),
            cost_estimate=cost(flops=0, bytes_accessed=tiles * 4096 * 16, transcendentals=0),
            name=name,
        )(*([self.me] if place else []), *arrays)
        if carries:
            *result, self.vec = result
        return result

    def corner(self):
        self.received = self.hops[: len(self.keeps)]
        self.vec_arrival = self.hops[-1]
        to_x, to_y = self.run(
            corner_kernel, [(3, 0), (3, 1), (1, 0), (2, 1)], [], [(4, BF, True), (4, BF, False)], "corner"
        )
        self.hops = [hop(to_x, 2), hop(to_y, 4)]

    def sides(self):
        self.early = self.hops
        self.vec_arrival = self.hops[0]
        to_x, to_y = self.run(
            side_kernel, [(1, 1), (2, 0)], self.early, [(2, BF, False), (2, BF, True)], "sides"
        )
        self.hops = [hop(to_x, 2), hop(to_y, 4)]

    def planes(self):
        self.vec_arrival = self.hops[1]
        outs = [(1, F32, False)] + [(1, BF, True)] * 3
        self.mine, *messages = self.run(
            plane_kernel, [(0, 0), (0, 1)], self.early + self.hops, outs, "planes", place=True
        )
        self.hops = messages

    def cross(self):
        self.hops = [hop(message, 8 * (i + 1)) for i, message in enumerate(self.hops)]

    def total(self):
        tiles = self.tiles
        if self.vec is not None:
            self.vec = self.vec + sum(other[tiles:].astype(F32) for other in self.hops)
        return self.mine + sum(other[:tiles].astype(F32) for other in self.hops)


def meet(hops, values):
    return lax.optimization_barrier((hops, values))


def tiles_of(array):
    return array.reshape(array.shape[:2] + (-1, 16, 128))


def spans(segments, pad_segment):
    pad = pad_segment[:, None]
    seen = jnp.where(segments == pad, -1, segments)
    first, last = segments[:, ::128], segments[:, 127::128]
    last = jnp.minimum(last, pad - 1)
    below = jnp.sum(segments[:, None, :] < first[:, :, None], axis=2)
    upto = jnp.sum(segments[:, None, :] <= last[:, :, None], axis=2)
    start = below // 128
    count = jnp.where(first == pad, 0, (upto + 127) // 128 - start)
    both = jnp.stack([jnp.where(count == 0, 0, start), count], axis=2)
    return seen, both.reshape(segments.shape[0], 8).astype(jnp.int32)


def layer(tokens, attn_matrices, ffn_matrices, vectors, segments, pad_segment, cotangent, size):
    fast = size == OWNERS
    each = vectors.shape[0]
    place = lax.axis_index("fsdp") if fast else jnp.zeros((), jnp.int32)
    me = place.reshape(1).astype(jnp.int32)
    my_z = place >> 3
    rows = segments.shape[0]
    seen, span = spans(segments, pad_segment)
    segc = seen.reshape(rows * SLOTS, 1)
    segr = seen.reshape(rows, 1, SLOTS)

    if fast:
        lower = place < OWNERS // 2
        flat = jnp.zeros((VEC_ROWS * 128,), BF)
        mine = lax.dynamic_update_slice(flat, vectors, (place * each,)).reshape(VEC_TILES, 16, 128)
        attn_in = Gather(retile(attn_matrices, 6), mine)
        ffn_in = Gather(jnp.where(lower, retile(ffn_matrices, 24), retile(ffn_matrices, 6)))
        attn_in.planes()
        attn_in.hops, (ffn_in.own, segc, segr, span) = meet(
            attn_in.hops, (ffn_in.own, segc, segr, span)
        )
        ffn_in.planes()
        attn_in.sides()
        attn_in.hops, ffn_in.hops[:2] = meet(attn_in.hops, ffn_in.hops[:2])
        attn_in.corner()
        pieces, vecs = attn_in.pieces(), attn_in.vectors()
        ffn_in.hops, pieces = meet(ffn_in.hops, pieces)
        ffn_in.sides()
    else:
        gathered, ffn_tiles, vecs = gather_plain(attn_matrices, ffn_matrices, vectors)
        pieces = [gathered]
    query, key, value, ctx, lse, wa, vec = attn_fwd(
        fast, me, span, pieces, vecs, tokens, segc, segr
    )
    if fast:
        ffn_in.hops, (ctx, wa, vec) = meet(ffn_in.hops, (ctx, wa, vec))
        ffn_in.corner()
    n1, rstd = norm_fwd(wa, ctx, tokens, vec)
    if fast:
        ffn_in.hops, (n1, rstd) = meet(ffn_in.hops, (n1, rstd))
        ffn_pieces = ffn_in.pieces()
    else:
        ffn_pieces = [ffn_tiles]
    out, dw1k, dw1s, dw2k, dw2s, vg, dh1, da, dctx = ffn_layer(
        fast, me, ffn_pieces, wa, n1, rstd, cotangent, segc, vec
    )
    if not fast:
        first = attn_bwd(span, query, key, value, ctx, dctx, lse, segc, segr, 0, 3)
        second = attn_bwd(span, query, key, value, ctx, dctx, lse, segc, segr, 3, 3)
        dwk, dws, vg = proj_grad(me, tokens, ctx, first, second, da, vg)
        dx = input_grad(wa, dh1, first, second)
        vector_terms = vg.reshape(-1)[: 12 * D]
        return (out, dx) + reduce_plain((dw1k, dw1s, dw2k, dw2s), (dwk, dws), vector_terms)

    ffn = Reduction([tiles_of(dw1k), tiles_of(dw2k)], [tiles_of(dw1s), tiles_of(dw2s)], me)
    first = attn_bwd(span, query, key, value, ctx, dctx, lse, segc, segr, 0, 3)
    ffn.hops, (first, dctx) = meet(ffn.hops, (first, dctx))
    ffn.corner()
    second = attn_bwd(span, query, key, value, ctx, dctx, lse, segc, segr, 3, 3)
    dwk, dws, vg = proj_grad(me, tokens, ctx, first, second, da, vg)
    ffn.hops, (dwk, dws, vg, first) = meet(ffn.hops, (dwk, dws, vg, first))
    ffn.sides()
    attn = Reduction([tiles_of(dwk)], [tiles_of(dws)], me, vg.reshape(VEC_TILES, 16, 128))
    dx = input_grad(wa, dh1, first, second)
    (ffn.hops, attn.hops), dx = meet((ffn.hops, attn.hops), dx)
    ffn.planes()
    ffn.hops, attn.hops = meet(ffn.hops, attn.hops)
    ffn.cross()
    attn.corner()
    ffn.hops[:2], attn.hops = meet(ffn.hops[:2], attn.hops)
    attn.sides()
    ffn.hops[2:], attn.hops = meet(ffn.hops[2:], attn.hops)
    attn.planes()
    attn.cross()
    ffn.hops, attn.hops = meet(ffn.hops, attn.hops)

    ffn_sum = ffn.total()
    ffn_grad = jnp.where(lower, untile(ffn_sum, 24), untile(ffn_sum, 6))
    attn_grad = untile(attn.total(), 6)
    vector_grad = lax.dynamic_slice(attn.vec.reshape(-1), (place * each,), (each,))
    return out, dx, attn_grad, ffn_grad, vector_grad


def solution(mesh):
    size = mesh.shape["fsdp"]
    return jax.shard_map(
        functools.partial(layer, size=size),
        mesh=mesh,
        in_specs=(
            P("fsdp", None),
            P("fsdp", None),
            P("fsdp", None),
            P("fsdp"),
            P("fsdp", None),
            P("fsdp"),
            P("fsdp", None),
        ),
        out_specs=(P("fsdp", None), P("fsdp", None), P("fsdp", None), P("fsdp", None), P("fsdp")),
        check_vma=False,
    )
```

```python
import functools

import jax
import jax.numpy as jnp
from jax import lax
from jax.experimental import pallas as pl
from jax.experimental.pallas import tpu as pltpu
from jax.sharding import PartitionSpec as P

D = 768
FF = 3072
SLOTS = 512
BF = jnp.bfloat16
F32 = jnp.float32
NN = ((1,), (0,))
NT = ((1,), (1,))
TN = ((0,), (0,))
OWNERS = 32
ATTN_TILES = 36
FFN_TILES = 72
COST_SCALE = 1
VMEM_LIMIT = 64 * 1024 * 1024

TAIL_SLOPE = 0.39 * 0.5**0.5
TAIL_POLY = (
    0.11766260955586648,
    0.04569420719462487,
    0.32477969950633645,
    -0.3177001395785759,
    0.44333218507090993,
    -0.11376856259852677,
)


def dot(left, right, dims):
    return lax.dot_general(left, right, (dims, ((), ())), preferred_element_type=F32)


def params(**kwargs):
    return pltpu.CompilerParams(vmem_limit_bytes=VMEM_LIMIT, **kwargs)


def cost(flops, bytes_accessed, transcendentals):
    return pl.CostEstimate(
        flops=flops // COST_SCALE,
        bytes_accessed=bytes_accessed // COST_SCALE,
        transcendentals=transcendentals // COST_SCALE,
    )


def whole(shape):
    zeros = (0,) * len(shape)
    return pl.BlockSpec(shape, lambda *_: zeros)


ANY = pl.BlockSpec(memory_space=pl.ANY)
VEC_TILES = 5
VEC_ROWS = 16 * VEC_TILES


def row(vec_ref, index, width=D):
    blocks = width // 128
    return jnp.concatenate([vec_ref[pl.ds(6 * index + i, 1), :] for i in range(blocks)], axis=1)


def put_row(vec_ref, index, value, first=0):
    for i in range(value.shape[1] // 128):
        vec_ref[pl.ds(6 * index + first + i, 1), :] = value[:, 128 * i : 128 * i + 128]


def square_cols(tiles, first, col):
    parts = [tiles[pl.ds(first, 8), i * 6 + col] for i in range(6)]
    return jnp.stack(parts, axis=1).reshape(D, 128)


def square(tiles, first):
    return jnp.concatenate([square_cols(tiles, first, col) for col in range(6)], axis=1)


def up_col(tiles, col):
    parts = [tiles[pl.ds(0, 16), i * 24 + col] for i in range(3)]
    return jnp.stack(parts, axis=1).reshape(D, 128)


def up_chunk(tiles, chunk):
    return jnp.concatenate([up_col(tiles, chunk * 6 + col) for col in range(6)], axis=1)


def down_chunk(tiles, chunk):
    cols = []
    for col in range(6):
        parts = [tiles[pl.ds(16 + 4 * chunk, 4), i * 6 + col] for i in range(12)]
        cols.append(jnp.stack(parts, axis=1).reshape(D, 128))
    return jnp.concatenate(cols, axis=1)


def piece_count(parts):
    return 2 * (3 * parts + 2)


def piece_copies(me, refs, tiles, parts, w_s):
    yxc, my_z = me & 7, me >> 3
    planes = []
    for step in range(4):
        copies = []
        for core in range(2):
            arrays = refs[core * (3 * parts + 2) :]
            for side in range(4):
                if side == 3:
                    source, index = arrays[3 * parts + step // 2], step % 2
                elif parts == 2 and step == 3:
                    source, index = arrays[2 * side + 1], 0
                else:
                    source, index = arrays[parts * side], step
                owner = 8 * (my_z ^ step) + (yxc ^ (2 * side + core))
                copies.append((source.at[pl.ds(index * tiles, tiles)], w_s.at[owner]))
        planes.append(copies)
    return planes


def attn_copies(fast, me, refs, w_s, sems):
    if not fast:
        return [pltpu.make_async_copy(refs[0], w_s, sems.at[0])]
    planes = piece_copies(me, refs, ATTN_TILES, 1, w_s)
    copies = [copy for plane in planes for copy in plane]
    return [pltpu.make_async_copy(src, dst, sems.at[i]) for i, (src, dst) in enumerate(copies)]


def attn_fwd_kernel(fast, me_ref, span_ref, *args):
    count = piece_count(1) if fast else 1
    refs = args[:count]
    (
        vec_ref, x_ref, segc_ref, segr_ref,
        q_ref, k_ref, v_ref, ctx_ref, lse_ref, wa_ref, vec_out_ref,
        w_s, vt_s, sems, out_sem,
    ) = args[count:]
    line, col = pl.program_id(0), pl.program_id(1)
    first_step = (line == 0) & (col == 0)
    last_step = (line == pl.num_programs(0) - 1) & (col == pl.num_programs(1) - 1)
    out_copy = pltpu.make_async_copy(w_s, wa_ref, out_sem)

    @pl.when(first_step)
    def _():
        copies = attn_copies(fast, me_ref[0], refs, w_s, sems)
        for copy in copies:
            copy.start()
        vec = vec_ref[0].astype(F32)
        for i in range(1, vec_ref.shape[0]):
            vec = vec + vec_ref[i].astype(F32)
        vec_out_ref[...] = vec.reshape(VEC_ROWS, 128)
        for copy in copies:
            copy.wait()
        out_copy.start()

    @pl.when(last_step)
    def _():
        out_copy.wait()

    cols = [2 * col, 2 * col + 1]
    weight = jnp.concatenate([square_cols(w_s, 8 * m, c) for m in range(3) for c in cols], axis=1)
    qkv = dot(x_ref[...], weight, NN)
    bias_q = jnp.concatenate([vec_out_ref[pl.ds(c, 1), :] for c in cols], axis=1)
    bias_v = jnp.concatenate([vec_out_ref[pl.ds(6 + c, 1), :] for c in cols], axis=1)
    q_ref[...] = (qkv[:, :256] + bias_q).astype(BF) * 0.125
    k_ref[...] = qkv[:, 256:512].astype(BF)
    v_ref[...] = (qkv[:, 512:] + bias_v).astype(BF)
    lane = lax.broadcasted_iota(jnp.int32, (1, 128), 1)
    low = lane < 64
    zero = jnp.zeros((), BF)

    for pair in range(2):
        vt_s[pl.ds(128 * pair, 128), :] = v_ref[:, 128 * pair : 128 * pair + 128].T

    def attend(block, carry):
        rows = pl.ds(pl.multiple_of(block * 128, 128), 128)
        start, count = span_ref[line, 2 * block], span_ref[line, 2 * block + 1]

        @pl.when(count == 0)
        def _():
            ctx_ref[rows, :] = jnp.zeros((128, 256), BF)
            lse_ref[:, rows] = jnp.zeros((4, 128), F32)

        def window(size):
            @pl.when(count == size)
            def _():
                seen = pl.ds(pl.multiple_of(start * 128, 128), 128 * size)
                seg_row = segr_ref[:, rows]
                blocked = jnp.where(segc_ref[seen, :] == seg_row, 0.0, -1e30)
                keep = jnp.where(jnp.broadcast_to(seg_row, (64, 128)) < 0, 0.0, 1.0)
                scores = []
                for head in range(4):
                    lanes = slice(128 * (head // 2), 128 * (head // 2) + 128)
                    query = q_ref[rows, lanes]
                    query = jnp.where(low, query, zero) if head % 2 == 0 else jnp.where(low, zero, query)
                    scores.append(dot(k_ref[seen, lanes], query, NT) + blocked)
                tops = [jnp.max(score, axis=0, keepdims=True) for score in scores]
                expds = [jnp.exp(score - top) for score, top in zip(scores, tops)]
                totals = [jnp.sum(expd, axis=0, keepdims=True) for expd in expds]
                outs = []
                for head in range(4):
                    values = vt_s[pl.ds(64 * head, 64), seen]
                    out = dot(values, expds[head].astype(BF), NN)
                    outs.append(out * (1.0 / totals[head]) * keep)
                    lse_ref[pl.ds(head, 1), rows] = tops[head] + jnp.log(totals[head])
                ctx_ref[rows, :] = jnp.concatenate(outs, axis=0).T.astype(BF)

        for size in range(1, 5):
            window(size)
        return carry

    lax.fori_loop(0, 4, attend, 0)


def attn_fwd(fast, me, span, pieces, vec, tokens, segc, segr):
    count = tokens.shape[0]
    rows = count // SLOTS
    part = pl.BlockSpec((SLOTS, 256), lambda r, j, m, s: (r, j))
    slot = pl.BlockSpec((SLOTS, 1), lambda r, j, m, s: (r, 0))
    shape = jax.ShapeDtypeStruct
    return pl.pallas_call(
        functools.partial(attn_fwd_kernel, fast),
        grid_spec=pltpu.PrefetchScalarGridSpec(
            num_scalar_prefetch=2,
            grid=(rows, 3),
            in_specs=[ANY] * len(pieces)
            + [
                whole(vec.shape),
                pl.BlockSpec((SLOTS, D), lambda r, j, m, s: (r, 0)),
                slot,
                pl.BlockSpec((None, 1, SLOTS), lambda r, j, m, s: (r, 0, 0)),
            ],
            out_specs=[part] * 4
            + [pl.BlockSpec((None, None, 4, SLOTS), lambda r, j, m, s: (r, j, 0, 0)), ANY, whole((VEC_ROWS, 128))],
            scratch_shapes=[
                pltpu.VMEM((OWNERS, ATTN_TILES, 16, 128), BF),
                pltpu.VMEM((256, SLOTS), BF),
                pltpu.SemaphoreType.DMA((160,)),
                pltpu.SemaphoreType.DMA,
            ],
        ),
        out_shape=[shape((count, D), BF)] * 4
        + [
            shape((rows, 3, 4, SLOTS), F32),
            shape((OWNERS, ATTN_TILES, 16, 128), BF),
            shape((VEC_ROWS, 128), F32),
        ],
        compiler_params=params(),
        cost_estimate=cost(
            flops=2 * count * D * (3 * D + 4 * SLOTS), bytes_accessed=count * D * 12, transcendentals=count * SLOTS * 12
        ),
        name="attn_fwd",
    )(me, span, *pieces, vec, tokens, segc, segr)


def norm_parts(hidden):
    mean = jnp.mean(hidden, axis=1, keepdims=True)
    centered = hidden - mean
    var = jnp.mean(centered * centered, axis=1, keepdims=True)
    rstd = lax.rsqrt(var + 1e-12)
    return centered * rstd, rstd


def gelu_parts(u):
    size = jnp.abs(u)
    t = pl.reciprocal(1.0 + TAIL_SLOPE * size)
    poly = jnp.full_like(t, TAIL_POLY[-1])
    for coef in TAIL_POLY[-2::-1]:
        poly = poly * t + coef
    bell = jnp.exp(u * u * -0.5)
    tail = poly * t * bell
    phi_cdf = jnp.where(u > 0, 1.0 - tail, tail)
    return u * phi_cdf, phi_cdf + u * bell * 0.3989422804014327


NORM_TILE = 256


def norm_fwd_kernel(wa_ref, ctx_ref, x_ref, vec_ref, n1_ref, rstd_ref, wo_s, sem):
    copy = pltpu.make_async_copy(wa_ref.at[pl.ds(24, 8)], wo_s, sem)

    @pl.when(pl.program_id(0) == 0)
    def _():
        copy.start()
        copy.wait()

    hidden = x_ref[...].astype(F32) + dot(ctx_ref[...], square(wo_s, 0), NN) + row(vec_ref, 2)
    normed, rstd = norm_parts(hidden)
    n1_ref[...] = normed
    rstd_ref[...] = jnp.broadcast_to(rstd, rstd_ref.shape)


def norm_fwd(wa, ctx, tokens, vec):
    count = tokens.shape[0]
    rows = pl.BlockSpec((NORM_TILE, D), lambda i: (i, 0))
    slim = pl.BlockSpec((NORM_TILE, 128), lambda i: (i, 0))
    shape = jax.ShapeDtypeStruct
    return pl.pallas_call(
        norm_fwd_kernel,
        grid=(count // NORM_TILE,),
        in_specs=[ANY, rows, rows, whole((VEC_ROWS, 128))],
        out_specs=[rows, slim],
        out_shape=[shape((count, D), F32), shape((count, 128), F32)],
        scratch_shapes=[pltpu.VMEM((8, ATTN_TILES, 16, 128), BF), pltpu.SemaphoreType.DMA],
        compiler_params=params(),
        cost_estimate=cost(
            flops=2 * count * D * D, bytes_accessed=count * D * 9, transcendentals=0
        ),
        name="norm_fwd",
    )(wa, ctx, tokens, vec)


def ffn_copies(fast, me, refs, w_s, sems):
    if not fast:
        pairs = [[(refs[0].at[pl.ds(16 * m, 16)], w_s.at[pl.ds(16 * m, 16)])] for m in range(2)]
    else:
        planes = piece_copies(me, refs, FFN_TILES, 1, w_s)
        pairs = [planes[0] + planes[1], planes[2] + planes[3]]
    return [
        [pltpu.make_async_copy(src, dst, sems.at[m, i]) for i, (src, dst) in enumerate(group)]
        for m, group in enumerate(pairs)
    ]


MID_TILE = 1024


def pick(mine, even, odd):
    return jnp.where(mine == 0, even, odd), jnp.where(mine == 0, odd, even)


def norm_grad(normed, rstd, t):
    mean_t = jnp.mean(t, axis=1, keepdims=True)
    mean_tn = jnp.mean(t * normed, axis=1, keepdims=True)
    return (t - mean_t - normed * mean_tn) * rstd


def column_sum(value):
    return jnp.sum(value.astype(F32), axis=0, keepdims=True)


def ffn_kernel(fast, me_ref, *args):
    pieces = piece_count(1) if fast else 1
    (
        wa_ref, n1_ref, rstd_ref, cot_ref, seg_ref, vec_ref,
        out_ref, dw1k_ref, dw1s_ref, dw2k_ref, dw2s_ref, vg_ref, dh1_ref, da_ref, dctx_ref,
        w_s, wo_s, g_s, gp_s, yb_s, ybt_s, dz_s, du_s, r_s, ua_s, ub_s, sems, wo_sem,
    ) = args[pieces:]
    step = pl.program_id(0)
    me = me_ref[0]
    core, my_x, my_y = me & 1, (me >> 1) & 1, (me >> 2) & 1
    copies = ffn_copies(fast, me, args[:pieces], w_s, sems)
    holds_up = me < OWNERS // 2
    wo_copy = pltpu.make_async_copy(wa_ref.at[pl.ds(24, 8)], wo_s, wo_sem)
    count = n1_ref.shape[0]

    def tile(i, size):
        return pl.ds(pl.multiple_of(i * size, size), size)

    def wait_for(matrix):
        for group in range(2):

            @pl.when(holds_up == (group == matrix))
            def _(group=group):
                for copy in copies[group]:
                    copy.wait()

    @pl.when(step == 0)
    def _():
        for group in copies:
            for copy in group:
                copy.start()
        wo_copy.start()

        def body(i, carry):
            rows = tile(i, NORM_TILE)
            y_one = n1_ref[rows, :] * row(vec_ref, 3) + row(vec_ref, 4)
            yb_s[rows, :] = y_one.astype(BF)
            dh1_ref[rows, :] = y_one + row(vec_ref, 9)
            return carry

        lax.fori_loop(0, count // NORM_TILE, body, 0)
        ybt_s[...] = yb_s[...].T
        wait_for(0)

    @pl.when(step == 0)
    def _():
        def weights_of(sub):
            weight = jnp.concatenate([up_col(w_s, 2 * sub + i) for i in range(2)], axis=1)
            bias = jnp.concatenate([vec_ref[pl.ds(30 + 2 * sub + i, 1), :] for i in range(2)], axis=1)
            return weight, bias

        def advance(new_ref, new_sub, old_ref, old_sub):
            weight, bias = weights_of(new_sub)
            chunk = lax.div(old_sub, 3)
            lanes = tile(old_sub - 3 * chunk, 256)
            for first in range(0, count, 128):
                rows = slice(first, first + 128)
                new_ref[rows, :] = dot(yb_s[rows, :], weight, NN) + bias
                act, slope = gelu_parts(old_ref[rows, :])
                g_s[chunk, rows, lanes] = act.astype(BF)
                gp_s[chunk, rows, lanes] = slope.astype(BF)

        weight, bias = weights_of(0)
        ua_s[...] = dot(yb_s[...], weight, NN) + bias

        def widen(i, carry):
            advance(ub_s, 2 * i + 1, ua_s, 2 * i)
            advance(ua_s, jnp.minimum(2 * i + 2, 11), ub_s, 2 * i + 1)
            return carry

        lax.fori_loop(0, 6, widen, 0)
        wait_for(1)

        def narrow(i, carry):
            rows = tile(i, MID_TILE)
            total = dh1_ref[rows, :]
            for chunk in range(4):
                total = total + dot(g_s[chunk, rows, :], down_chunk(w_s, chunk), NN)
            dh1_ref[rows, :] = total
            return carry

        lax.fori_loop(0, count // MID_TILE, narrow, 0)

    @pl.when(step == 0)
    def _():
        def body(i, sums):
            rows = tile(i, NORM_TILE)
            normed, rstd = norm_parts(dh1_ref[rows, :])
            gain = row(vec_ref, 10)
            out_ref[rows, :] = (normed * gain + row(vec_ref, 11)).astype(BF)
            err = cot_ref[rows, :].astype(F32)
            dh2 = norm_grad(normed, rstd, gain * err)
            dz = dh2.astype(BF)
            dh1_ref[rows, :] = dh2
            dz_s[rows, :] = dz
            return (
                sums[0] + column_sum(dz),
                sums[1] + column_sum(err * normed),
                sums[2] + column_sum(err),
            )

        zero = jnp.zeros((1, D), F32)
        sums = lax.fori_loop(0, count // NORM_TILE, body, (zero, zero, zero))
        vg_ref[...] = jnp.zeros_like(vg_ref)
        for i in range(3):
            put_row(vg_ref, 9 + i, sums[i])

    @pl.when(step >= 1)
    def _():
        chunk = step - 1

        def back(i, total):
            rows = tile(i, MID_TILE)
            dg = dot(dz_s[rows, :], down_chunk(w_s, chunk), NT)
            du = (gp_s[chunk, rows, :].astype(F32) * dg).astype(BF)
            du_s[rows, :] = du
            dh1_ref[rows, :] += dot(du, up_chunk(w_s, chunk), NT)
            return total + column_sum(du)

        put_row(vg_ref, 5 + chunk, lax.fori_loop(0, count // MID_TILE, back, jnp.zeros((1, D), F32)))

        def weights(half, carry):
            lanes = tile(half, 384)
            r_s[...] = dot(ybt_s[lanes, :], du_s[...], NN).astype(BF)
            for pair in range(4):
                even, odd = r_s[pl.ds(pair * 96, 48), :], r_s[pl.ds(pair * 96 + 48, 48), :]
                keep, send = pick(core, even, odd)
                place = (((pair >> 1) ^ my_y) << 1) | ((pair & 1) ^ my_x)
                for col in range(6):
                    spot = slice(col * 128, col * 128 + 128)
                    dw1k_ref[place, half, :, col] = keep[:, spot].reshape(3, 16, 128)
                    dw1s_ref[place, half, :, col] = send[:, spot].reshape(3, 16, 128)
            r_s[...] = dot(g_s[chunk, :, lanes], dz_s[...], TN).astype(BF)
            keep, send = pick(core, r_s[:192, :], r_s[192:, :])
            for col in range(6):
                spot = slice(col * 128, col * 128 + 128)
                dw2k_ref[half ^ my_x, 0, :, col] = keep[:, spot].reshape(12, 16, 128)
                dw2s_ref[half ^ my_x, 0, :, col] = send[:, spot].reshape(12, 16, 128)
            return carry

        lax.fori_loop(0, 2, weights, 0)

    @pl.when(step == 4)
    def _():
        wo_copy.wait()

        def body(i, sums):
            rows = tile(i, NORM_TILE)
            dy1, normed = dh1_ref[rows, :], n1_ref[rows, :]
            dh1 = norm_grad(normed, rstd_ref[rows, 0:1], dy1 * row(vec_ref, 3))
            da = dh1.astype(BF)
            dh1_ref[rows, :] = dh1
            da_ref[rows, :] = da
            back = dot(da, square(wo_s, 0), NT)
            dctx_ref[rows, :] = jnp.where(seg_ref[rows, :] >= 0, back, 0.0).astype(BF)
            return (
                sums[0] + column_sum(da),
                sums[1] + column_sum(dy1 * normed),
                sums[2] + column_sum(dy1),
            )

        zero = jnp.zeros((1, D), F32)
        sums = lax.fori_loop(0, count // NORM_TILE, body, (zero, zero, zero))
        for i in range(3):
            put_row(vg_ref, 2 + i, sums[i])


def ffn_layer(fast, me, pieces, wa, n1, rstd, cotangent, segc, vec):
    count = n1.shape[0]
    once = pl.Buffered(1)

    def single(shape):
        zeros = (0,) * len(shape)
        return pl.BlockSpec(shape, lambda *_: zeros, pipeline_mode=once)

    full = whole((count, D))
    up = pl.BlockSpec(
        (4, 2, 3, 6, 16, 128), lambda s, m: (0, 0, 0, jnp.maximum(s - 1, 0), 0, 0)
    )

    def down_index(s, m):
        chunk = jnp.maximum(s - 1, 0)
        return ((chunk % 2) ^ ((m[0] >> 2) & 1), chunk // 2, 0, 0, 0, 0)

    down = pl.BlockSpec((2, 1, 12, 6, 16, 128), down_index)
    shape = jax.ShapeDtypeStruct
    return pl.pallas_call(
        functools.partial(ffn_kernel, fast),
        grid_spec=pltpu.PrefetchScalarGridSpec(
            num_scalar_prefetch=1,
            grid=(5,),
            in_specs=[ANY] * len(pieces)
            + [
                ANY,
                single((count, D)),
                single((count, 128)),
                single((count, D)),
                single((count, 1)),
                single((VEC_ROWS, 128)),
            ],
            out_specs=[full, up, up, down, down, whole((VEC_ROWS, 128)), full, full, full],
            scratch_shapes=[
                pltpu.VMEM((OWNERS, FFN_TILES, 16, 128), BF),
                pltpu.VMEM((8, ATTN_TILES, 16, 128), BF),
                pltpu.VMEM((4, count, D), BF),
                pltpu.VMEM((4, count, D), BF),
                pltpu.VMEM((count, D), BF),
                pltpu.VMEM((D, count), BF),
                pltpu.VMEM((count, D), BF),
                pltpu.VMEM((count, D), BF),
                pltpu.VMEM((D // 2, D), BF),
                pltpu.VMEM((count, 256), F32),
                pltpu.VMEM((count, 256), F32),
                pltpu.SemaphoreType.DMA((2, 40)),
                pltpu.SemaphoreType.DMA,
            ],
        ),
        out_shape=[shape((count, D), BF)]
        + [shape((4, 2, 3, 24, 16, 128), BF)] * 2
        + [shape((4, 2, 12, 6, 16, 128), BF)] * 2
        + [shape((VEC_ROWS, 128), F32), shape((count, D), F32)]
        + [shape((count, D), BF)] * 2,
        compiler_params=params(),
        cost_estimate=cost(
            flops=12 * count * D * FF, bytes_accessed=count * D * 30, transcendentals=count * FF
        ),
        name="ffn_layer",
    )(me, *pieces, wa, n1, rstd, cotangent, segc, vec)


def attn_bwd_kernel(
    first, span_ref, q_ref, k_ref, v_ref, ctx_ref, dctx_ref, lse_ref, segc_ref, segr_ref, d_ref, dqt_s, dots_s
):
    line = pl.program_id(0)
    pairs = q_ref.shape[1] // 128
    lane = lax.broadcasted_iota(jnp.int32, (1, 128), 1)
    low = lane < 64
    zero = jnp.zeros((), BF)
    spots = [slice(128 * pair, 128 * pair + 128) for pair in range(pairs)]
    for pair, lanes in enumerate(spots):
        products = (dctx_ref[:, lanes].astype(F32) * ctx_ref[:, lanes].astype(F32)).T
        for head in range(2):
            place = slice(4 * pair + head, 4 * pair + head + 1)
            dots_s[place, :] = jnp.sum(products[64 * head : 64 * head + 64], axis=0, keepdims=True)
            index = 2 * (first + pair) + head
            place = slice(4 * pair + 2 + head, 4 * pair + 3 + head)
            dots_s[place, :] = lse_ref[index // 4, index % 4 : index % 4 + 1, :]
    dqt_s[...] = jnp.zeros_like(dqt_s)

    def both(value):
        return jnp.concatenate([jnp.where(low, value, zero), jnp.where(low, zero, value)], axis=0)

    def block_step(block, carry):
        rows = pl.ds(pl.multiple_of(block * 128, 128), 128)
        start, count = span_ref[line, 2 * block], span_ref[line, 2 * block + 1]

        @pl.when(count == 0)
        def _():
            d_ref[1, rows, :] = jnp.zeros((128, 128 * pairs), BF)
            d_ref[2, rows, :] = jnp.zeros((128, 128 * pairs), BF)

        def window(size):
            @pl.when(count == size)
            def _():
                seen = pl.ds(pl.multiple_of(start * 128, 128), 128 * size)
                seg_row = segr_ref[:, seen]
                allowed = segc_ref[rows, :] == jnp.where(seg_row < 0, -2, seg_row)
                allowed = jnp.concatenate([allowed, allowed], axis=0)

                def spread(pair, offset):
                    lines = [dots_s[4 * pair + offset + h : 4 * pair + offset + h + 1, seen] for h in range(2)]
                    return jnp.concatenate([jnp.broadcast_to(r, (128, 128 * size)) for r in lines], axis=0)

                keys = [both(k_ref[rows, lanes]) for lanes in spots]
                queries = [q_ref[seen, lanes] for lanes in spots]
                dctxs = [dctx_ref[seen, lanes] for lanes in spots]
                scores = [dot(k, q, NT) for k, q in zip(keys, queries)]
                dprobs = [dot(both(v_ref[rows, lanes]), dctx, NT) for lanes, dctx in zip(spots, dctxs)]
                probs = [
                    jnp.where(allowed, jnp.exp(score - spread(pair, 2)), 0.0)
                    for pair, score in enumerate(scores)
                ]
                dscores = [
                    (prob * (dprob - spread(pair, 0))).astype(BF)
                    for pair, (prob, dprob) in enumerate(zip(probs, dprobs))
                ]
                dvs = [dot(prob.astype(BF), dctx, NN) for prob, dctx in zip(probs, dctxs)]
                dks = [dot(dscore, query, NN) for dscore, query in zip(dscores, queries)]
                dqs = [dot(key, dscore, TN) for key, dscore in zip(keys, dscores)]
                for pair, lanes in enumerate(spots):
                    dqt_s[lanes, seen] += dqs[pair]
                    d_ref[1, rows, lanes] = jnp.where(low, dks[pair][:128], dks[pair][128:]).astype(BF)
                    d_ref[2, rows, lanes] = jnp.where(low, dvs[pair][:128], dvs[pair][128:]).astype(BF)

        for size in range(1, 5):
            window(size)
        return carry

    lax.fori_loop(0, 4, block_step, 0)
    d_ref[0] = (dqt_s[...].T * 0.125).astype(BF)


def attn_bwd(span, query, key, value, ctx, dctx, lse, segc, segr, first, cols):
    count = query.shape[0]
    rows = count // SLOTS
    width = 128 * cols
    part = pl.BlockSpec((SLOTS, width), lambda r, s: (r, first // cols))
    return pl.pallas_call(
        functools.partial(attn_bwd_kernel, first),
        grid_spec=pltpu.PrefetchScalarGridSpec(
            num_scalar_prefetch=1,
            grid=(rows,),
            in_specs=[part] * 5
            + [
                pl.BlockSpec((None, 3, 4, SLOTS), lambda r, s: (r, 0, 0, 0)),
                pl.BlockSpec((SLOTS, 1), lambda r, s: (r, 0)),
                pl.BlockSpec((None, 1, SLOTS), lambda r, s: (r, 0, 0)),
            ],
            out_specs=pl.BlockSpec((3, SLOTS, width), lambda r, s: (0, r, 0)),
            scratch_shapes=[pltpu.VMEM((width, SLOTS), F32), pltpu.VMEM((4 * cols, SLOTS), F32)],
        ),
        out_shape=jax.ShapeDtypeStruct((3, count, width), BF),
        compiler_params=params(),
        cost_estimate=cost(
            flops=10 * count * D * SLOTS, bytes_accessed=count * D * 16, transcendentals=count * SLOTS * 12
        ),
        name="attn_bwd",
    )(span, query, key, value, ctx, dctx, lse, segc, segr)


def proj_grad_kernel(me_ref, x_ref, ctx_ref, first_ref, second_ref, da_ref, vg_in_ref, dwk_ref, dws_ref, vg_ref, r_s):
    step = pl.program_id(0)
    me = me_ref[0]
    core, my_x, my_y = me & 1, (me >> 1) & 1, (me >> 2) & 1

    @pl.when(step == 0)
    def _():
        vg_ref[...] = vg_in_ref[...]

    @pl.when(step < 3)
    def _():
        grad = jnp.concatenate([first_ref[...], second_ref[...]], axis=1)
        r_s[...] = dot(x_ref[...], grad, TN).astype(BF)

        @pl.when(step != 1)
        def _():
            put_row(vg_ref, step >> 1, column_sum(grad))

    @pl.when(step == 3)
    def _():
        r_s[...] = dot(ctx_ref[...], da_ref[...], TN).astype(BF)

    for pair in range(4):
        even, odd = r_s[pl.ds(pair * 192, 96), :], r_s[pl.ds(pair * 192 + 96, 96), :]
        keep, send = pick(core, even, odd)
        place = (((pair >> 1) ^ my_y) << 1) | ((pair & 1) ^ my_x)
        for col in range(6):
            lanes = slice(col * 128, col * 128 + 128)
            dwk_ref[place, 0, :, col] = keep[:, lanes].reshape(6, 16, 128)
            dws_ref[place, 0, :, col] = send[:, lanes].reshape(6, 16, 128)


def proj_grad(me, tokens, ctx, first, second, da, vg):
    count, width = first.shape[1:]
    out = pl.BlockSpec((4, 1, 6, 6, 16, 128), lambda i, m: (0, i, 0, 0, 0, 0))
    full = whole((count, D))
    part = pl.BlockSpec((None, count, width), lambda i, m: (jnp.minimum(i, 2), 0, 0))
    shape = jax.ShapeDtypeStruct
    return pl.pallas_call(
        proj_grad_kernel,
        grid_spec=pltpu.PrefetchScalarGridSpec(
            num_scalar_prefetch=1,
            grid=(4,),
            in_specs=[full, full, part, part, full, whole((VEC_ROWS, 128))],
            out_specs=[out, out, whole((VEC_ROWS, 128))],
            scratch_shapes=[pltpu.VMEM((D, D), BF)],
        ),
        out_shape=[shape((4, 4, 6, 6, 16, 128), BF)] * 2 + [shape((VEC_ROWS, 128), F32)],
        compiler_params=params(),
        cost_estimate=cost(
            flops=8 * count * D * D, bytes_accessed=count * D * 20, transcendentals=0
        ),
        name="proj_grad",
    )(me, tokens, ctx, first, second, da, vg)


def input_grad_kernel(wa_ref, dh1_ref, da_ref, db_ref, out_ref, w_s, sems):
    @pl.when(pl.program_id(0) == 0)
    def _():
        copies = [
            pltpu.make_async_copy(
                wa_ref.at[pl.ds(8 * m, 8)],
                w_s.at[pl.ds(8 * m, 8)],
                sems.at[m],
            )
            for m in range(3)
        ]
        for copy in copies:
            copy.start()
        for copy in copies:
            copy.wait()

    total = dh1_ref[...]
    for m in range(3):
        grad = jnp.concatenate([da_ref[m], db_ref[m]], axis=1)
        total = total + dot(grad, square(w_s, 8 * m), NT)
    out_ref[...] = total.astype(BF)


def input_grad(wa, dh1, first, second):
    count = dh1.shape[0]
    rows = pl.BlockSpec((NORM_TILE, D), lambda i: (i, 0))
    return pl.pallas_call(
        input_grad_kernel,
        grid=(count // NORM_TILE,),
        in_specs=[ANY, rows] + [pl.BlockSpec((3, NORM_TILE, D // 2), lambda i: (0, i, 0))] * 2,
        out_specs=rows,
        out_shape=jax.ShapeDtypeStruct((count, D), BF),
        scratch_shapes=[
            pltpu.VMEM((24, ATTN_TILES, 16, 128), BF),
            pltpu.SemaphoreType.DMA((3,)),
        ],
        compiler_params=params(),
        cost_estimate=cost(
            flops=6 * count * D * D, bytes_accessed=count * D * 18, transcendentals=0
        ),
        name="input_grad",
    )(wa, dh1, first, second)


def retile(flat, blocks):
    tall = flat.shape[0] // (16 * blocks)
    tiles = flat.reshape(tall, 16, blocks, 128).transpose(0, 2, 1, 3)
    return tiles.reshape(tall * blocks, 16, 128)


def untile(tiles, blocks):
    tall = tiles.shape[0] // blocks
    flat = tiles.reshape(tall, blocks, 16, 128).transpose(0, 2, 1, 3)
    return flat.reshape(tall * blocks * 16, 128)


def pad_vectors(flat):
    return jnp.pad(flat, (0, VEC_ROWS * 128 - flat.shape[0])).reshape(VEC_TILES, 16, 128)


def gather_plain(attn, ffn, vectors):
    attn = lax.all_gather(attn, "fsdp", axis=0, tiled=True)
    ffn = lax.all_gather(ffn, "fsdp", axis=0, tiled=True)
    vec = lax.all_gather(vectors, "fsdp", axis=0, tiled=True)
    half = ffn.shape[0] // 2
    tiles = jnp.concatenate([retile(ffn[:half], 24), retile(ffn[half:], 6)], axis=0)
    attn_tiles = retile(attn, 6).reshape(OWNERS, ATTN_TILES, 16, 128)
    return attn_tiles, tiles.reshape(OWNERS, FFN_TILES, 16, 128), pad_vectors(vec)[None]


class Gather:
    def __init__(self, tiles, vec=None):
        self.own, self.tiles, self.vec = tiles, tiles.shape[0], vec

    def ride(self, message):
        return message if self.vec is None else jnp.concatenate([message, self.vec], axis=0)

    def landed(self, messages, size):
        if self.vec is None:
            return messages
        total = self.vec.astype(F32) + sum(m[size:].astype(F32) for m in messages)
        self.vec = total.astype(BF)
        return [m[:size] for m in messages]

    def planes(self):
        message = self.ride(self.own)
        self.hops = [hop(message, 8 * step) for step in (1, 2, 3)]

    def join(self):
        others = self.landed(self.hops, self.tiles)
        self.parts = [jnp.concatenate([self.own] + others, axis=0)]

    def sides(self):
        first, *rest = self.parts
        self.hops = [hop(self.ride(first), 2), hop(first, 4)]
        self.hops += [hop(part, bit) for part in rest for bit in (2, 4)]

    def corner(self):
        size = self.parts[0].shape[0]
        self.over_x = self.landed(self.hops[:1], size) + self.hops[2::2]
        self.over_y = self.hops[1::2]
        low = self.over_y[0][: 2 * self.tiles]
        high = jnp.concatenate([self.over_x[0][2 * self.tiles :]] + self.over_x[1:], axis=0)
        self.hops = [hop(low, 2), hop(self.ride(high), 4)]

    def pieces(self):
        (high,) = self.landed(self.hops[1:], 2 * self.tiles)
        out = self.parts + self.over_x + self.over_y
        return out + [self.hops[0], high]

    def mirrored(self, pieces, ready=None):
        ready = ready or {}
        return pieces + [ready[i] if i in ready else hop(piece, 1) for i, piece in enumerate(pieces)]

    def vectors(self):
        return jnp.stack([self.vec, hop(self.vec, 1)], axis=0)


def hop(value, bit):
    pairs = [(i, i ^ bit) for i in range(OWNERS)]
    return lax.ppermute(value, "fsdp", pairs)


def reduce_plain(ffn_terms, attn_terms, vector_terms):
    def absolute(keep, send):
        planes = keep.shape[1]
        both = jnp.stack([keep, send], axis=1)
        return jnp.moveaxis(both, 2, 0).reshape(planes * 8, -1, 16, 128)

    dw1k, dw1s, dw2k, dw2s = ffn_terms
    up = untile(absolute(dw1k, dw1s).reshape(-1, 16, 128), 24)
    down = untile(absolute(dw2k, dw2s).reshape(-1, 16, 128), 6)
    proj = untile(absolute(*attn_terms).reshape(-1, 16, 128), 6)

    def scatter(value):
        return lax.psum_scatter(value.astype(F32), "fsdp", scatter_dimension=0, tiled=True)

    return scatter(proj), scatter(jnp.concatenate([up, down], axis=0)), scatter(vector_terms)


def get(message, index, tiles):
    if len(message.shape) == 3:
        return message[pl.ds(index * tiles, tiles)].astype(F32)
    return message[index].astype(F32)


def put(message, index, tiles, value):
    if len(message.shape) == 3:
        message[pl.ds(index * tiles, tiles)] = value.astype(message.dtype)
    else:
        message[index] = value.astype(message.dtype)


def take_terms(refs, spots, leaves):
    terms = {}
    for spot in spots:
        planes = []
        for _ in range(leaves):
            keep, other = refs.pop(0), refs.pop(0)
            planes += [(keep, other, p) for p in range(keep.shape[1])]
        terms[spot] = planes

    def term(spot, index):
        keep, other, plane = terms[spot][index]
        return keep[0, plane].astype(F32) + other[0, plane].astype(F32)

    return term, terms[spots[0]][0][0].shape[2]


def take_vec(refs, vec):
    if not vec:
        return None
    state, arrival = refs.pop(0), refs.pop(0)
    return state[...] + arrival[pl.ds(arrival.shape[0] - VEC_TILES, VEC_TILES)].astype(F32)


def put_tail(message, total):
    message[pl.ds(message.shape[0] - VEC_TILES, VEC_TILES)] = total.astype(BF)


def corner_kernel(leaves, vec, *refs):
    refs = list(refs)
    term, tiles = take_terms(refs, [(3, 0), (3, 1), (1, 0), (2, 1)], leaves)
    total = take_vec(refs, vec)
    to_x, to_y = refs[:2]
    for i in range(2):
        put(to_x, i, tiles, term((3, 0), i))
        put(to_x, 2 + i, tiles, term((1, 0), i))
        put(to_y, i, tiles, term((3, 1), i))
        put(to_y, 2 + i, tiles, term((2, 1), i))
    if vec:
        put_tail(to_x, total)
        refs[2][...] = total


def side_kernel(leaves, vec, *refs):
    refs = list(refs)
    term, tiles = take_terms(refs, [(1, 1), (2, 0)], leaves)
    from_x, from_y = refs.pop(0), refs.pop(0)
    total = take_vec(refs, vec)
    to_x, to_y = refs[:2]
    for i in range(2):
        put(to_x, i, tiles, term((1, 1), i) + get(from_y, i, tiles))
        put(to_y, i, tiles, term((2, 0), i) + get(from_x, i, tiles))
    if vec:
        put_tail(to_y, total)
        refs[2][...] = total


def plane_kernel(leaves, vec, me_ref, *refs):
    refs = list(refs)
    term, tiles = take_terms(refs, [(0, 0), (0, 1)], leaves)
    from_x, from_y, from_x_two, from_y_two = (refs.pop(0) for _ in range(4))
    total = take_vec(refs, vec)
    mine, outs, own = refs[0], refs[1:4], refs[-1]
    for i in range(2):
        lower = term((0, 0), i) + get(from_x, 2 + i, tiles) + get(from_y_two, i, tiles)
        upper = term((0, 1), i) + get(from_y, 2 + i, tiles) + get(from_x_two, i, tiles)
        own[2 * i if leaves == 2 else i] = lower
        own[2 * i + 1 if leaves == 2 else 2 + i] = upper
    my_z = me_ref[0] >> 3
    mine[...] = own[my_z]
    for step in range(3):
        if vec:
            outs[step][pl.ds(0, tiles)] = own[my_z ^ (step + 1)].astype(BF)
            put_tail(outs[step], total)
        else:
            outs[step][...] = own[my_z ^ (step + 1)].astype(BF)
    if vec:
        refs[4][...] = total


class Reduction:
    def __init__(self, keeps, sends, me, vec=None):
        self.keeps, self.me, self.vec = keeps, me, vec
        self.hops = [hop(send, 1) for send in sends]
        if vec is not None:
            self.hops.append(hop(vec.astype(BF), 1))
        self.tiles = keeps[0].shape[2]
        self.steps = 3 if vec is None else 1

    def run(self, kernel, spots, arrivals, outs, name, place=False):
        leaves, tiles, block = len(self.keeps), self.tiles, self.tiles // self.steps
        carries = self.vec is not None
        arrays, in_specs = [], []
        for spot, half in spots:
            for keep, other in zip(self.keeps, self.received, strict=True):
                spec = pl.BlockSpec(
                    (1, keep.shape[1] // 2, block, 16, 128),
                    lambda t, *_, spot=spot, half=half: (spot, half, t, 0, 0),
                )
                arrays += [keep, other]
                in_specs += [spec, spec]

        def message_spec(shape):
            if len(shape) == 4:
                return pl.BlockSpec((shape[0], block, 16, 128), lambda t, *_: (0, t, 0, 0))
            if carries:
                return whole(shape)
            return pl.BlockSpec((block, 16, 128), lambda t, *_: (t, 0, 0))

        for array in arrivals:
            arrays.append(array)
            in_specs.append(message_spec(array.shape))
        if carries:
            arrays += [self.vec, self.vec_arrival]
            in_specs += [whole(self.vec.shape), whole(self.vec_arrival.shape)]
        out_shape = []
        for planes, dtype, tail in outs:
            tail = VEC_TILES if tail and carries else 0
            if carries:
                dims = (planes * tiles + tail, 16, 128)
            else:
                dims = (planes, tiles, 16, 128) if planes > 1 else (tiles, 16, 128)
            out_shape.append(jax.ShapeDtypeStruct(dims, dtype))
        out_specs = [message_spec(shape.shape) for shape in out_shape]
        if carries:
            out_shape.append(jax.ShapeDtypeStruct(self.vec.shape, F32))
            out_specs.append(whole(self.vec.shape))
        result = pl.pallas_call(
            functools.partial(kernel, leaves, carries),
            grid_spec=pltpu.PrefetchScalarGridSpec(
                num_scalar_prefetch=1 if place else 0,
                grid=(self.steps,),
                in_specs=in_specs,
                out_specs=out_specs,
                scratch_shapes=[pltpu.VMEM((4, block, 16, 128), F32)] if place else [],
            ),
            out_shape=out_shape,
            compiler_params=params(),
            cost_estimate=cost(flops=0, bytes_accessed=tiles * 4096 * 16, transcendentals=0),
            name=name,
        )(*([self.me] if place else []), *arrays)
        if carries:
            *result, self.vec = result
        return result

    def corner(self):
        self.received = self.hops[: len(self.keeps)]
        self.vec_arrival = self.hops[-1]
        to_x, to_y = self.run(
            corner_kernel, [(3, 0), (3, 1), (1, 0), (2, 1)], [], [(4, BF, True), (4, BF, False)], "corner"
        )
        self.messages = [to_x, to_y]

    def send(self):
        self.hops = [hop(self.messages[0], 2), hop(self.messages[1], 4)]

    def sides(self):
        self.early = self.hops
        self.vec_arrival = self.hops[0]
        to_x, to_y = self.run(
            side_kernel, [(1, 1), (2, 0)], self.early, [(2, BF, False), (2, BF, True)], "sides"
        )
        self.hops = [hop(to_x, 2), hop(to_y, 4)]

    def planes(self):
        self.vec_arrival = self.hops[1]
        outs = [(1, F32, False)] + [(1, BF, True)] * 3
        self.mine, *messages = self.run(
            plane_kernel, [(0, 0), (0, 1)], self.early + self.hops, outs, "planes", place=True
        )
        self.hops = messages

    def cross(self):
        self.hops = [hop(message, 8 * (i + 1)) for i, message in enumerate(self.hops)]

    def total(self):
        tiles = self.tiles
        if self.vec is not None:
            self.vec = self.vec + sum(other[tiles:].astype(F32) for other in self.hops)
        return self.mine + sum(other[:tiles].astype(F32) for other in self.hops)


def meet(hops, values):
    return lax.optimization_barrier((hops, values))


def tiles_of(array):
    return array.reshape(array.shape[:2] + (-1, 16, 128))


def spans(segments, pad_segment):
    pad = pad_segment[:, None]
    seen = jnp.where(segments == pad, -1, segments)
    first, last = segments[:, ::128], segments[:, 127::128]
    last = jnp.minimum(last, pad - 1)
    below = jnp.sum(segments[:, None, :] < first[:, :, None], axis=2)
    upto = jnp.sum(segments[:, None, :] <= last[:, :, None], axis=2)
    start = below // 128
    count = jnp.where(first == pad, 0, (upto + 127) // 128 - start)
    both = jnp.stack([jnp.where(count == 0, 0, start), count], axis=2)
    return seen, both.reshape(segments.shape[0], 8).astype(jnp.int32)


def layer(tokens, attn_matrices, ffn_matrices, vectors, segments, pad_segment, cotangent, size):
    fast = size == OWNERS
    each = vectors.shape[0]
    place = lax.axis_index("fsdp") if fast else jnp.zeros((), jnp.int32)
    me = place.reshape(1).astype(jnp.int32)
    my_z = place >> 3
    rows = segments.shape[0]
    seen, span = spans(segments, pad_segment)
    segc = seen.reshape(rows * SLOTS, 1)
    segr = seen.reshape(rows, 1, SLOTS)

    if fast:
        lower = place < OWNERS // 2
        flat = jnp.zeros((VEC_ROWS * 128,), BF)
        mine = lax.dynamic_update_slice(flat, vectors, (place * each,)).reshape(VEC_TILES, 16, 128)
        attn_in = Gather(retile(attn_matrices, 6), mine)
        ffn_in = Gather(jnp.where(lower, retile(ffn_matrices, 24), retile(ffn_matrices, 6)))
        attn_in.planes()
        attn_in.hops, (ffn_in.own, segc, segr, span) = meet(
            attn_in.hops, (ffn_in.own, segc, segr, span)
        )
        ffn_in.planes()
        attn_in.join()
        attn_in.sides()
        attn_in.hops, ffn_in.hops[:2] = meet(attn_in.hops, ffn_in.hops[:2])
        attn_in.corner()
        pieces, vecs = attn_in.mirrored(attn_in.pieces()), attn_in.vectors()
        ffn_in.hops, (pieces, vecs) = meet(ffn_in.hops, (pieces, vecs))
        ffn_in.join()
        ffn_in.sides()
    else:
        gathered, ffn_tiles, vecs = gather_plain(attn_matrices, ffn_matrices, vectors)
        pieces = [gathered]
    query, key, value, ctx, lse, wa, vec = attn_fwd(
        fast, me, span, pieces, vecs, tokens, segc, segr
    )
    if fast:
        ffn_in.hops, (ctx, wa, vec) = meet(ffn_in.hops, (ctx, wa, vec))
        ffn_in.corner()
        large = (ffn_in.parts[0], ffn_in.over_x[0], ffn_in.over_y[0])
        ready = {i: hop(part, 1) for i, part in enumerate(large)}
    n1, rstd = norm_fwd(wa, ctx, tokens, vec)
    if fast:
        ffn_in.hops, (n1, rstd) = meet(ffn_in.hops, (n1, rstd))
        ffn_pieces = ffn_in.mirrored(ffn_in.pieces(), ready)
    else:
        ffn_pieces = [ffn_tiles]
    out, dw1k, dw1s, dw2k, dw2s, vg, dh1, da, dctx = ffn_layer(
        fast, me, ffn_pieces, wa, n1, rstd, cotangent, segc, vec
    )
    if not fast:
        first = attn_bwd(span, query, key, value, ctx, dctx, lse, segc, segr, 0, 3)
        second = attn_bwd(span, query, key, value, ctx, dctx, lse, segc, segr, 3, 3)
        dwk, dws, vg = proj_grad(me, tokens, ctx, first, second, da, vg)
        dx = input_grad(wa, dh1, first, second)
        vector_terms = vg.reshape(-1)[: 12 * D]
        return (out, dx) + reduce_plain((dw1k, dw1s, dw2k, dw2s), (dwk, dws), vector_terms)

    ffn = Reduction([tiles_of(dw1k), tiles_of(dw2k)], [tiles_of(dw1s), tiles_of(dw2s)], me)
    first = attn_bwd(span, query, key, value, ctx, dctx, lse, segc, segr, 0, 3)
    ffn.hops, (first, dctx) = meet(ffn.hops, (first, dctx))
    ffn.corner()
    ffn.send()
    second = attn_bwd(span, query, key, value, ctx, dctx, lse, segc, segr, 3, 3)
    dwk, dws, vg = proj_grad(me, tokens, ctx, first, second, da, vg)
    ffn.hops, (dwk, dws, vg, first) = meet(ffn.hops, (dwk, dws, vg, first))
    ffn.sides()
    attn = Reduction([tiles_of(dwk)], [tiles_of(dws)], me, vg.reshape(VEC_TILES, 16, 128))
    dx = input_grad(wa, dh1, first, second)
    attn.hops, dx = meet(attn.hops, dx)
    attn.corner()
    ffn.hops, attn.messages = meet(ffn.hops, attn.messages)
    attn.send()
    ffn.planes()
    ffn.cross()
    ffn.hops[:2], attn.hops = meet(ffn.hops[:2], attn.hops)
    attn.sides()
    ffn.hops[2:], attn.hops = meet(ffn.hops[2:], attn.hops)
    attn.planes()
    attn.cross()
    ffn.hops, attn.hops = meet(ffn.hops, attn.hops)

    ffn_sum = ffn.total()
    ffn_grad = jnp.where(lower, untile(ffn_sum, 24), untile(ffn_sum, 6))
    attn_grad = untile(attn.total(), 6)
    vector_grad = lax.dynamic_slice(attn.vec.reshape(-1), (place * each,), (each,))
    return out, dx, attn_grad, ffn_grad, vector_grad


def solution(mesh):
    size = mesh.shape["fsdp"]
    return jax.shard_map(
        functools.partial(layer, size=size),
        mesh=mesh,
        in_specs=(
            P("fsdp", None),
            P("fsdp", None),
            P("fsdp", None),
            P("fsdp"),
            P("fsdp", None),
            P("fsdp"),
            P("fsdp", None),
        ),
        out_specs=(P("fsdp", None), P("fsdp", None), P("fsdp", None), P("fsdp", None), P("fsdp")),
        check_vma=False,
    )
```

```python
import functools

import jax
import jax.numpy as jnp
from jax import lax
from jax.experimental import pallas as pl
from jax.experimental.pallas import tpu as pltpu
from jax.sharding import PartitionSpec as P

D = 768
FF = 3072
SLOTS = 512
BF = jnp.bfloat16
F32 = jnp.float32
NN = ((1,), (0,))
NT = ((1,), (1,))
TN = ((0,), (0,))
OWNERS = 32
ATTN_TILES = 36
FFN_TILES = 72
COST_SCALE = 1
VMEM_LIMIT = 64 * 1024 * 1024

TAIL_SLOPE = 0.39 * 0.5**0.5
TAIL_POLY = (
    0.11766260955586648,
    0.04569420719462487,
    0.32477969950633645,
    -0.3177001395785759,
    0.44333218507090993,
    -0.11376856259852677,
)


def dot(left, right, dims):
    return lax.dot_general(left, right, (dims, ((), ())), preferred_element_type=F32)


def params(**kwargs):
    return pltpu.CompilerParams(vmem_limit_bytes=VMEM_LIMIT, **kwargs)


def cost(flops, bytes_accessed, transcendentals):
    return pl.CostEstimate(
        flops=flops // COST_SCALE,
        bytes_accessed=bytes_accessed // COST_SCALE,
        transcendentals=transcendentals // COST_SCALE,
    )


def whole(shape):
    zeros = (0,) * len(shape)
    return pl.BlockSpec(shape, lambda *_: zeros)


ANY = pl.BlockSpec(memory_space=pl.ANY)
VEC_TILES = 5
VEC_ROWS = 16 * VEC_TILES


def row(vec_ref, index, width=D):
    blocks = width // 128
    return jnp.concatenate([vec_ref[pl.ds(6 * index + i, 1), :] for i in range(blocks)], axis=1)


def put_row(vec_ref, index, value, first=0):
    for i in range(value.shape[1] // 128):
        vec_ref[pl.ds(6 * index + first + i, 1), :] = value[:, 128 * i : 128 * i + 128]


def square_cols(tiles, first, col):
    parts = [tiles[pl.ds(first, 8), i * 6 + col] for i in range(6)]
    return jnp.stack(parts, axis=1).reshape(D, 128)


def square(tiles, first):
    return jnp.concatenate([square_cols(tiles, first, col) for col in range(6)], axis=1)


def up_col(tiles, col):
    parts = [tiles[pl.ds(0, 16), i * 24 + col] for i in range(3)]
    return jnp.stack(parts, axis=1).reshape(D, 128)


def up_chunk(tiles, chunk):
    return jnp.concatenate([up_col(tiles, chunk * 6 + col) for col in range(6)], axis=1)


def down_chunk(tiles, chunk):
    cols = []
    for col in range(6):
        parts = [tiles[pl.ds(16 + 4 * chunk, 4), i * 6 + col] for i in range(12)]
        cols.append(jnp.stack(parts, axis=1).reshape(D, 128))
    return jnp.concatenate(cols, axis=1)


def piece_count(parts):
    return 2 * (3 * parts + 2)


def piece_copies(me, refs, tiles, parts, w_s):
    yxc, my_z = me & 7, me >> 3
    planes = []
    for step in range(4):
        copies = []
        for core in range(2):
            arrays = refs[core * (3 * parts + 2) :]
            for side in range(4):
                if side == 3:
                    source, index = arrays[3 * parts + step // 2], step % 2
                elif parts == 2 and step == 3:
                    source, index = arrays[2 * side + 1], 0
                else:
                    source, index = arrays[parts * side], step
                owner = 8 * (my_z ^ step) + (yxc ^ (2 * side + core))
                copies.append((source.at[pl.ds(index * tiles, tiles)], w_s.at[owner]))
        planes.append(copies)
    return planes


def attn_copies(fast, me, refs, w_s, sems):
    if not fast:
        return [pltpu.make_async_copy(refs[0], w_s, sems.at[0])]
    planes = piece_copies(me, refs, ATTN_TILES, 1, w_s)
    copies = [copy for plane in planes for copy in plane]
    return [pltpu.make_async_copy(src, dst, sems.at[i]) for i, (src, dst) in enumerate(copies)]


def attn_fwd_kernel(fast, me_ref, span_ref, *args):
    count = piece_count(1) if fast else 1
    refs = args[:count]
    (
        vec_ref, x_ref, segc_ref, segr_ref,
        q_ref, k_ref, v_ref, ctx_ref, lse_ref, wa_ref, vec_out_ref,
        w_s, vt_s, sems, out_sem,
    ) = args[count:]
    line, col = pl.program_id(0), pl.program_id(1)
    first_step = (line == 0) & (col == 0)
    last_step = (line == pl.num_programs(0) - 1) & (col == pl.num_programs(1) - 1)
    out_copy = pltpu.make_async_copy(w_s, wa_ref, out_sem)

    @pl.when(first_step)
    def _():
        copies = attn_copies(fast, me_ref[0], refs, w_s, sems)
        for copy in copies:
            copy.start()
        vec = vec_ref[0].astype(F32)
        for i in range(1, vec_ref.shape[0]):
            vec = vec + vec_ref[i].astype(F32)
        vec_out_ref[...] = vec.reshape(VEC_ROWS, 128)
        for copy in copies:
            copy.wait()
        out_copy.start()

    @pl.when(last_step)
    def _():
        out_copy.wait()

    cols = [2 * col, 2 * col + 1]
    weight = jnp.concatenate([square_cols(w_s, 8 * m, c) for m in range(3) for c in cols], axis=1)
    qkv = dot(x_ref[...], weight, NN)
    bias_q = jnp.concatenate([vec_out_ref[pl.ds(c, 1), :] for c in cols], axis=1)
    bias_v = jnp.concatenate([vec_out_ref[pl.ds(6 + c, 1), :] for c in cols], axis=1)
    q_ref[...] = (qkv[:, :256] + bias_q).astype(BF) * 0.125
    k_ref[...] = qkv[:, 256:512].astype(BF)
    v_ref[...] = (qkv[:, 512:] + bias_v).astype(BF)
    lane = lax.broadcasted_iota(jnp.int32, (1, 128), 1)
    low = lane < 64
    zero = jnp.zeros((), BF)

    for pair in range(2):
        vt_s[pl.ds(128 * pair, 128), :] = v_ref[:, 128 * pair : 128 * pair + 128].T

    def attend(block, carry):
        rows = pl.ds(pl.multiple_of(block * 128, 128), 128)
        start, count = span_ref[line, 2 * block], span_ref[line, 2 * block + 1]

        @pl.when(count == 0)
        def _():
            ctx_ref[rows, :] = jnp.zeros((128, 256), BF)
            lse_ref[:, rows] = jnp.zeros((4, 128), F32)

        def window(size):
            @pl.when(count == size)
            def _():
                seen = pl.ds(pl.multiple_of(start * 128, 128), 128 * size)
                seg_row = segr_ref[:, rows]
                blocked = jnp.where(segc_ref[seen, :] == seg_row, 0.0, -1e30)
                keep = jnp.where(jnp.broadcast_to(seg_row, (64, 128)) < 0, 0.0, 1.0)
                scores = []
                for head in range(4):
                    lanes = slice(128 * (head // 2), 128 * (head // 2) + 128)
                    query = q_ref[rows, lanes]
                    query = jnp.where(low, query, zero) if head % 2 == 0 else jnp.where(low, zero, query)
                    scores.append(dot(k_ref[seen, lanes], query, NT) + blocked)
                tops = [jnp.max(score, axis=0, keepdims=True) for score in scores]
                expds = [jnp.exp(score - top) for score, top in zip(scores, tops)]
                totals = [jnp.sum(expd, axis=0, keepdims=True) for expd in expds]
                outs = []
                for head in range(4):
                    values = vt_s[pl.ds(64 * head, 64), seen]
                    out = dot(values, expds[head].astype(BF), NN)
                    outs.append(out * (1.0 / totals[head]) * keep)
                    lse_ref[pl.ds(head, 1), rows] = tops[head] + jnp.log(totals[head])
                ctx_ref[rows, :] = jnp.concatenate(outs, axis=0).T.astype(BF)

        for size in range(1, 5):
            window(size)
        return carry

    lax.fori_loop(0, 4, attend, 0)


def attn_fwd(fast, me, span, pieces, vec, tokens, segc, segr):
    count = tokens.shape[0]
    rows = count // SLOTS
    part = pl.BlockSpec((SLOTS, 256), lambda r, j, m, s: (r, j))
    slot = pl.BlockSpec((SLOTS, 1), lambda r, j, m, s: (r, 0))
    shape = jax.ShapeDtypeStruct
    return pl.pallas_call(
        functools.partial(attn_fwd_kernel, fast),
        grid_spec=pltpu.PrefetchScalarGridSpec(
            num_scalar_prefetch=2,
            grid=(rows, 3),
            in_specs=[ANY] * len(pieces)
            + [
                whole(vec.shape),
                pl.BlockSpec((SLOTS, D), lambda r, j, m, s: (r, 0)),
                slot,
                pl.BlockSpec((None, 1, SLOTS), lambda r, j, m, s: (r, 0, 0)),
            ],
            out_specs=[part] * 4
            + [pl.BlockSpec((None, None, 4, SLOTS), lambda r, j, m, s: (r, j, 0, 0)), ANY, whole((VEC_ROWS, 128))],
            scratch_shapes=[
                pltpu.VMEM((OWNERS, ATTN_TILES, 16, 128), BF),
                pltpu.VMEM((256, SLOTS), BF),
                pltpu.SemaphoreType.DMA((160,)),
                pltpu.SemaphoreType.DMA,
            ],
        ),
        out_shape=[shape((count, D), BF)] * 4
        + [
            shape((rows, 3, 4, SLOTS), F32),
            shape((OWNERS, ATTN_TILES, 16, 128), BF),
            shape((VEC_ROWS, 128), F32),
        ],
        compiler_params=params(),
        cost_estimate=cost(
            flops=2 * count * D * (3 * D + 4 * SLOTS), bytes_accessed=count * D * 12, transcendentals=count * SLOTS * 12
        ),
        name="attn_fwd",
    )(me, span, *pieces, vec, tokens, segc, segr)


def norm_parts(hidden):
    mean = jnp.mean(hidden, axis=1, keepdims=True)
    centered = hidden - mean
    var = jnp.mean(centered * centered, axis=1, keepdims=True)
    rstd = lax.rsqrt(var + 1e-12)
    return centered * rstd, rstd


def gelu_parts(u):
    size = jnp.abs(u)
    t = pl.reciprocal(1.0 + TAIL_SLOPE * size)
    poly = jnp.full_like(t, TAIL_POLY[-1])
    for coef in TAIL_POLY[-2::-1]:
        poly = poly * t + coef
    bell = jnp.exp(u * u * -0.5)
    tail = poly * t * bell
    phi_cdf = jnp.where(u > 0, 1.0 - tail, tail)
    return u * phi_cdf, phi_cdf + u * bell * 0.3989422804014327


NORM_TILE = 256


def norm_fwd_kernel(wa_ref, ctx_ref, x_ref, vec_ref, n1_ref, rstd_ref, wo_s, sem):
    copy = pltpu.make_async_copy(wa_ref.at[pl.ds(24, 8)], wo_s, sem)

    @pl.when(pl.program_id(0) == 0)
    def _():
        copy.start()
        copy.wait()

    hidden = x_ref[...].astype(F32) + dot(ctx_ref[...], square(wo_s, 0), NN) + row(vec_ref, 2)
    normed, rstd = norm_parts(hidden)
    n1_ref[...] = normed
    rstd_ref[...] = jnp.broadcast_to(rstd, rstd_ref.shape)


def norm_fwd(wa, ctx, tokens, vec):
    count = tokens.shape[0]
    rows = pl.BlockSpec((NORM_TILE, D), lambda i: (i, 0))
    slim = pl.BlockSpec((NORM_TILE, 128), lambda i: (i, 0))
    shape = jax.ShapeDtypeStruct
    return pl.pallas_call(
        norm_fwd_kernel,
        grid=(count // NORM_TILE,),
        in_specs=[ANY, rows, rows, whole((VEC_ROWS, 128))],
        out_specs=[rows, slim],
        out_shape=[shape((count, D), F32), shape((count, 128), F32)],
        scratch_shapes=[pltpu.VMEM((8, ATTN_TILES, 16, 128), BF), pltpu.SemaphoreType.DMA],
        compiler_params=params(),
        cost_estimate=cost(
            flops=2 * count * D * D, bytes_accessed=count * D * 9, transcendentals=0
        ),
        name="norm_fwd",
    )(wa, ctx, tokens, vec)


def ffn_copies(fast, me, refs, w_s, sems):
    if not fast:
        pairs = [[(refs[0].at[pl.ds(16 * m, 16)], w_s.at[pl.ds(16 * m, 16)])] for m in range(2)]
    else:
        planes = piece_copies(me, refs, FFN_TILES, 1, w_s)
        pairs = [planes[0] + planes[1], planes[2] + planes[3]]
    return [
        [pltpu.make_async_copy(src, dst, sems.at[m, i]) for i, (src, dst) in enumerate(group)]
        for m, group in enumerate(pairs)
    ]


MID_TILE = 1024


def pick(mine, even, odd):
    return jnp.where(mine == 0, even, odd), jnp.where(mine == 0, odd, even)


def norm_grad(normed, rstd, t):
    mean_t = jnp.mean(t, axis=1, keepdims=True)
    mean_tn = jnp.mean(t * normed, axis=1, keepdims=True)
    return (t - mean_t - normed * mean_tn) * rstd


def column_sum(value):
    return jnp.sum(value.astype(F32), axis=0, keepdims=True)


def ffn_kernel(fast, me_ref, *args):
    pieces = piece_count(1) if fast else 1
    (
        wa_ref, n1_ref, rstd_ref, cot_ref, seg_ref, vec_ref,
        out_ref, dw1k_ref, dw1s_ref, dw2k_ref, dw2s_ref, vg_ref, dh1_ref, da_ref, dctx_ref,
        w_s, wo_s, g_s, gp_s, yb_s, ybt_s, dz_s, du_s, r_s, ua_s, ub_s, sems, wo_sem,
    ) = args[pieces:]
    step = pl.program_id(0)
    me = me_ref[0]
    core, my_x, my_y = me & 1, (me >> 1) & 1, (me >> 2) & 1
    copies = ffn_copies(fast, me, args[:pieces], w_s, sems)
    holds_up = me < OWNERS // 2
    wo_copy = pltpu.make_async_copy(wa_ref.at[pl.ds(24, 8)], wo_s, wo_sem)
    count = n1_ref.shape[0]

    def tile(i, size):
        return pl.ds(pl.multiple_of(i * size, size), size)

    def wait_for(matrix):
        for group in range(2):

            @pl.when(holds_up == (group == matrix))
            def _(group=group):
                for copy in copies[group]:
                    copy.wait()

    @pl.when(step == 0)
    def _():
        for group in copies:
            for copy in group:
                copy.start()
        wo_copy.start()

        def body(i, carry):
            rows = tile(i, NORM_TILE)
            y_one = n1_ref[rows, :] * row(vec_ref, 3) + row(vec_ref, 4)
            yb_s[rows, :] = y_one.astype(BF)
            dh1_ref[rows, :] = y_one + row(vec_ref, 9)
            return carry

        lax.fori_loop(0, count // NORM_TILE, body, 0)
        ybt_s[...] = yb_s[...].T
        wait_for(0)

    @pl.when(step == 0)
    def _():
        def weights_of(sub):
            weight = jnp.concatenate([up_col(w_s, 2 * sub + i) for i in range(2)], axis=1)
            bias = jnp.concatenate([vec_ref[pl.ds(30 + 2 * sub + i, 1), :] for i in range(2)], axis=1)
            return weight, bias

        def advance(new_ref, new_sub, old_ref, old_sub):
            weight, bias = weights_of(new_sub)
            chunk = lax.div(old_sub, 3)
            lanes = tile(old_sub - 3 * chunk, 256)
            for first in range(0, count, 128):
                rows = slice(first, first + 128)
                new_ref[rows, :] = dot(yb_s[rows, :], weight, NN) + bias
                act, slope = gelu_parts(old_ref[rows, :])
                g_s[chunk, rows, lanes] = act.astype(BF)
                gp_s[chunk, rows, lanes] = slope.astype(BF)

        weight, bias = weights_of(0)
        ua_s[...] = dot(yb_s[...], weight, NN) + bias

        def widen(i, carry):
            advance(ub_s, 2 * i + 1, ua_s, 2 * i)
            advance(ua_s, jnp.minimum(2 * i + 2, 11), ub_s, 2 * i + 1)
            return carry

        lax.fori_loop(0, 6, widen, 0)
        wait_for(1)

        def narrow(i, carry):
            rows = tile(i, MID_TILE)
            total = dh1_ref[rows, :]
            for chunk in range(4):
                total = total + dot(g_s[chunk, rows, :], down_chunk(w_s, chunk), NN)
            dh1_ref[rows, :] = total
            return carry

        lax.fori_loop(0, count // MID_TILE, narrow, 0)

    @pl.when(step == 0)
    def _():
        def body(i, sums):
            rows = tile(i, NORM_TILE)
            normed, rstd = norm_parts(dh1_ref[rows, :])
            gain = row(vec_ref, 10)
            out_ref[rows, :] = (normed * gain + row(vec_ref, 11)).astype(BF)
            err = cot_ref[rows, :].astype(F32)
            dh2 = norm_grad(normed, rstd, gain * err)
            dz = dh2.astype(BF)
            dh1_ref[rows, :] = dh2
            dz_s[rows, :] = dz
            return (
                sums[0] + column_sum(dz),
                sums[1] + column_sum(err * normed),
                sums[2] + column_sum(err),
            )

        zero = jnp.zeros((1, D), F32)
        sums = lax.fori_loop(0, count // NORM_TILE, body, (zero, zero, zero))
        vg_ref[...] = jnp.zeros_like(vg_ref)
        for i in range(3):
            put_row(vg_ref, 9 + i, sums[i])

    @pl.when(step >= 1)
    def _():
        chunk = step - 1

        def back(i, total):
            rows = tile(i, MID_TILE)
            dg = dot(dz_s[rows, :], down_chunk(w_s, chunk), NT)
            du = (gp_s[chunk, rows, :].astype(F32) * dg).astype(BF)
            du_s[rows, :] = du
            dh1_ref[rows, :] += dot(du, up_chunk(w_s, chunk), NT)
            return total + column_sum(du)

        put_row(vg_ref, 5 + chunk, lax.fori_loop(0, count // MID_TILE, back, jnp.zeros((1, D), F32)))

        def weights(half, carry):
            lanes = tile(half, 384)
            r_s[...] = dot(ybt_s[lanes, :], du_s[...], NN).astype(BF)
            for pair in range(4):
                even, odd = r_s[pl.ds(pair * 96, 48), :], r_s[pl.ds(pair * 96 + 48, 48), :]
                keep, send = pick(core, even, odd)
                place = (((pair >> 1) ^ my_y) << 1) | ((pair & 1) ^ my_x)
                for col in range(6):
                    spot = slice(col * 128, col * 128 + 128)
                    dw1k_ref[place, half, :, col] = keep[:, spot].reshape(3, 16, 128)
                    dw1s_ref[place, half, :, col] = send[:, spot].reshape(3, 16, 128)
            r_s[...] = dot(g_s[chunk, :, lanes], dz_s[...], TN).astype(BF)
            keep, send = pick(core, r_s[:192, :], r_s[192:, :])
            for col in range(6):
                spot = slice(col * 128, col * 128 + 128)
                dw2k_ref[half ^ my_x, 0, :, col] = keep[:, spot].reshape(12, 16, 128)
                dw2s_ref[half ^ my_x, 0, :, col] = send[:, spot].reshape(12, 16, 128)
            return carry

        lax.fori_loop(0, 2, weights, 0)

    @pl.when(step == 4)
    def _():
        wo_copy.wait()

        def body(i, sums):
            rows = tile(i, NORM_TILE)
            dy1, normed = dh1_ref[rows, :], n1_ref[rows, :]
            dh1 = norm_grad(normed, rstd_ref[rows, 0:1], dy1 * row(vec_ref, 3))
            da = dh1.astype(BF)
            dh1_ref[rows, :] = dh1
            da_ref[rows, :] = da
            back = dot(da, square(wo_s, 0), NT)
            dctx_ref[rows, :] = jnp.where(seg_ref[rows, :] >= 0, back, 0.0).astype(BF)
            return (
                sums[0] + column_sum(da),
                sums[1] + column_sum(dy1 * normed),
                sums[2] + column_sum(dy1),
            )

        zero = jnp.zeros((1, D), F32)
        sums = lax.fori_loop(0, count // NORM_TILE, body, (zero, zero, zero))
        for i in range(3):
            put_row(vg_ref, 2 + i, sums[i])


def ffn_layer(fast, me, pieces, wa, n1, rstd, cotangent, segc, vec):
    count = n1.shape[0]
    once = pl.Buffered(1)

    def single(shape):
        zeros = (0,) * len(shape)
        return pl.BlockSpec(shape, lambda *_: zeros, pipeline_mode=once)

    full = whole((count, D))
    up = pl.BlockSpec(
        (4, 2, 3, 6, 16, 128), lambda s, m: (0, 0, 0, jnp.maximum(s - 1, 0), 0, 0)
    )

    def down_index(s, m):
        chunk = jnp.maximum(s - 1, 0)
        return ((chunk % 2) ^ ((m[0] >> 2) & 1), chunk // 2, 0, 0, 0, 0)

    down = pl.BlockSpec((2, 1, 12, 6, 16, 128), down_index)
    shape = jax.ShapeDtypeStruct
    return pl.pallas_call(
        functools.partial(ffn_kernel, fast),
        grid_spec=pltpu.PrefetchScalarGridSpec(
            num_scalar_prefetch=1,
            grid=(5,),
            in_specs=[ANY] * len(pieces)
            + [
                ANY,
                single((count, D)),
                single((count, 128)),
                single((count, D)),
                single((count, 1)),
                single((VEC_ROWS, 128)),
            ],
            out_specs=[full, up, up, down, down, whole((VEC_ROWS, 128)), full, full, full],
            scratch_shapes=[
                pltpu.VMEM((OWNERS, FFN_TILES, 16, 128), BF),
                pltpu.VMEM((8, ATTN_TILES, 16, 128), BF),
                pltpu.VMEM((4, count, D), BF),
                pltpu.VMEM((4, count, D), BF),
                pltpu.VMEM((count, D), BF),
                pltpu.VMEM((D, count), BF),
                pltpu.VMEM((count, D), BF),
                pltpu.VMEM((count, D), BF),
                pltpu.VMEM((D // 2, D), BF),
                pltpu.VMEM((count, 256), F32),
                pltpu.VMEM((count, 256), F32),
                pltpu.SemaphoreType.DMA((2, 40)),
                pltpu.SemaphoreType.DMA,
            ],
        ),
        out_shape=[shape((count, D), BF)]
        + [shape((4, 2, 3, 24, 16, 128), BF)] * 2
        + [shape((4, 2, 12, 6, 16, 128), BF)] * 2
        + [shape((VEC_ROWS, 128), F32), shape((count, D), F32)]
        + [shape((count, D), BF)] * 2,
        compiler_params=params(),
        cost_estimate=cost(
            flops=12 * count * D * FF, bytes_accessed=count * D * 30, transcendentals=count * FF
        ),
        name="ffn_layer",
    )(me, *pieces, wa, n1, rstd, cotangent, segc, vec)


def attn_bwd_kernel(
    first, span_ref, q_ref, k_ref, v_ref, ctx_ref, dctx_ref, lse_ref, segc_ref, segr_ref, d_ref, dqt_s, dots_s
):
    line = pl.program_id(0)
    pairs = q_ref.shape[1] // 128
    lane = lax.broadcasted_iota(jnp.int32, (1, 128), 1)
    low = lane < 64
    zero = jnp.zeros((), BF)
    spots = [slice(128 * pair, 128 * pair + 128) for pair in range(pairs)]
    for pair, lanes in enumerate(spots):
        products = (dctx_ref[:, lanes].astype(F32) * ctx_ref[:, lanes].astype(F32)).T
        for head in range(2):
            place = slice(4 * pair + head, 4 * pair + head + 1)
            dots_s[place, :] = jnp.sum(products[64 * head : 64 * head + 64], axis=0, keepdims=True)
            index = 2 * (first + pair) + head
            place = slice(4 * pair + 2 + head, 4 * pair + 3 + head)
            dots_s[place, :] = lse_ref[index // 4, index % 4 : index % 4 + 1, :]
    dqt_s[...] = jnp.zeros_like(dqt_s)

    def both(value):
        return jnp.concatenate([jnp.where(low, value, zero), jnp.where(low, zero, value)], axis=0)

    def block_step(block, carry):
        rows = pl.ds(pl.multiple_of(block * 128, 128), 128)
        start, count = span_ref[line, 2 * block], span_ref[line, 2 * block + 1]

        @pl.when(count == 0)
        def _():
            d_ref[1, rows, :] = jnp.zeros((128, 128 * pairs), BF)
            d_ref[2, rows, :] = jnp.zeros((128, 128 * pairs), BF)

        def window(size):
            @pl.when(count == size)
            def _():
                seen = pl.ds(pl.multiple_of(start * 128, 128), 128 * size)
                seg_row = segr_ref[:, seen]
                allowed = segc_ref[rows, :] == jnp.where(seg_row < 0, -2, seg_row)
                allowed = jnp.concatenate([allowed, allowed], axis=0)

                def spread(pair, offset):
                    lines = [dots_s[4 * pair + offset + h : 4 * pair + offset + h + 1, seen] for h in range(2)]
                    return jnp.concatenate([jnp.broadcast_to(r, (128, 128 * size)) for r in lines], axis=0)

                keys = [both(k_ref[rows, lanes]) for lanes in spots]
                queries = [q_ref[seen, lanes] for lanes in spots]
                dctxs = [dctx_ref[seen, lanes] for lanes in spots]
                scores = [dot(k, q, NT) for k, q in zip(keys, queries)]
                dprobs = [dot(both(v_ref[rows, lanes]), dctx, NT) for lanes, dctx in zip(spots, dctxs)]
                probs = [
                    jnp.where(allowed, jnp.exp(score - spread(pair, 2)), 0.0)
                    for pair, score in enumerate(scores)
                ]
                dscores = [
                    (prob * (dprob - spread(pair, 0))).astype(BF)
                    for pair, (prob, dprob) in enumerate(zip(probs, dprobs))
                ]
                dvs = [dot(prob.astype(BF), dctx, NN) for prob, dctx in zip(probs, dctxs)]
                dks = [dot(dscore, query, NN) for dscore, query in zip(dscores, queries)]
                dqs = [dot(key, dscore, TN) for key, dscore in zip(keys, dscores)]
                for pair, lanes in enumerate(spots):
                    dqt_s[lanes, seen] += dqs[pair]
                    d_ref[1, rows, lanes] = jnp.where(low, dks[pair][:128], dks[pair][128:]).astype(BF)
                    d_ref[2, rows, lanes] = jnp.where(low, dvs[pair][:128], dvs[pair][128:]).astype(BF)

        for size in range(1, 5):
            window(size)
        return carry

    lax.fori_loop(0, 4, block_step, 0)
    d_ref[0] = (dqt_s[...].T * 0.125).astype(BF)


def attn_bwd(span, query, key, value, ctx, dctx, lse, segc, segr, first, cols):
    count = query.shape[0]
    rows = count // SLOTS
    width = 128 * cols
    part = pl.BlockSpec((SLOTS, width), lambda r, s: (r, first // cols))
    return pl.pallas_call(
        functools.partial(attn_bwd_kernel, first),
        grid_spec=pltpu.PrefetchScalarGridSpec(
            num_scalar_prefetch=1,
            grid=(rows,),
            in_specs=[part] * 5
            + [
                pl.BlockSpec((None, 3, 4, SLOTS), lambda r, s: (r, 0, 0, 0)),
                pl.BlockSpec((SLOTS, 1), lambda r, s: (r, 0)),
                pl.BlockSpec((None, 1, SLOTS), lambda r, s: (r, 0, 0)),
            ],
            out_specs=pl.BlockSpec((3, SLOTS, width), lambda r, s: (0, r, 0)),
            scratch_shapes=[pltpu.VMEM((width, SLOTS), F32), pltpu.VMEM((4 * cols, SLOTS), F32)],
        ),
        out_shape=jax.ShapeDtypeStruct((3, count, width), BF),
        compiler_params=params(),
        cost_estimate=cost(
            flops=10 * count * D * SLOTS, bytes_accessed=count * D * 16, transcendentals=count * SLOTS * 12
        ),
        name="attn_bwd",
    )(span, query, key, value, ctx, dctx, lse, segc, segr)


def proj_grad_kernel(me_ref, x_ref, ctx_ref, first_ref, second_ref, third_ref, da_ref, vg_in_ref, dwk_ref, dws_ref, vg_ref, r_s):
    step = pl.program_id(0)
    me = me_ref[0]
    core, my_x, my_y = me & 1, (me >> 1) & 1, (me >> 2) & 1

    @pl.when(step == 0)
    def _():
        vg_ref[...] = vg_in_ref[...]

    @pl.when(step < 3)
    def _():
        grad = jnp.concatenate([first_ref[...], second_ref[...], third_ref[...]], axis=1)
        r_s[...] = dot(x_ref[...], grad, TN).astype(BF)

        @pl.when(step != 1)
        def _():
            put_row(vg_ref, step >> 1, column_sum(grad))

    @pl.when(step == 3)
    def _():
        r_s[...] = dot(ctx_ref[...], da_ref[...], TN).astype(BF)

    for pair in range(4):
        even, odd = r_s[pl.ds(pair * 192, 96), :], r_s[pl.ds(pair * 192 + 96, 96), :]
        keep, send = pick(core, even, odd)
        place = (((pair >> 1) ^ my_y) << 1) | ((pair & 1) ^ my_x)
        for col in range(6):
            lanes = slice(col * 128, col * 128 + 128)
            dwk_ref[place, 0, :, col] = keep[:, lanes].reshape(6, 16, 128)
            dws_ref[place, 0, :, col] = send[:, lanes].reshape(6, 16, 128)


def proj_grad(me, tokens, ctx, grads, da, vg):
    count, width = grads[0].shape[1:]
    out = pl.BlockSpec((4, 1, 6, 6, 16, 128), lambda i, m: (0, i, 0, 0, 0, 0))
    full = whole((count, D))
    part = pl.BlockSpec((None, count, width), lambda i, m: (jnp.minimum(i, 2), 0, 0))
    shape = jax.ShapeDtypeStruct
    return pl.pallas_call(
        proj_grad_kernel,
        grid_spec=pltpu.PrefetchScalarGridSpec(
            num_scalar_prefetch=1,
            grid=(4,),
            in_specs=[full, full, part, part, part, full, whole((VEC_ROWS, 128))],
            out_specs=[out, out, whole((VEC_ROWS, 128))],
            scratch_shapes=[pltpu.VMEM((D, D), BF)],
        ),
        out_shape=[shape((4, 4, 6, 6, 16, 128), BF)] * 2 + [shape((VEC_ROWS, 128), F32)],
        compiler_params=params(),
        cost_estimate=cost(
            flops=8 * count * D * D, bytes_accessed=count * D * 20, transcendentals=0
        ),
        name="proj_grad",
    )(me, tokens, ctx, *grads, da, vg)


def input_grad_kernel(wa_ref, dh1_ref, da_ref, db_ref, dc_ref, out_ref, w_s, sems):
    @pl.when(pl.program_id(0) == 0)
    def _():
        copies = [
            pltpu.make_async_copy(
                wa_ref.at[pl.ds(8 * m, 8)],
                w_s.at[pl.ds(8 * m, 8)],
                sems.at[m],
            )
            for m in range(3)
        ]
        for copy in copies:
            copy.start()
        for copy in copies:
            copy.wait()

    total = dh1_ref[...]
    for m in range(3):
        grad = jnp.concatenate([da_ref[m], db_ref[m], dc_ref[m]], axis=1)
        total = total + dot(grad, square(w_s, 8 * m), NT)
    out_ref[...] = total.astype(BF)


def input_grad(wa, dh1, grads):
    count = dh1.shape[0]
    rows = pl.BlockSpec((NORM_TILE, D), lambda i: (i, 0))
    return pl.pallas_call(
        input_grad_kernel,
        grid=(count // NORM_TILE,),
        in_specs=[ANY, rows] + [pl.BlockSpec((3, NORM_TILE, D // 3), lambda i: (0, i, 0))] * 3,
        out_specs=rows,
        out_shape=jax.ShapeDtypeStruct((count, D), BF),
        scratch_shapes=[
            pltpu.VMEM((24, ATTN_TILES, 16, 128), BF),
            pltpu.SemaphoreType.DMA((3,)),
        ],
        compiler_params=params(),
        cost_estimate=cost(
            flops=6 * count * D * D, bytes_accessed=count * D * 18, transcendentals=0
        ),
        name="input_grad",
    )(wa, dh1, *grads)


def retile(flat, blocks):
    tall = flat.shape[0] // (16 * blocks)
    tiles = flat.reshape(tall, 16, blocks, 128).transpose(0, 2, 1, 3)
    return tiles.reshape(tall * blocks, 16, 128)


def untile(tiles, blocks):
    tall = tiles.shape[0] // blocks
    flat = tiles.reshape(tall, blocks, 16, 128).transpose(0, 2, 1, 3)
    return flat.reshape(tall * blocks * 16, 128)


def pad_vectors(flat):
    return jnp.pad(flat, (0, VEC_ROWS * 128 - flat.shape[0])).reshape(VEC_TILES, 16, 128)


def gather_plain(attn, ffn, vectors):
    attn = lax.all_gather(attn, "fsdp", axis=0, tiled=True)
    ffn = lax.all_gather(ffn, "fsdp", axis=0, tiled=True)
    vec = lax.all_gather(vectors, "fsdp", axis=0, tiled=True)
    half = ffn.shape[0] // 2
    tiles = jnp.concatenate([retile(ffn[:half], 24), retile(ffn[half:], 6)], axis=0)
    attn_tiles = retile(attn, 6).reshape(OWNERS, ATTN_TILES, 16, 128)
    return attn_tiles, tiles.reshape(OWNERS, FFN_TILES, 16, 128), pad_vectors(vec)[None]


class Gather:
    def __init__(self, tiles, vec=None):
        self.own, self.tiles, self.vec = tiles, tiles.shape[0], vec

    def ride(self, message):
        return message if self.vec is None else jnp.concatenate([message, self.vec], axis=0)

    def landed(self, messages, size):
        if self.vec is None:
            return messages
        total = self.vec.astype(F32) + sum(m[size:].astype(F32) for m in messages)
        self.vec = total.astype(BF)
        return [m[:size] for m in messages]

    def planes(self):
        message = self.ride(self.own)
        self.hops = [hop(message, 8 * step) for step in (1, 2, 3)]

    def join(self):
        others = self.landed(self.hops, self.tiles)
        self.parts = [jnp.concatenate([self.own] + others, axis=0)]

    def sides(self):
        first, *rest = self.parts
        self.hops = [hop(self.ride(first), 2), hop(first, 4)]
        self.hops += [hop(part, bit) for part in rest for bit in (2, 4)]

    def corner(self):
        size = self.parts[0].shape[0]
        self.over_x = self.landed(self.hops[:1], size) + self.hops[2::2]
        self.over_y = self.hops[1::2]
        low = self.over_y[0][: 2 * self.tiles]
        high = jnp.concatenate([self.over_x[0][2 * self.tiles :]] + self.over_x[1:], axis=0)
        self.hops = [hop(low, 2), hop(self.ride(high), 4)]

    def pieces(self):
        (high,) = self.landed(self.hops[1:], 2 * self.tiles)
        out = self.parts + self.over_x + self.over_y
        return out + [self.hops[0], high]

    def mirrored(self, pieces, ready=None):
        ready = ready or {}
        return pieces + [ready[i] if i in ready else hop(piece, 1) for i, piece in enumerate(pieces)]

    def vectors(self):
        return jnp.stack([self.vec, hop(self.vec, 1)], axis=0)


def hop(value, bit):
    pairs = [(i, i ^ bit) for i in range(OWNERS)]
    return lax.ppermute(value, "fsdp", pairs)


def reduce_plain(ffn_terms, attn_terms, vector_terms):
    def absolute(keep, send):
        planes = keep.shape[1]
        both = jnp.stack([keep, send], axis=1)
        return jnp.moveaxis(both, 2, 0).reshape(planes * 8, -1, 16, 128)

    dw1k, dw1s, dw2k, dw2s = ffn_terms
    up = untile(absolute(dw1k, dw1s).reshape(-1, 16, 128), 24)
    down = untile(absolute(dw2k, dw2s).reshape(-1, 16, 128), 6)
    proj = untile(absolute(*attn_terms).reshape(-1, 16, 128), 6)

    def scatter(value):
        return lax.psum_scatter(value.astype(F32), "fsdp", scatter_dimension=0, tiled=True)

    return scatter(proj), scatter(jnp.concatenate([up, down], axis=0)), scatter(vector_terms)


def get(message, index, tiles):
    if len(message.shape) == 3:
        return message[pl.ds(index * tiles, tiles)].astype(F32)
    return message[index].astype(F32)


def put(message, index, tiles, value):
    if len(message.shape) == 3:
        message[pl.ds(index * tiles, tiles)] = value.astype(message.dtype)
    else:
        message[index] = value.astype(message.dtype)


def take_terms(refs, spots, leaves):
    terms = {}
    for spot in spots:
        planes = []
        for _ in range(leaves):
            keep, other = refs.pop(0), refs.pop(0)
            planes += [(keep, other, p) for p in range(keep.shape[1])]
        terms[spot] = planes

    def term(spot, index):
        keep, other, plane = terms[spot][index]
        return keep[0, plane].astype(F32) + other[0, plane].astype(F32)

    return term, terms[spots[0]][0][0].shape[2]


def take_vec(refs, vec):
    if not vec:
        return None
    state, arrival = refs.pop(0), refs.pop(0)
    return state[...] + arrival[pl.ds(arrival.shape[0] - VEC_TILES, VEC_TILES)].astype(F32)


def put_tail(message, total):
    message[pl.ds(message.shape[0] - VEC_TILES, VEC_TILES)] = total.astype(BF)


def corner_kernel(leaves, vec, *refs):
    refs = list(refs)
    term, tiles = take_terms(refs, [(3, 0), (3, 1), (1, 0), (2, 1)], leaves)
    total = take_vec(refs, vec)
    to_x, to_y = refs[:2]
    for i in range(2):
        put(to_x, i, tiles, term((3, 0), i))
        put(to_x, 2 + i, tiles, term((1, 0), i))
        put(to_y, i, tiles, term((3, 1), i))
        put(to_y, 2 + i, tiles, term((2, 1), i))
    if vec:
        put_tail(to_x, total)
        refs[2][...] = total


def side_kernel(leaves, vec, *refs):
    refs = list(refs)
    term, tiles = take_terms(refs, [(1, 1), (2, 0)], leaves)
    from_x, from_y = refs.pop(0), refs.pop(0)
    total = take_vec(refs, vec)
    to_x, to_y = refs[:2]
    for i in range(2):
        put(to_x, i, tiles, term((1, 1), i) + get(from_y, i, tiles))
        put(to_y, i, tiles, term((2, 0), i) + get(from_x, i, tiles))
    if vec:
        put_tail(to_y, total)
        refs[2][...] = total


def plane_kernel(leaves, vec, me_ref, *refs):
    refs = list(refs)
    term, tiles = take_terms(refs, [(0, 0), (0, 1)], leaves)
    from_x, from_y, from_x_two, from_y_two = (refs.pop(0) for _ in range(4))
    total = take_vec(refs, vec)
    mine, outs, own = refs[0], refs[1:4], refs[-1]
    for i in range(2):
        lower = term((0, 0), i) + get(from_x, 2 + i, tiles) + get(from_y_two, i, tiles)
        upper = term((0, 1), i) + get(from_y, 2 + i, tiles) + get(from_x_two, i, tiles)
        own[2 * i if leaves == 2 else i] = lower
        own[2 * i + 1 if leaves == 2 else 2 + i] = upper
    my_z = me_ref[0] >> 3
    mine[...] = own[my_z]
    for step in range(3):
        if vec:
            outs[step][pl.ds(0, tiles)] = own[my_z ^ (step + 1)].astype(BF)
            put_tail(outs[step], total)
        else:
            outs[step][...] = own[my_z ^ (step + 1)].astype(BF)
    if vec:
        refs[4][...] = total


class Reduction:
    def __init__(self, keeps, sends, me, vec=None):
        self.keeps, self.me, self.vec = keeps, me, vec
        self.hops = [hop(send, 1) for send in sends]
        if vec is not None:
            self.hops.append(hop(vec.astype(BF), 1))
        self.tiles = keeps[0].shape[2]
        self.steps = 3 if vec is None else 1

    def run(self, kernel, spots, arrivals, outs, name, place=False):
        leaves, tiles, block = len(self.keeps), self.tiles, self.tiles // self.steps
        carries = self.vec is not None
        arrays, in_specs = [], []
        for spot, half in spots:
            for keep, other in zip(self.keeps, self.received, strict=True):
                spec = pl.BlockSpec(
                    (1, keep.shape[1] // 2, block, 16, 128),
                    lambda t, *_, spot=spot, half=half: (spot, half, t, 0, 0),
                )
                arrays += [keep, other]
                in_specs += [spec, spec]

        def message_spec(shape):
            if len(shape) == 4:
                return pl.BlockSpec((shape[0], block, 16, 128), lambda t, *_: (0, t, 0, 0))
            if carries:
                return whole(shape)
            return pl.BlockSpec((block, 16, 128), lambda t, *_: (t, 0, 0))

        for array in arrivals:
            arrays.append(array)
            in_specs.append(message_spec(array.shape))
        if carries:
            arrays += [self.vec, self.vec_arrival]
            in_specs += [whole(self.vec.shape), whole(self.vec_arrival.shape)]
        out_shape = []
        for planes, dtype, tail in outs:
            tail = VEC_TILES if tail and carries else 0
            if carries:
                dims = (planes * tiles + tail, 16, 128)
            else:
                dims = (planes, tiles, 16, 128) if planes > 1 else (tiles, 16, 128)
            out_shape.append(jax.ShapeDtypeStruct(dims, dtype))
        out_specs = [message_spec(shape.shape) for shape in out_shape]
        if carries:
            out_shape.append(jax.ShapeDtypeStruct(self.vec.shape, F32))
            out_specs.append(whole(self.vec.shape))
        result = pl.pallas_call(
            functools.partial(kernel, leaves, carries),
            grid_spec=pltpu.PrefetchScalarGridSpec(
                num_scalar_prefetch=1 if place else 0,
                grid=(self.steps,),
                in_specs=in_specs,
                out_specs=out_specs,
                scratch_shapes=[pltpu.VMEM((4, block, 16, 128), F32)] if place else [],
            ),
            out_shape=out_shape,
            compiler_params=params(),
            cost_estimate=cost(flops=0, bytes_accessed=tiles * 4096 * 16, transcendentals=0),
            name=name,
        )(*([self.me] if place else []), *arrays)
        if carries:
            *result, self.vec = result
        return result

    def corner(self):
        self.received = self.hops[: len(self.keeps)]
        self.vec_arrival = self.hops[-1]
        to_x, to_y = self.run(
            corner_kernel, [(3, 0), (3, 1), (1, 0), (2, 1)], [], [(4, BF, True), (4, BF, False)], "corner"
        )
        self.messages = [to_x, to_y]

    def send(self):
        self.hops = [hop(self.messages[0], 2), hop(self.messages[1], 4)]

    def sides(self):
        self.early = self.hops
        self.vec_arrival = self.hops[0]
        to_x, to_y = self.run(
            side_kernel, [(1, 1), (2, 0)], self.early, [(2, BF, False), (2, BF, True)], "sides"
        )
        self.hops = [hop(to_x, 2), hop(to_y, 4)]

    def planes(self):
        self.vec_arrival = self.hops[1]
        outs = [(1, F32, False)] + [(1, BF, True)] * 3
        self.mine, *messages = self.run(
            plane_kernel, [(0, 0), (0, 1)], self.early + self.hops, outs, "planes", place=True
        )
        self.hops = messages

    def cross(self):
        self.hops = [hop(message, 8 * (i + 1)) for i, message in enumerate(self.hops)]

    def total(self):
        tiles = self.tiles
        if self.vec is not None:
            self.vec = self.vec + sum(other[tiles:].astype(F32) for other in self.hops)
        return self.mine + sum(other[:tiles].astype(F32) for other in self.hops)


def meet(hops, values):
    return lax.optimization_barrier((hops, values))


def tiles_of(array):
    return array.reshape(array.shape[:2] + (-1, 16, 128))


def spans(segments, pad_segment):
    pad = pad_segment[:, None]
    seen = jnp.where(segments == pad, -1, segments)
    first, last = segments[:, ::128], segments[:, 127::128]
    last = jnp.minimum(last, pad - 1)
    below = jnp.sum(segments[:, None, :] < first[:, :, None], axis=2)
    upto = jnp.sum(segments[:, None, :] <= last[:, :, None], axis=2)
    start = below // 128
    count = jnp.where(first == pad, 0, (upto + 127) // 128 - start)
    both = jnp.stack([jnp.where(count == 0, 0, start), count], axis=2)
    return seen, both.reshape(segments.shape[0], 8).astype(jnp.int32)


def layer(tokens, attn_matrices, ffn_matrices, vectors, segments, pad_segment, cotangent, size):
    fast = size == OWNERS
    each = vectors.shape[0]
    place = lax.axis_index("fsdp") if fast else jnp.zeros((), jnp.int32)
    me = place.reshape(1).astype(jnp.int32)
    my_z = place >> 3
    rows = segments.shape[0]
    seen, span = spans(segments, pad_segment)
    segc = seen.reshape(rows * SLOTS, 1)
    segr = seen.reshape(rows, 1, SLOTS)

    if fast:
        lower = place < OWNERS // 2
        flat = jnp.zeros((VEC_ROWS * 128,), BF)
        mine = lax.dynamic_update_slice(flat, vectors, (place * each,)).reshape(VEC_TILES, 16, 128)
        attn_in = Gather(retile(attn_matrices, 6), mine)
        ffn_in = Gather(jnp.where(lower, retile(ffn_matrices, 24), retile(ffn_matrices, 6)))
        attn_in.planes()
        attn_in.hops, (ffn_in.own, segc, segr, span) = meet(
            attn_in.hops, (ffn_in.own, segc, segr, span)
        )
        ffn_in.planes()
        attn_in.join()
        attn_in.sides()
        attn_in.hops, ffn_in.hops[:2] = meet(attn_in.hops, ffn_in.hops[:2])
        attn_in.corner()
        pieces, vecs = attn_in.mirrored(attn_in.pieces()), attn_in.vectors()
        ffn_in.hops, (pieces, vecs) = meet(ffn_in.hops, (pieces, vecs))
        ffn_in.join()
        ffn_in.sides()
    else:
        gathered, ffn_tiles, vecs = gather_plain(attn_matrices, ffn_matrices, vectors)
        pieces = [gathered]
    query, key, value, ctx, lse, wa, vec = attn_fwd(
        fast, me, span, pieces, vecs, tokens, segc, segr
    )
    if fast:
        ffn_in.hops, (ctx, wa, vec) = meet(ffn_in.hops, (ctx, wa, vec))
        ffn_in.corner()
        large = (ffn_in.parts[0], ffn_in.over_x[0], ffn_in.over_y[0])
        ready = {i: hop(part, 1) for i, part in enumerate(large)}
    n1, rstd = norm_fwd(wa, ctx, tokens, vec)
    if fast:
        ffn_in.hops, (n1, rstd) = meet(ffn_in.hops, (n1, rstd))
        ffn_pieces = ffn_in.mirrored(ffn_in.pieces(), ready)
    else:
        ffn_pieces = [ffn_tiles]
    out, dw1k, dw1s, dw2k, dw2s, vg, dh1, da, dctx = ffn_layer(
        fast, me, ffn_pieces, wa, n1, rstd, cotangent, segc, vec
    )
    def attend_back(first, dctx):
        return attn_bwd(span, query, key, value, ctx, dctx, lse, segc, segr, first, 2)

    if not fast:
        grads = [attend_back(first, dctx) for first in (0, 2, 4)]
        dwk, dws, vg = proj_grad(me, tokens, ctx, grads, da, vg)
        dx = input_grad(wa, dh1, grads)
        vector_terms = vg.reshape(-1)[: 12 * D]
        return (out, dx) + reduce_plain((dw1k, dw1s, dw2k, dw2s), (dwk, dws), vector_terms)

    ffn = Reduction([tiles_of(dw1k), tiles_of(dw2k)], [tiles_of(dw1s), tiles_of(dw2s)], me)
    first = attend_back(0, dctx)
    ffn.hops, (first, dctx) = meet(ffn.hops, (first, dctx))
    ffn.corner()
    ffn.send()
    grads = [first, attend_back(2, dctx), attend_back(4, dctx)]
    dwk, dws, vg = proj_grad(me, tokens, ctx, grads, da, vg)
    ffn.hops, (dwk, dws, vg, grads) = meet(ffn.hops, (dwk, dws, vg, grads))
    ffn.sides()
    attn = Reduction([tiles_of(dwk)], [tiles_of(dws)], me, vg.reshape(VEC_TILES, 16, 128))
    dx = input_grad(wa, dh1, grads)
    attn.hops, dx = meet(attn.hops, dx)
    attn.corner()
    ffn.hops, attn.messages = meet(ffn.hops, attn.messages)
    attn.send()
    ffn.planes()
    ffn.cross()
    ffn.hops[:2], attn.hops = meet(ffn.hops[:2], attn.hops)
    attn.sides()
    ffn.hops[2:], attn.hops = meet(ffn.hops[2:], attn.hops)
    attn.planes()
    attn.cross()
    ffn.hops, attn.hops = meet(ffn.hops, attn.hops)

    ffn_sum = ffn.total()
    ffn_grad = jnp.where(lower, untile(ffn_sum, 24), untile(ffn_sum, 6))
    attn_grad = untile(attn.total(), 6)
    vector_grad = lax.dynamic_slice(attn.vec.reshape(-1), (place * each,), (each,))
    return out, dx, attn_grad, ffn_grad, vector_grad


def solution(mesh):
    size = mesh.shape["fsdp"]
    return jax.shard_map(
        functools.partial(layer, size=size),
        mesh=mesh,
        in_specs=(
            P("fsdp", None),
            P("fsdp", None),
            P("fsdp", None),
            P("fsdp"),
            P("fsdp", None),
            P("fsdp"),
            P("fsdp", None),
        ),
        out_specs=(P("fsdp", None), P("fsdp", None), P("fsdp", None), P("fsdp", None), P("fsdp")),
        check_vma=False,
    )
```

```python
import functools

import jax
import jax.numpy as jnp
from jax import lax
from jax.experimental import pallas as pl
from jax.experimental.pallas import tpu as pltpu
from jax.sharding import PartitionSpec as P

D = 768
FF = 3072
SLOTS = 512
BF = jnp.bfloat16
F32 = jnp.float32
NN = ((1,), (0,))
NT = ((1,), (1,))
TN = ((0,), (0,))
OWNERS = 32
ATTN_TILES = 36
FFN_TILES = 72
COST_SCALE = 1
VMEM_LIMIT = 64 * 1024 * 1024

TAIL_SLOPE = 0.39 * 0.5**0.5
TAIL_POLY = (
    0.11766260955586648,
    0.04569420719462487,
    0.32477969950633645,
    -0.3177001395785759,
    0.44333218507090993,
    -0.11376856259852677,
)


def dot(left, right, dims):
    return lax.dot_general(left, right, (dims, ((), ())), preferred_element_type=F32)


def params(**kwargs):
    return pltpu.CompilerParams(vmem_limit_bytes=VMEM_LIMIT, **kwargs)


def cost(flops, bytes_accessed, transcendentals):
    return pl.CostEstimate(
        flops=flops // COST_SCALE,
        bytes_accessed=bytes_accessed // COST_SCALE,
        transcendentals=transcendentals // COST_SCALE,
    )


def whole(shape):
    zeros = (0,) * len(shape)
    return pl.BlockSpec(shape, lambda *_: zeros)


ANY = pl.BlockSpec(memory_space=pl.ANY)
VEC_TILES = 5
VEC_ROWS = 16 * VEC_TILES


def row(vec_ref, index, width=D):
    blocks = width // 128
    return jnp.concatenate([vec_ref[pl.ds(6 * index + i, 1), :] for i in range(blocks)], axis=1)


def put_row(vec_ref, index, value, first=0):
    for i in range(value.shape[1] // 128):
        vec_ref[pl.ds(6 * index + first + i, 1), :] = value[:, 128 * i : 128 * i + 128]


def square_cols(tiles, first, col):
    parts = [tiles[pl.ds(first, 8), i * 6 + col] for i in range(6)]
    return jnp.stack(parts, axis=1).reshape(D, 128)


def square(tiles, first):
    return jnp.concatenate([square_cols(tiles, first, col) for col in range(6)], axis=1)


def up_col(tiles, col):
    parts = [tiles[pl.ds(0, 16), i * 24 + col] for i in range(3)]
    return jnp.stack(parts, axis=1).reshape(D, 128)


def up_chunk(tiles, chunk):
    return jnp.concatenate([up_col(tiles, chunk * 6 + col) for col in range(6)], axis=1)


def down_chunk(tiles, chunk):
    cols = []
    for col in range(6):
        parts = [tiles[pl.ds(16 + 4 * chunk, 4), i * 6 + col] for i in range(12)]
        cols.append(jnp.stack(parts, axis=1).reshape(D, 128))
    return jnp.concatenate(cols, axis=1)


def piece_count(parts):
    return 2 * (3 * parts + 2)


def piece_copies(me, refs, tiles, parts, w_s):
    yxc, my_z = me & 7, me >> 3
    planes = []
    for step in range(4):
        copies = []
        for core in range(2):
            arrays = refs[core * (3 * parts + 2) :]
            for side in range(4):
                if side == 3:
                    source, index = arrays[3 * parts + step // 2], step % 2
                elif parts == 2 and step == 3:
                    source, index = arrays[2 * side + 1], 0
                else:
                    source, index = arrays[parts * side], step
                owner = 8 * (my_z ^ step) + (yxc ^ (2 * side + core))
                copies.append((source.at[pl.ds(index * tiles, tiles)], w_s.at[owner]))
        planes.append(copies)
    return planes


def attn_copies(fast, me, refs, w_s, sems):
    if not fast:
        return [pltpu.make_async_copy(refs[0], w_s, sems.at[0])]
    planes = piece_copies(me, refs, ATTN_TILES, 1, w_s)
    copies = [copy for plane in planes for copy in plane]
    return [pltpu.make_async_copy(src, dst, sems.at[i]) for i, (src, dst) in enumerate(copies)]


def attn_fwd_kernel(fast, me_ref, span_ref, *args):
    count = piece_count(1) if fast else 1
    refs = args[:count]
    (
        vec_ref, x_ref, segc_ref, segr_ref,
        q_ref, k_ref, v_ref, ctx_ref, lse_ref, wa_ref, vec_out_ref,
        w_s, vt_s, sems, out_sem,
    ) = args[count:]
    line, col = pl.program_id(0), pl.program_id(1)
    first_step = (line == 0) & (col == 0)
    last_step = (line == pl.num_programs(0) - 1) & (col == pl.num_programs(1) - 1)
    out_copy = pltpu.make_async_copy(w_s, wa_ref, out_sem)

    @pl.when(first_step)
    def _():
        copies = attn_copies(fast, me_ref[0], refs, w_s, sems)
        for copy in copies:
            copy.start()
        vec = vec_ref[0].astype(F32)
        for i in range(1, vec_ref.shape[0]):
            vec = vec + vec_ref[i].astype(F32)
        vec_out_ref[...] = vec.reshape(VEC_ROWS, 128)
        for copy in copies:
            copy.wait()
        out_copy.start()

    @pl.when(last_step)
    def _():
        out_copy.wait()

    cols = [2 * col, 2 * col + 1]
    weight = jnp.concatenate([square_cols(w_s, 8 * m, c) for m in range(3) for c in cols], axis=1)
    qkv = dot(x_ref[...], weight, NN)
    bias_q = jnp.concatenate([vec_out_ref[pl.ds(c, 1), :] for c in cols], axis=1)
    bias_v = jnp.concatenate([vec_out_ref[pl.ds(6 + c, 1), :] for c in cols], axis=1)
    q_ref[...] = (qkv[:, :256] + bias_q).astype(BF) * 0.125
    k_ref[...] = qkv[:, 256:512].astype(BF)
    v_ref[...] = (qkv[:, 512:] + bias_v).astype(BF)
    lane = lax.broadcasted_iota(jnp.int32, (1, 128), 1)
    low = lane < 64
    zero = jnp.zeros((), BF)

    for pair in range(2):
        vt_s[pl.ds(128 * pair, 128), :] = v_ref[:, 128 * pair : 128 * pair + 128].T

    def attend(block, carry):
        rows = pl.ds(pl.multiple_of(block * 128, 128), 128)
        start, count = span_ref[line, 2 * block], span_ref[line, 2 * block + 1]

        @pl.when(count == 0)
        def _():
            ctx_ref[rows, :] = jnp.zeros((128, 256), BF)
            lse_ref[:, rows] = jnp.zeros((4, 128), F32)

        def window(size):
            @pl.when(count == size)
            def _():
                seen = pl.ds(pl.multiple_of(start * 128, 128), 128 * size)
                seg_row = segr_ref[:, rows]
                blocked = jnp.where(segc_ref[seen, :] == seg_row, 0.0, -1e30)
                keep = jnp.where(jnp.broadcast_to(seg_row, (64, 128)) < 0, 0.0, 1.0)
                scores = []
                for head in range(4):
                    lanes = slice(128 * (head // 2), 128 * (head // 2) + 128)
                    query = q_ref[rows, lanes]
                    query = jnp.where(low, query, zero) if head % 2 == 0 else jnp.where(low, zero, query)
                    scores.append(dot(k_ref[seen, lanes], query, NT) + blocked)
                tops = [jnp.max(score, axis=0, keepdims=True) for score in scores]
                expds = [jnp.exp(score - top) for score, top in zip(scores, tops)]
                totals = [jnp.sum(expd, axis=0, keepdims=True) for expd in expds]
                outs = []
                for head in range(4):
                    values = vt_s[pl.ds(64 * head, 64), seen]
                    out = dot(values, expds[head].astype(BF), NN)
                    outs.append(out * (1.0 / totals[head]) * keep)
                    lse_ref[pl.ds(head, 1), rows] = tops[head] + jnp.log(totals[head])
                ctx_ref[rows, :] = jnp.concatenate(outs, axis=0).T.astype(BF)

        for size in range(1, 5):
            window(size)
        return carry

    lax.fori_loop(0, 4, attend, 0)


def attn_fwd(fast, me, span, pieces, vec, tokens, segc, segr):
    count = tokens.shape[0]
    rows = count // SLOTS
    part = pl.BlockSpec((SLOTS, 256), lambda r, j, m, s: (r, j))
    slot = pl.BlockSpec((SLOTS, 1), lambda r, j, m, s: (r, 0))
    shape = jax.ShapeDtypeStruct
    return pl.pallas_call(
        functools.partial(attn_fwd_kernel, fast),
        grid_spec=pltpu.PrefetchScalarGridSpec(
            num_scalar_prefetch=2,
            grid=(rows, 3),
            in_specs=[ANY] * len(pieces)
            + [
                whole(vec.shape),
                pl.BlockSpec((SLOTS, D), lambda r, j, m, s: (r, 0)),
                slot,
                pl.BlockSpec((None, 1, SLOTS), lambda r, j, m, s: (r, 0, 0)),
            ],
            out_specs=[part] * 4
            + [pl.BlockSpec((None, None, 4, SLOTS), lambda r, j, m, s: (r, j, 0, 0)), ANY, whole((VEC_ROWS, 128))],
            scratch_shapes=[
                pltpu.VMEM((OWNERS, ATTN_TILES, 16, 128), BF),
                pltpu.VMEM((256, SLOTS), BF),
                pltpu.SemaphoreType.DMA((160,)),
                pltpu.SemaphoreType.DMA,
            ],
        ),
        out_shape=[shape((count, D), BF)] * 4
        + [
            shape((rows, 3, 4, SLOTS), F32),
            shape((OWNERS, ATTN_TILES, 16, 128), BF),
            shape((VEC_ROWS, 128), F32),
        ],
        compiler_params=params(),
        cost_estimate=cost(
            flops=2 * count * D * (3 * D + 4 * SLOTS), bytes_accessed=count * D * 12, transcendentals=count * SLOTS * 12
        ),
        name="attn_fwd",
    )(me, span, *pieces, vec, tokens, segc, segr)


def norm_parts(hidden):
    mean = jnp.mean(hidden, axis=1, keepdims=True)
    centered = hidden - mean
    var = jnp.mean(centered * centered, axis=1, keepdims=True)
    rstd = lax.rsqrt(var + 1e-12)
    return centered * rstd, rstd


def gelu_parts(u):
    size = jnp.abs(u)
    t = pl.reciprocal(1.0 + TAIL_SLOPE * size)
    poly = jnp.full_like(t, TAIL_POLY[-1])
    for coef in TAIL_POLY[-2::-1]:
        poly = poly * t + coef
    bell = jnp.exp(u * u * -0.5)
    tail = poly * t * bell
    phi_cdf = jnp.where(u > 0, 1.0 - tail, tail)
    return u * phi_cdf, phi_cdf + u * bell * 0.3989422804014327


NORM_TILE = 256


def norm_fwd_kernel(wa_ref, ctx_ref, x_ref, vec_ref, n1_ref, rstd_ref, wo_s, sem):
    copy = pltpu.make_async_copy(wa_ref.at[pl.ds(24, 8)], wo_s, sem)

    @pl.when(pl.program_id(0) == 0)
    def _():
        copy.start()
        copy.wait()

    hidden = x_ref[...].astype(F32) + dot(ctx_ref[...], square(wo_s, 0), NN) + row(vec_ref, 2)
    normed, rstd = norm_parts(hidden)
    n1_ref[...] = normed
    rstd_ref[...] = jnp.broadcast_to(rstd, rstd_ref.shape)


def norm_fwd(wa, ctx, tokens, vec):
    count = tokens.shape[0]
    rows = pl.BlockSpec((NORM_TILE, D), lambda i: (i, 0))
    slim = pl.BlockSpec((NORM_TILE, 128), lambda i: (i, 0))
    shape = jax.ShapeDtypeStruct
    return pl.pallas_call(
        norm_fwd_kernel,
        grid=(count // NORM_TILE,),
        in_specs=[ANY, rows, rows, whole((VEC_ROWS, 128))],
        out_specs=[rows, slim],
        out_shape=[shape((count, D), F32), shape((count, 128), F32)],
        scratch_shapes=[pltpu.VMEM((8, ATTN_TILES, 16, 128), BF), pltpu.SemaphoreType.DMA],
        compiler_params=params(),
        cost_estimate=cost(
            flops=2 * count * D * D, bytes_accessed=count * D * 9, transcendentals=0
        ),
        name="norm_fwd",
    )(wa, ctx, tokens, vec)


def ffn_copies(fast, me, refs, w_s, sems):
    if not fast:
        pairs = [[(refs[0].at[pl.ds(16 * m, 16)], w_s.at[pl.ds(16 * m, 16)])] for m in range(2)]
    else:
        planes = piece_copies(me, refs, FFN_TILES, 1, w_s)
        pairs = [planes[0] + planes[1], planes[2] + planes[3]]
    return [
        [pltpu.make_async_copy(src, dst, sems.at[m, i]) for i, (src, dst) in enumerate(group)]
        for m, group in enumerate(pairs)
    ]


MID_TILE = 1024


def pick(mine, even, odd):
    return jnp.where(mine == 0, even, odd), jnp.where(mine == 0, odd, even)


def norm_grad(normed, rstd, t):
    mean_t = jnp.mean(t, axis=1, keepdims=True)
    mean_tn = jnp.mean(t * normed, axis=1, keepdims=True)
    return (t - mean_t - normed * mean_tn) * rstd


def column_sum(value):
    return jnp.sum(value.astype(F32), axis=0, keepdims=True)


def ffn_kernel(fast, me_ref, *args):
    pieces = piece_count(1) if fast else 1
    (
        wa_ref, n1_ref, rstd_ref, cot_ref, seg_ref, vec_ref,
        out_ref, dw1k_ref, dw1s_ref, dw2k_ref, dw2s_ref, vg_ref, dh1_ref, da_ref, dctx_ref,
        w_s, wo_s, g_s, gp_s, yb_s, ybt_s, dz_s, du_s, r_s, ua_s, ub_s, sems, wo_sem,
    ) = args[pieces:]
    step = pl.program_id(0)
    me = me_ref[0]
    core, my_x, my_y = me & 1, (me >> 1) & 1, (me >> 2) & 1
    copies = ffn_copies(fast, me, args[:pieces], w_s, sems)
    holds_up = me < OWNERS // 2
    wo_copy = pltpu.make_async_copy(wa_ref.at[pl.ds(24, 8)], wo_s, wo_sem)
    count = n1_ref.shape[0]

    def tile(i, size):
        return pl.ds(pl.multiple_of(i * size, size), size)

    def wait_for(matrix):
        for group in range(2):

            @pl.when(holds_up == (group == matrix))
            def _(group=group):
                for copy in copies[group]:
                    copy.wait()

    @pl.when(step == 0)
    def _():
        for group in copies:
            for copy in group:
                copy.start()
        wo_copy.start()

        def body(i, carry):
            rows = tile(i, NORM_TILE)
            y_one = n1_ref[rows, :] * row(vec_ref, 3) + row(vec_ref, 4)
            yb_s[rows, :] = y_one.astype(BF)
            dh1_ref[rows, :] = y_one + row(vec_ref, 9)
            return carry

        lax.fori_loop(0, count // NORM_TILE, body, 0)
        ybt_s[...] = yb_s[...].T
        wait_for(0)

    @pl.when(step == 0)
    def _():
        def weights_of(sub):
            weight = jnp.concatenate([up_col(w_s, 2 * sub + i) for i in range(2)], axis=1)
            bias = jnp.concatenate([vec_ref[pl.ds(30 + 2 * sub + i, 1), :] for i in range(2)], axis=1)
            return weight, bias

        def advance(new_ref, new_sub, old_ref, old_sub):
            weight, bias = weights_of(new_sub)
            chunk = lax.div(old_sub, 3)
            lanes = tile(old_sub - 3 * chunk, 256)
            for first in range(0, count, 128):
                rows = slice(first, first + 128)
                new_ref[rows, :] = dot(yb_s[rows, :], weight, NN) + bias
                act, slope = gelu_parts(old_ref[rows, :])
                g_s[chunk, rows, lanes] = act.astype(BF)
                gp_s[chunk, rows, lanes] = slope.astype(BF)

        weight, bias = weights_of(0)
        ua_s[...] = dot(yb_s[...], weight, NN) + bias

        def widen(i, carry):
            advance(ub_s, 2 * i + 1, ua_s, 2 * i)
            advance(ua_s, jnp.minimum(2 * i + 2, 11), ub_s, 2 * i + 1)
            return carry

        lax.fori_loop(0, 6, widen, 0)
        wait_for(1)

        def narrow(i, carry):
            rows = tile(i, MID_TILE)
            total = dh1_ref[rows, :]
            for chunk in range(4):
                total = total + dot(g_s[chunk, rows, :], down_chunk(w_s, chunk), NN)
            dh1_ref[rows, :] = total
            return carry

        lax.fori_loop(0, count // MID_TILE, narrow, 0)

    @pl.when(step == 0)
    def _():
        def body(i, sums):
            rows = tile(i, NORM_TILE)
            normed, rstd = norm_parts(dh1_ref[rows, :])
            gain = row(vec_ref, 10)
            out_ref[rows, :] = (normed * gain + row(vec_ref, 11)).astype(BF)
            err = cot_ref[rows, :].astype(F32)
            dh2 = norm_grad(normed, rstd, gain * err)
            dz = dh2.astype(BF)
            dh1_ref[rows, :] = dh2
            dz_s[rows, :] = dz
            return (
                sums[0] + column_sum(dz),
                sums[1] + column_sum(err * normed),
                sums[2] + column_sum(err),
            )

        zero = jnp.zeros((1, D), F32)
        sums = lax.fori_loop(0, count // NORM_TILE, body, (zero, zero, zero))
        vg_ref[...] = jnp.zeros_like(vg_ref)
        for i in range(3):
            put_row(vg_ref, 9 + i, sums[i])

    @pl.when(step >= 1)
    def _():
        chunk = step - 1

        def back(i, total):
            rows = tile(i, MID_TILE)
            dg = dot(dz_s[rows, :], down_chunk(w_s, chunk), NT)
            du = (gp_s[chunk, rows, :].astype(F32) * dg).astype(BF)
            du_s[rows, :] = du
            dh1_ref[rows, :] += dot(du, up_chunk(w_s, chunk), NT)
            return total + column_sum(du)

        put_row(vg_ref, 5 + chunk, lax.fori_loop(0, count // MID_TILE, back, jnp.zeros((1, D), F32)))

        def weights(half, carry):
            lanes = tile(half, 384)
            r_s[...] = dot(ybt_s[lanes, :], du_s[...], NN).astype(BF)
            for pair in range(4):
                even, odd = r_s[pl.ds(pair * 96, 48), :], r_s[pl.ds(pair * 96 + 48, 48), :]
                keep, send = pick(core, even, odd)
                place = (((pair >> 1) ^ my_y) << 1) | ((pair & 1) ^ my_x)
                for col in range(6):
                    spot = slice(col * 128, col * 128 + 128)
                    dw1k_ref[place, half, :, col] = keep[:, spot].reshape(3, 16, 128)
                    dw1s_ref[place, half, :, col] = send[:, spot].reshape(3, 16, 128)
            r_s[...] = dot(g_s[chunk, :, lanes], dz_s[...], TN).astype(BF)
            keep, send = pick(core, r_s[:192, :], r_s[192:, :])
            for col in range(6):
                spot = slice(col * 128, col * 128 + 128)
                dw2k_ref[half ^ my_x, 0, :, col] = keep[:, spot].reshape(12, 16, 128)
                dw2s_ref[half ^ my_x, 0, :, col] = send[:, spot].reshape(12, 16, 128)
            return carry

        lax.fori_loop(0, 2, weights, 0)

    @pl.when(step == 4)
    def _():
        wo_copy.wait()

        def body(i, sums):
            rows = tile(i, NORM_TILE)
            dy1, normed = dh1_ref[rows, :], n1_ref[rows, :]
            dh1 = norm_grad(normed, rstd_ref[rows, 0:1], dy1 * row(vec_ref, 3))
            da = dh1.astype(BF)
            dh1_ref[rows, :] = dh1
            da_ref[rows, :] = da
            back = dot(da, square(wo_s, 0), NT)
            dctx_ref[rows, :] = jnp.where(seg_ref[rows, :] >= 0, back, 0.0).astype(BF)
            return (
                sums[0] + column_sum(da),
                sums[1] + column_sum(dy1 * normed),
                sums[2] + column_sum(dy1),
            )

        zero = jnp.zeros((1, D), F32)
        sums = lax.fori_loop(0, count // NORM_TILE, body, (zero, zero, zero))
        for i in range(3):
            put_row(vg_ref, 2 + i, sums[i])


def ffn_layer(fast, me, pieces, wa, n1, rstd, cotangent, segc, vec):
    count = n1.shape[0]
    once = pl.Buffered(1)

    def single(shape):
        zeros = (0,) * len(shape)
        return pl.BlockSpec(shape, lambda *_: zeros, pipeline_mode=once)

    full = whole((count, D))
    up = pl.BlockSpec(
        (4, 2, 3, 6, 16, 128), lambda s, m: (0, 0, 0, jnp.maximum(s - 1, 0), 0, 0)
    )

    def down_index(s, m):
        chunk = jnp.maximum(s - 1, 0)
        return ((chunk % 2) ^ ((m[0] >> 2) & 1), chunk // 2, 0, 0, 0, 0)

    down = pl.BlockSpec((2, 1, 12, 6, 16, 128), down_index)
    shape = jax.ShapeDtypeStruct
    return pl.pallas_call(
        functools.partial(ffn_kernel, fast),
        grid_spec=pltpu.PrefetchScalarGridSpec(
            num_scalar_prefetch=1,
            grid=(5,),
            in_specs=[ANY] * len(pieces)
            + [
                ANY,
                single((count, D)),
                single((count, 128)),
                single((count, D)),
                single((count, 1)),
                single((VEC_ROWS, 128)),
            ],
            out_specs=[full, up, up, down, down, whole((VEC_ROWS, 128)), full, full, full],
            scratch_shapes=[
                pltpu.VMEM((OWNERS, FFN_TILES, 16, 128), BF),
                pltpu.VMEM((8, ATTN_TILES, 16, 128), BF),
                pltpu.VMEM((4, count, D), BF),
                pltpu.VMEM((4, count, D), BF),
                pltpu.VMEM((count, D), BF),
                pltpu.VMEM((D, count), BF),
                pltpu.VMEM((count, D), BF),
                pltpu.VMEM((count, D), BF),
                pltpu.VMEM((D // 2, D), BF),
                pltpu.VMEM((count, 256), F32),
                pltpu.VMEM((count, 256), F32),
                pltpu.SemaphoreType.DMA((2, 40)),
                pltpu.SemaphoreType.DMA,
            ],
        ),
        out_shape=[shape((count, D), BF)]
        + [shape((4, 2, 3, 24, 16, 128), BF)] * 2
        + [shape((4, 2, 12, 6, 16, 128), BF)] * 2
        + [shape((VEC_ROWS, 128), F32), shape((count, D), F32)]
        + [shape((count, D), BF)] * 2,
        compiler_params=params(),
        cost_estimate=cost(
            flops=12 * count * D * FF, bytes_accessed=count * D * 30, transcendentals=count * FF
        ),
        name="ffn_layer",
    )(me, *pieces, wa, n1, rstd, cotangent, segc, vec)


def attn_bwd_kernel(
    first, span_ref, q_ref, k_ref, v_ref, ctx_ref, dctx_ref, lse_ref, segc_ref, segr_ref, d_ref, dqt_s, dots_s
):
    line = pl.program_id(0)
    pairs = q_ref.shape[1] // 128
    lane = lax.broadcasted_iota(jnp.int32, (1, 128), 1)
    low = lane < 64
    zero = jnp.zeros((), BF)
    spots = [slice(128 * pair, 128 * pair + 128) for pair in range(pairs)]
    for pair, lanes in enumerate(spots):
        products = (dctx_ref[:, lanes].astype(F32) * ctx_ref[:, lanes].astype(F32)).T
        for head in range(2):
            place = slice(4 * pair + head, 4 * pair + head + 1)
            dots_s[place, :] = jnp.sum(products[64 * head : 64 * head + 64], axis=0, keepdims=True)
            index = 2 * (first + pair) + head
            place = slice(4 * pair + 2 + head, 4 * pair + 3 + head)
            dots_s[place, :] = lse_ref[index // 4, index % 4 : index % 4 + 1, :]
    dqt_s[...] = jnp.zeros_like(dqt_s)

    def both(value):
        return jnp.concatenate([jnp.where(low, value, zero), jnp.where(low, zero, value)], axis=0)

    def block_step(block, carry):
        rows = pl.ds(pl.multiple_of(block * 128, 128), 128)
        start, count = span_ref[line, 2 * block], span_ref[line, 2 * block + 1]

        @pl.when(count == 0)
        def _():
            d_ref[1, rows, :] = jnp.zeros((128, 128 * pairs), BF)
            d_ref[2, rows, :] = jnp.zeros((128, 128 * pairs), BF)

        def window(size):
            @pl.when(count == size)
            def _():
                seen = pl.ds(pl.multiple_of(start * 128, 128), 128 * size)
                seg_row = segr_ref[:, seen]
                allowed = segc_ref[rows, :] == jnp.where(seg_row < 0, -2, seg_row)
                allowed = jnp.concatenate([allowed, allowed], axis=0)

                def spread(pair, offset):
                    lines = [dots_s[4 * pair + offset + h : 4 * pair + offset + h + 1, seen] for h in range(2)]
                    return jnp.concatenate([jnp.broadcast_to(r, (128, 128 * size)) for r in lines], axis=0)

                keys = [both(k_ref[rows, lanes]) for lanes in spots]
                queries = [q_ref[seen, lanes] for lanes in spots]
                dctxs = [dctx_ref[seen, lanes] for lanes in spots]
                scores = [dot(k, q, NT) for k, q in zip(keys, queries)]
                dprobs = [dot(both(v_ref[rows, lanes]), dctx, NT) for lanes, dctx in zip(spots, dctxs)]
                probs = [
                    jnp.where(allowed, jnp.exp(score - spread(pair, 2)), 0.0)
                    for pair, score in enumerate(scores)
                ]
                dscores = [
                    (prob * (dprob - spread(pair, 0))).astype(BF)
                    for pair, (prob, dprob) in enumerate(zip(probs, dprobs))
                ]
                dvs = [dot(prob.astype(BF), dctx, NN) for prob, dctx in zip(probs, dctxs)]
                dks = [dot(dscore, query, NN) for dscore, query in zip(dscores, queries)]
                dqs = [dot(key, dscore, TN) for key, dscore in zip(keys, dscores)]
                for pair, lanes in enumerate(spots):
                    dqt_s[lanes, seen] += dqs[pair]
                    d_ref[1, rows, lanes] = jnp.where(low, dks[pair][:128], dks[pair][128:]).astype(BF)
                    d_ref[2, rows, lanes] = jnp.where(low, dvs[pair][:128], dvs[pair][128:]).astype(BF)

        for size in range(1, 5):
            window(size)
        return carry

    lax.fori_loop(0, 4, block_step, 0)
    d_ref[0] = (dqt_s[...].T * 0.125).astype(BF)


def attn_bwd(span, query, key, value, ctx, dctx, lse, segc, segr, first, cols):
    count = query.shape[0]
    rows = count // SLOTS
    width = 128 * cols
    part = pl.BlockSpec((SLOTS, width), lambda r, s: (r, first // cols))
    return pl.pallas_call(
        functools.partial(attn_bwd_kernel, first),
        grid_spec=pltpu.PrefetchScalarGridSpec(
            num_scalar_prefetch=1,
            grid=(rows,),
            in_specs=[part] * 5
            + [
                pl.BlockSpec((None, 3, 4, SLOTS), lambda r, s: (r, 0, 0, 0)),
                pl.BlockSpec((SLOTS, 1), lambda r, s: (r, 0)),
                pl.BlockSpec((None, 1, SLOTS), lambda r, s: (r, 0, 0)),
            ],
            out_specs=pl.BlockSpec((3, SLOTS, width), lambda r, s: (0, r, 0)),
            scratch_shapes=[pltpu.VMEM((width, SLOTS), F32), pltpu.VMEM((4 * cols, SLOTS), F32)],
        ),
        out_shape=jax.ShapeDtypeStruct((3, count, width), BF),
        compiler_params=params(),
        cost_estimate=cost(
            flops=10 * count * D * SLOTS, bytes_accessed=count * D * 16, transcendentals=count * SLOTS * 12
        ),
        name="attn_bwd",
    )(span, query, key, value, ctx, dctx, lse, segc, segr)


def proj_grad_kernel(me_ref, x_ref, ctx_ref, first_ref, second_ref, da_ref, vg_in_ref, dwk_ref, dws_ref, vg_ref, r_s):
    step = pl.program_id(0)
    me = me_ref[0]
    core, my_x, my_y = me & 1, (me >> 1) & 1, (me >> 2) & 1

    @pl.when(step == 0)
    def _():
        vg_ref[...] = vg_in_ref[...]

    @pl.when(step < 3)
    def _():
        grad = jnp.concatenate([first_ref[...], second_ref[...]], axis=1)
        r_s[...] = dot(x_ref[...], grad, TN).astype(BF)

        @pl.when(step != 1)
        def _():
            put_row(vg_ref, step >> 1, column_sum(grad))

    @pl.when(step == 3)
    def _():
        r_s[...] = dot(ctx_ref[...], da_ref[...], TN).astype(BF)

    for pair in range(4):
        even, odd = r_s[pl.ds(pair * 192, 96), :], r_s[pl.ds(pair * 192 + 96, 96), :]
        keep, send = pick(core, even, odd)
        place = (((pair >> 1) ^ my_y) << 1) | ((pair & 1) ^ my_x)
        for col in range(6):
            lanes = slice(col * 128, col * 128 + 128)
            dwk_ref[place, 0, :, col] = keep[:, lanes].reshape(6, 16, 128)
            dws_ref[place, 0, :, col] = send[:, lanes].reshape(6, 16, 128)


def proj_grad(me, tokens, ctx, first, second, da, vg):
    count, width = first.shape[1:]
    out = pl.BlockSpec((4, 1, 6, 6, 16, 128), lambda i, m: (0, i, 0, 0, 0, 0))
    full = whole((count, D))
    part = pl.BlockSpec((None, count, width), lambda i, m: (jnp.minimum(i, 2), 0, 0))
    shape = jax.ShapeDtypeStruct
    return pl.pallas_call(
        proj_grad_kernel,
        grid_spec=pltpu.PrefetchScalarGridSpec(
            num_scalar_prefetch=1,
            grid=(4,),
            in_specs=[full, full, part, part, full, whole((VEC_ROWS, 128))],
            out_specs=[out, out, whole((VEC_ROWS, 128))],
            scratch_shapes=[pltpu.VMEM((D, D), BF)],
        ),
        out_shape=[shape((4, 4, 6, 6, 16, 128), BF)] * 2 + [shape((VEC_ROWS, 128), F32)],
        compiler_params=params(),
        cost_estimate=cost(
            flops=8 * count * D * D, bytes_accessed=count * D * 20, transcendentals=0
        ),
        name="proj_grad",
    )(me, tokens, ctx, first, second, da, vg)


def input_grad_kernel(wa_ref, dh1_ref, da_ref, db_ref, out_ref, w_s, sems):
    @pl.when(pl.program_id(0) == 0)
    def _():
        copies = [
            pltpu.make_async_copy(
                wa_ref.at[pl.ds(8 * m, 8)],
                w_s.at[pl.ds(8 * m, 8)],
                sems.at[m],
            )
            for m in range(3)
        ]
        for copy in copies:
            copy.start()
        for copy in copies:
            copy.wait()

    total = dh1_ref[...]
    for m in range(3):
        grad = jnp.concatenate([da_ref[m], db_ref[m]], axis=1)
        total = total + dot(grad, square(w_s, 8 * m), NT)
    out_ref[...] = total.astype(BF)


def input_grad(wa, dh1, first, second):
    count = dh1.shape[0]
    rows = pl.BlockSpec((NORM_TILE, D), lambda i: (i, 0))
    return pl.pallas_call(
        input_grad_kernel,
        grid=(count // NORM_TILE,),
        in_specs=[ANY, rows] + [pl.BlockSpec((3, NORM_TILE, D // 2), lambda i: (0, i, 0))] * 2,
        out_specs=rows,
        out_shape=jax.ShapeDtypeStruct((count, D), BF),
        scratch_shapes=[
            pltpu.VMEM((24, ATTN_TILES, 16, 128), BF),
            pltpu.SemaphoreType.DMA((3,)),
        ],
        compiler_params=params(),
        cost_estimate=cost(
            flops=6 * count * D * D, bytes_accessed=count * D * 18, transcendentals=0
        ),
        name="input_grad",
    )(wa, dh1, first, second)


def retile(flat, blocks):
    tall = flat.shape[0] // (16 * blocks)
    tiles = flat.reshape(tall, 16, blocks, 128).transpose(0, 2, 1, 3)
    return tiles.reshape(tall * blocks, 16, 128)


def untile(tiles, blocks):
    tall = tiles.shape[0] // blocks
    flat = tiles.reshape(tall, blocks, 16, 128).transpose(0, 2, 1, 3)
    return flat.reshape(tall * blocks * 16, 128)


def pad_vectors(flat):
    return jnp.pad(flat, (0, VEC_ROWS * 128 - flat.shape[0])).reshape(VEC_TILES, 16, 128)


def gather_plain(attn, ffn, vectors):
    attn = lax.all_gather(attn, "fsdp", axis=0, tiled=True)
    ffn = lax.all_gather(ffn, "fsdp", axis=0, tiled=True)
    vec = lax.all_gather(vectors, "fsdp", axis=0, tiled=True)
    half = ffn.shape[0] // 2
    tiles = jnp.concatenate([retile(ffn[:half], 24), retile(ffn[half:], 6)], axis=0)
    attn_tiles = retile(attn, 6).reshape(OWNERS, ATTN_TILES, 16, 128)
    return attn_tiles, tiles.reshape(OWNERS, FFN_TILES, 16, 128), pad_vectors(vec)[None]


class Gather:
    def __init__(self, tiles, vec=None):
        self.own, self.tiles, self.vec = tiles, tiles.shape[0], vec

    def ride(self, message):
        return message if self.vec is None else jnp.concatenate([message, self.vec], axis=0)

    def landed(self, messages, size):
        if self.vec is None:
            return messages
        total = self.vec.astype(F32) + sum(m[size:].astype(F32) for m in messages)
        self.vec = total.astype(BF)
        return [m[:size] for m in messages]

    def planes(self):
        message = self.ride(self.own)
        self.hops = [hop(message, 8 * step) for step in (1, 2, 3)]

    def join(self):
        others = self.landed(self.hops, self.tiles)
        self.parts = [jnp.concatenate([self.own] + others, axis=0)]

    def sides(self):
        first, *rest = self.parts
        self.hops = [hop(self.ride(first), 2), hop(first, 4)]
        self.hops += [hop(part, bit) for part in rest for bit in (2, 4)]

    def corner(self):
        size = self.parts[0].shape[0]
        self.over_x = self.landed(self.hops[:1], size) + self.hops[2::2]
        self.over_y = self.hops[1::2]
        low = self.over_y[0][: 2 * self.tiles]
        high = jnp.concatenate([self.over_x[0][2 * self.tiles :]] + self.over_x[1:], axis=0)
        self.hops = [hop(low, 2), hop(self.ride(high), 4)]

    def pieces(self):
        (high,) = self.landed(self.hops[1:], 2 * self.tiles)
        out = self.parts + self.over_x + self.over_y
        return out + [self.hops[0], high]

    def mirrored(self, pieces, ready=None):
        ready = ready or {}
        return pieces + [ready[i] if i in ready else hop(piece, 1) for i, piece in enumerate(pieces)]

    def vectors(self):
        return jnp.stack([self.vec, hop(self.vec, 1)], axis=0)


def hop(value, bit):
    pairs = [(i, i ^ bit) for i in range(OWNERS)]
    return lax.ppermute(value, "fsdp", pairs)


def reduce_plain(ffn_terms, attn_terms, vector_terms):
    def absolute(keep, send):
        planes = keep.shape[1]
        both = jnp.stack([keep, send], axis=1)
        return jnp.moveaxis(both, 2, 0).reshape(planes * 8, -1, 16, 128)

    dw1k, dw1s, dw2k, dw2s = ffn_terms
    up = untile(absolute(dw1k, dw1s).reshape(-1, 16, 128), 24)
    down = untile(absolute(dw2k, dw2s).reshape(-1, 16, 128), 6)
    proj = untile(absolute(*attn_terms).reshape(-1, 16, 128), 6)

    def scatter(value):
        return lax.psum_scatter(value.astype(F32), "fsdp", scatter_dimension=0, tiled=True)

    return scatter(proj), scatter(jnp.concatenate([up, down], axis=0)), scatter(vector_terms)


def get(message, index, tiles):
    if len(message.shape) == 3:
        return message[pl.ds(index * tiles, tiles)].astype(F32)
    return message[index].astype(F32)


def put(message, index, tiles, value):
    if len(message.shape) == 3:
        message[pl.ds(index * tiles, tiles)] = value.astype(message.dtype)
    else:
        message[index] = value.astype(message.dtype)


def take_terms(refs, spots, leaves):
    terms = {}
    for spot in spots:
        planes = []
        for _ in range(leaves):
            keep, other = refs.pop(0), refs.pop(0)
            planes += [(keep, other, p) for p in range(keep.shape[1])]
        terms[spot] = planes

    def term(spot, index):
        keep, other, plane = terms[spot][index]
        return keep[0, plane].astype(F32) + other[0, plane].astype(F32)

    return term, terms[spots[0]][0][0].shape[2]


def take_vec(refs, vec):
    if not vec:
        return None
    state, arrival = refs.pop(0), refs.pop(0)
    return state[...] + arrival[pl.ds(arrival.shape[0] - VEC_TILES, VEC_TILES)].astype(F32)


def put_tail(message, total):
    message[pl.ds(message.shape[0] - VEC_TILES, VEC_TILES)] = total.astype(BF)


def corner_kernel(leaves, vec, *refs):
    refs = list(refs)
    term, tiles = take_terms(refs, [(3, 0), (3, 1), (1, 0), (2, 1)], leaves)
    total = take_vec(refs, vec)
    to_x, to_y = refs[:2]
    for i in range(2):
        put(to_x, i, tiles, term((3, 0), i))
        put(to_x, 2 + i, tiles, term((1, 0), i))
        put(to_y, i, tiles, term((3, 1), i))
        put(to_y, 2 + i, tiles, term((2, 1), i))
    if vec:
        put_tail(to_x, total)
        refs[2][...] = total


def side_kernel(leaves, vec, *refs):
    refs = list(refs)
    term, tiles = take_terms(refs, [(1, 1), (2, 0)], leaves)
    from_x, from_y = refs.pop(0), refs.pop(0)
    total = take_vec(refs, vec)
    to_x, to_y = refs[:2]
    for i in range(2):
        put(to_x, i, tiles, term((1, 1), i) + get(from_y, i, tiles))
        put(to_y, i, tiles, term((2, 0), i) + get(from_x, i, tiles))
    if vec:
        put_tail(to_y, total)
        refs[2][...] = total


def plane_kernel(leaves, vec, me_ref, *refs):
    refs = list(refs)
    term, tiles = take_terms(refs, [(0, 0), (0, 1)], leaves)
    from_x, from_y, from_x_two, from_y_two = (refs.pop(0) for _ in range(4))
    total = take_vec(refs, vec)
    mine, outs, own = refs[0], refs[1:4], refs[-1]
    for i in range(2):
        lower = term((0, 0), i) + get(from_x, 2 + i, tiles) + get(from_y_two, i, tiles)
        upper = term((0, 1), i) + get(from_y, 2 + i, tiles) + get(from_x_two, i, tiles)
        own[2 * i if leaves == 2 else i] = lower
        own[2 * i + 1 if leaves == 2 else 2 + i] = upper
    my_z = me_ref[0] >> 3
    mine[...] = own[my_z]
    for step in range(3):
        if vec:
            outs[step][pl.ds(0, tiles)] = own[my_z ^ (step + 1)].astype(BF)
            put_tail(outs[step], total)
        else:
            outs[step][...] = own[my_z ^ (step + 1)].astype(BF)
    if vec:
        refs[4][...] = total


class Reduction:
    def __init__(self, keeps, sends, me, vec=None):
        self.keeps, self.me, self.vec = keeps, me, vec
        self.hops = [hop(send, 1) for send in sends]
        if vec is not None:
            self.hops.append(hop(vec.astype(BF), 1))
        self.tiles = keeps[0].shape[2]
        self.steps = 2 if vec is None else 1

    def run(self, kernel, spots, arrivals, outs, name, place=False):
        leaves, tiles, block = len(self.keeps), self.tiles, self.tiles // self.steps
        carries = self.vec is not None
        arrays, in_specs = [], []
        for spot, half in spots:
            for keep, other in zip(self.keeps, self.received, strict=True):
                spec = pl.BlockSpec(
                    (1, keep.shape[1] // 2, block, 16, 128),
                    lambda t, *_, spot=spot, half=half: (spot, half, t, 0, 0),
                )
                arrays += [keep, other]
                in_specs += [spec, spec]

        def message_spec(shape):
            if len(shape) == 4:
                return pl.BlockSpec((shape[0], block, 16, 128), lambda t, *_: (0, t, 0, 0))
            if carries:
                return whole(shape)
            return pl.BlockSpec((block, 16, 128), lambda t, *_: (t, 0, 0))

        for array in arrivals:
            arrays.append(array)
            in_specs.append(message_spec(array.shape))
        if carries:
            arrays += [self.vec, self.vec_arrival]
            in_specs += [whole(self.vec.shape), whole(self.vec_arrival.shape)]
        out_shape = []
        for planes, dtype, tail in outs:
            tail = VEC_TILES if tail and carries else 0
            if carries:
                dims = (planes * tiles + tail, 16, 128)
            else:
                dims = (planes, tiles, 16, 128) if planes > 1 else (tiles, 16, 128)
            out_shape.append(jax.ShapeDtypeStruct(dims, dtype))
        out_specs = [message_spec(shape.shape) for shape in out_shape]
        if carries:
            out_shape.append(jax.ShapeDtypeStruct(self.vec.shape, F32))
            out_specs.append(whole(self.vec.shape))
        result = pl.pallas_call(
            functools.partial(kernel, leaves, carries),
            grid_spec=pltpu.PrefetchScalarGridSpec(
                num_scalar_prefetch=1 if place else 0,
                grid=(self.steps,),
                in_specs=in_specs,
                out_specs=out_specs,
                scratch_shapes=[pltpu.VMEM((4, block, 16, 128), F32)] if place else [],
            ),
            out_shape=out_shape,
            compiler_params=params(),
            cost_estimate=cost(flops=0, bytes_accessed=tiles * 4096 * 16, transcendentals=0),
            name=name,
        )(*([self.me] if place else []), *arrays)
        if carries:
            *result, self.vec = result
        return result

    def corner(self):
        self.received = self.hops[: len(self.keeps)]
        self.vec_arrival = self.hops[-1]
        to_x, to_y = self.run(
            corner_kernel, [(3, 0), (3, 1), (1, 0), (2, 1)], [], [(4, BF, True), (4, BF, False)], "corner"
        )
        self.messages = [to_x, to_y]

    def send(self):
        self.hops = [hop(self.messages[0], 2), hop(self.messages[1], 4)]

    def sides(self):
        self.early = self.hops
        self.vec_arrival = self.hops[0]
        to_x, to_y = self.run(
            side_kernel, [(1, 1), (2, 0)], self.early, [(2, BF, False), (2, BF, True)], "sides"
        )
        self.hops = [hop(to_x, 2), hop(to_y, 4)]

    def planes(self):
        self.vec_arrival = self.hops[1]
        outs = [(1, F32, False)] + [(1, BF, True)] * 3
        self.mine, *messages = self.run(
            plane_kernel, [(0, 0), (0, 1)], self.early + self.hops, outs, "planes", place=True
        )
        self.hops = messages

    def cross(self):
        self.hops = [hop(message, 8 * (i + 1)) for i, message in enumerate(self.hops)]

    def total(self):
        tiles = self.tiles
        if self.vec is not None:
            self.vec = self.vec + sum(other[tiles:].astype(F32) for other in self.hops)
        return self.mine + sum(other[:tiles].astype(F32) for other in self.hops)


def meet(hops, values):
    return lax.optimization_barrier((hops, values))


def tiles_of(array):
    return array.reshape(array.shape[:2] + (-1, 16, 128))


def spans(segments, pad_segment):
    pad = pad_segment[:, None]
    seen = jnp.where(segments == pad, -1, segments)
    first, last = segments[:, ::128], segments[:, 127::128]
    last = jnp.minimum(last, pad - 1)
    below = jnp.sum(segments[:, None, :] < first[:, :, None], axis=2)
    upto = jnp.sum(segments[:, None, :] <= last[:, :, None], axis=2)
    start = below // 128
    count = jnp.where(first == pad, 0, (upto + 127) // 128 - start)
    both = jnp.stack([jnp.where(count == 0, 0, start), count], axis=2)
    return seen, both.reshape(segments.shape[0], 8).astype(jnp.int32)


def layer(tokens, attn_matrices, ffn_matrices, vectors, segments, pad_segment, cotangent, size):
    fast = size == OWNERS
    each = vectors.shape[0]
    place = lax.axis_index("fsdp") if fast else jnp.zeros((), jnp.int32)
    me = place.reshape(1).astype(jnp.int32)
    my_z = place >> 3
    rows = segments.shape[0]
    seen, span = spans(segments, pad_segment)
    segc = seen.reshape(rows * SLOTS, 1)
    segr = seen.reshape(rows, 1, SLOTS)

    if fast:
        lower = place < OWNERS // 2
        flat = jnp.zeros((VEC_ROWS * 128,), BF)
        mine = lax.dynamic_update_slice(flat, vectors, (place * each,)).reshape(VEC_TILES, 16, 128)
        attn_in = Gather(retile(attn_matrices, 6), mine)
        ffn_in = Gather(jnp.where(lower, retile(ffn_matrices, 24), retile(ffn_matrices, 6)))
        attn_in.planes()
        attn_in.hops, (ffn_in.own, segc, segr, span) = meet(
            attn_in.hops, (ffn_in.own, segc, segr, span)
        )
        ffn_in.planes()
        attn_in.join()
        attn_in.sides()
        attn_in.hops, ffn_in.hops[:2] = meet(attn_in.hops, ffn_in.hops[:2])
        attn_in.corner()
        pieces, vecs = attn_in.mirrored(attn_in.pieces()), attn_in.vectors()
        ffn_in.hops, (pieces, vecs) = meet(ffn_in.hops, (pieces, vecs))
        ffn_in.join()
        ffn_in.sides()
    else:
        gathered, ffn_tiles, vecs = gather_plain(attn_matrices, ffn_matrices, vectors)
        pieces = [gathered]
    query, key, value, ctx, lse, wa, vec = attn_fwd(
        fast, me, span, pieces, vecs, tokens, segc, segr
    )
    if fast:
        ffn_in.hops, (ctx, wa, vec) = meet(ffn_in.hops, (ctx, wa, vec))
        ffn_in.corner()
        large = (ffn_in.parts[0], ffn_in.over_x[0], ffn_in.over_y[0])
        ready = {i: hop(part, 1) for i, part in enumerate(large)}
    n1, rstd = norm_fwd(wa, ctx, tokens, vec)
    if fast:
        ffn_in.hops, (n1, rstd) = meet(ffn_in.hops, (n1, rstd))
        ffn_pieces = ffn_in.mirrored(ffn_in.pieces(), ready)
    else:
        ffn_pieces = [ffn_tiles]
    out, dw1k, dw1s, dw2k, dw2s, vg, dh1, da, dctx = ffn_layer(
        fast, me, ffn_pieces, wa, n1, rstd, cotangent, segc, vec
    )
    if not fast:
        first = attn_bwd(span, query, key, value, ctx, dctx, lse, segc, segr, 0, 3)
        second = attn_bwd(span, query, key, value, ctx, dctx, lse, segc, segr, 3, 3)
        dwk, dws, vg = proj_grad(me, tokens, ctx, first, second, da, vg)
        dx = input_grad(wa, dh1, first, second)
        vector_terms = vg.reshape(-1)[: 12 * D]
        return (out, dx) + reduce_plain((dw1k, dw1s, dw2k, dw2s), (dwk, dws), vector_terms)

    ffn = Reduction([tiles_of(dw1k), tiles_of(dw2k)], [tiles_of(dw1s), tiles_of(dw2s)], me)
    first = attn_bwd(span, query, key, value, ctx, dctx, lse, segc, segr, 0, 3)
    ffn.hops, (first, dctx) = meet(ffn.hops, (first, dctx))
    ffn.corner()
    ffn.send()
    second = attn_bwd(span, query, key, value, ctx, dctx, lse, segc, segr, 3, 3)
    dwk, dws, vg = proj_grad(me, tokens, ctx, first, second, da, vg)
    ffn.hops, (dwk, dws, vg, first) = meet(ffn.hops, (dwk, dws, vg, first))
    ffn.sides()
    attn = Reduction([tiles_of(dwk)], [tiles_of(dws)], me, vg.reshape(VEC_TILES, 16, 128))
    dx = input_grad(wa, dh1, first, second)
    attn.hops, dx = meet(attn.hops, dx)
    attn.corner()
    ffn.hops, attn.messages = meet(ffn.hops, attn.messages)
    attn.send()
    ffn.planes()
    ffn.cross()
    ffn.hops[:2], attn.hops = meet(ffn.hops[:2], attn.hops)
    attn.sides()
    ffn.hops[2:], attn.hops = meet(ffn.hops[2:], attn.hops)
    attn.planes()
    attn.cross()
    ffn.hops, attn.hops = meet(ffn.hops, attn.hops)

    ffn_sum = ffn.total()
    ffn_grad = jnp.where(lower, untile(ffn_sum, 24), untile(ffn_sum, 6))
    attn_grad = untile(attn.total(), 6)
    vector_grad = lax.dynamic_slice(attn.vec.reshape(-1), (place * each,), (each,))
    return out, dx, attn_grad, ffn_grad, vector_grad


def solution(mesh):
    size = mesh.shape["fsdp"]
    return jax.shard_map(
        functools.partial(layer, size=size),
        mesh=mesh,
        in_specs=(
            P("fsdp", None),
            P("fsdp", None),
            P("fsdp", None),
            P("fsdp"),
            P("fsdp", None),
            P("fsdp"),
            P("fsdp", None),
        ),
        out_specs=(P("fsdp", None), P("fsdp", None), P("fsdp", None), P("fsdp", None), P("fsdp")),
        check_vma=False,
    )
```
